32 devices in a mesh: depth: 4 (over z), wide: 8 (over y, x, core).
Axes of the slice: x: 2, y: 2, z: 4, core: 2. Of those that a mesh axis runs over, the one named last changes fastest.
Arguments:
- density: float32 [4, 4096, 4096], P('depth', 'wide'), may hold values from -4 to 4
- layer_top: float32 [4], P('depth'), may hold values from 0.75 to 1.5
- layer_thick: float32 [4], P('depth'), may hold values from 1.5 to 3
- sample_row: int32 [32, 256], P(('depth', 'wide')), may hold values from 0 to 127
- sample_col: int32 [32, 256], P(('depth', 'wide')), may hold values from 0 to 4095
- sample_frac: int32 [32, 2, 256], P(('depth', 'wide')), may hold values from 0 to 15
- sample_owner: int32 [32, 256, 1], P(('depth', 'wide')), may hold values from 0 to 7; in each aligned block of 256 rows (0 to 255, 256 to 511, ..., all dimensions but the last counted through in order) at most 64 rows name the same one
Outputs:
- gradient_grid: float32 [6, 4096, 4096], P(None, ('depth', 'wide'))
- line_samples: float32 [6, 32, 512], P(None, ('depth', 'wide'))
The draws below stay inside these ranges and needn't reach their ends.
Inputs may be any that keep to these rules, and one draw needn't show every extreme that they name: `sample_owner`: among the 256 samples of one tile no owner is named more than 64 times, a bound that some block reaches.
All inputs are finite; a program needn't handle non-finite values.
Results may differ from the reference program's by a relative error of at most 0.0001.
Values sent between devices are 32-bit elements; how exact they have to be, the bound alone decides.
No kernel may reach another device: no remote copies, remote signals or barrier semaphores. Data moves between devices by JAX's collectives and lax.ppermute only.
A program may use at most 320 MiB of HBM per device.

```python
import math
import jax
import jax.numpy as jnp
import numpy as np
from jax import lax

NG = 4096
QLEV = 16
SCAP = 256
LAYERS = 4
OWNERS = 8
TILES = 32
TROWS = 128
CAP = 64
N_WIDE = 8


def with_ends(values, key, low, largest):
    spot = [jax.random.randint(jax.random.fold_in(key, axis), (), 0, length) for axis, length in enumerate(values.shape)]
    main_axis = values.shape.index(max(values.shape))
    beside = spot[:main_axis] + [(spot[main_axis] + 1) % values.shape[main_axis]] + spot[main_axis + 1:]
    return values.at[tuple(spot)].set(low).at[tuple(beside)].set(largest)


def block_scale(stream_key, dims, split, low, top_value):
    factor_of, own = 1.0, jax.random.fold_in(stream_key, 6)
    for position, blocks in split:
        heights = jnp.exp(jax.random.uniform(jax.random.fold_in(own, position), (blocks,), jnp.float32, low / len(split), top_value / len(split)))
        factor_of = factor_of * jnp.repeat(heights, dims[position] // blocks).reshape([-1 if axis == position else 1 for axis in range(len(dims))])
    return factor_of


def deal_out(own_key, own, number, rows, amount, top, reach, skew):
    ranking = jax.random.permutation(own_key, amount)
    crowded, ordinary = load_shares(amount, rows * top, reach, skew, True), load_shares(amount, rows * top, reach, skew, False)
    places = jnp.arange(amount)

    def named(sizes, rotation):
        used = int((sizes > 0).sum())
        fixed = max(1, used // 4)
        passed = fixed + (places - fixed + rotation * (used - fixed)) % max(1, amount - fixed)
        return jnp.zeros((amount,), jnp.int32).at[ranking[jnp.where(places < fixed, places, passed)]].set(jnp.asarray(sizes, jnp.int32))

    sizes = jnp.where(number % 4 == 0, named(crowded, number // 4), named(ordinary, number - number // 4 - 1))
    mixed = jax.random.permutation(jax.random.fold_in(own, 3), amount)
    giver, receiver = mixed[0:amount // 2 * 2:2], mixed[1:amount // 2 * 2:2]
    margin = jnp.minimum(sizes[giver] - 1, reach - sizes[receiver]) // 2
    margin = jnp.where((giver == ranking[0]) | (receiver == ranking[0]) | (sizes[receiver] == 0), 0, jnp.maximum(margin, 0))
    passed = jax.random.randint(jax.random.fold_in(own, 4), (amount // 2,), 0, 1 << 20) % (margin + 1)
    sizes = sizes.at[giver].add(-passed).at[receiver].add(passed)
    members = jnp.searchsorted(jnp.cumsum(sizes), jnp.arange(rows * top), side="right").astype(jnp.int32)
    table = members.reshape(top, rows).T
    table = table[jax.random.permutation(jax.random.fold_in(own, 1), rows)]
    rotation = jax.random.randint(jax.random.fold_in(own, 2), (rows, 1), 0, top)
    return jnp.take_along_axis(table, (jnp.arange(top)[None, :] + rotation) % top, axis=1)


def load_shares(count, total, reach, skew, full):
    loads = [(1 << 20) // math.isqrt(standing ** skew) + 1 for standing in range(1, count + 1)]
    largest = reach if full else min(reach, max(-(-total // count), total * loads[0] // sum(loads)))
    least = 1 if total - largest >= count - 1 else 0
    holding, surplus = [largest] + [least] * (count - 1), total - largest - least * (count - 1)
    while surplus > 0:
        movable = [i for i in range(1, count) if holding[i] < largest] or [i for i in range(1, count) if holding[i] < reach]
        pool, remaining = sum([loads[i] for i in movable]), surplus
        for i in movable:
            addition = min(reach - holding[i], max(1, remaining * loads[i] // pool), surplus)
            holding[i] = holding[i] + addition
            surplus = surplus - addition
    return np.array(holding)


def noise(stream_key, dims, width, most, split=(), kind=jnp.bfloat16):
    result = width * jax.random.normal(stream_key, dims, jnp.float32)
    if split:
        result = result * block_scale(stream_key, dims, split, -0.22, 0.18)
    return jnp.clip(result, -most, most).astype(kind)


def setup_inputs(seed: int = 0) -> dict:
    splits = jax.random.split(jax.random.key(seed), 8)
    density = noise(splits[0], (LAYERS, NG, NG), 0.5, 4.0, ((0, 4), (1, 8)), jnp.float32)
    layer_top = jnp.clip(jnp.exp(math.log(1.5) - 0.6931472 * jax.random.uniform(splits[1], (LAYERS,), jnp.float32) ** block_scale(splits[1], (LAYERS,), ((0, 4),), -0.2, 0.2)), 0.75, 1.5)
    layer_thick = jnp.clip(1.5 + 1.5 * jax.random.uniform(splits[2], (LAYERS,), jnp.float32) ** block_scale(splits[2], (LAYERS,), ((0, 4),), -0.2, 0.2), 1.5, 3.0)
    sample_row = with_ends(jax.random.randint(splits[3], (TILES, SCAP), 0, TROWS), jax.random.fold_in(splits[3], 1), 0, TROWS - 1).astype(jnp.int32)
    sample_col = with_ends(jax.random.randint(splits[4], (TILES, SCAP), 0, NG), jax.random.fold_in(splits[4], 1), 0, NG - 1).astype(jnp.int32)
    sample_frac = with_ends(jax.random.randint(splits[5], (TILES, 2, SCAP), 0, QLEV), jax.random.fold_in(splits[5], 1), 0, QLEV - 1).astype(jnp.int32)
    sample_owner_keys = jax.random.split(jax.random.fold_in(splits[6], 1), TILES * SCAP // SCAP)
    sample_owner_turns = jax.random.permutation(jax.random.fold_in(splits[6], 3), TILES * SCAP // SCAP)
    sample_owner = jax.vmap(lambda own, number: deal_out(jax.random.fold_in(splits[6], 2), own, number, SCAP, OWNERS, 1, CAP, 2))(sample_owner_keys, sample_owner_turns).reshape((TILES, SCAP, 1))
    return {"density": density, "layer_top": layer_top, "layer_thick": layer_thick, "sample_row": sample_row, "sample_col": sample_col, "sample_frac": sample_frac, "sample_owner": sample_owner}


def cubic_kernel(distance):
    near_part = (1.5 * distance - 2.5) * distance * distance + 1.0
    far_part = ((-0.5 * distance + 2.5) * distance - 4.0) * distance + 2.0
    return jnp.where(distance <= 1.0, near_part, jnp.where(distance < 2.0, far_part, 0.0))

def weight_rows(levels):
    level_ids = jnp.arange(levels, dtype=jnp.int32)
    offsets = (level_ids.astype(jnp.float32) + 0.5) / levels - 0.5
    bases = jnp.where(level_ids < levels // 2, -1.0, 0.0).astype(jnp.float32)
    fraction = offsets - bases
    tap_pos = jnp.arange(4, dtype=jnp.int32).astype(jnp.float32) - 1.0
    return cubic_kernel(jnp.abs(fraction[:, None] - tap_pos[None, :]))

def wavenumber(wave_index, grid_len):
    signed_ids = jnp.where(wave_index < grid_len // 2, wave_index, wave_index - grid_len).astype(jnp.float32)
    full_wave = signed_ids * (2.0 * math.pi / grid_len)
    odd_wave = jnp.where(wave_index == grid_len // 2, 0.0, full_wave)
    return (full_wave, odd_wave)

def reference(density, layer_top, layer_thick, sample_row, sample_col, sample_frac, sample_owner):
    wave_ids = jnp.arange(NG, dtype=jnp.int32)
    full_wave, odd_wave = wavenumber(wave_ids, NG)
    full_y = full_wave[:, None]
    full_x = full_wave[None, :]
    odd_y = odd_wave[:, None]
    odd_x = odd_wave[None, :]
    squared = full_y * full_y + full_x * full_x
    magnitude = jnp.sqrt(squared)
    safe_square = jnp.where(squared > 0.0, squared, 1.0)
    safe_root = jnp.sqrt(safe_square)
    spectrum = None
    for layer in range(LAYERS):
        continuation = 2.0 * math.pi * (1.0 - jnp.exp(-magnitude * layer_thick[layer])) * jnp.exp(-magnitude * layer_top[layer])
        term = jnp.fft.fft2(density[layer]) * continuation
        spectrum = term if layer == 0 else spectrum + term
    channel_list = []
    channel_list.append(jnp.fft.ifft2(spectrum * (-full_x * full_x / safe_square)).real)
    channel_list.append(jnp.fft.ifft2(spectrum * (-odd_x * odd_y / safe_square)).real)
    channel_list.append(jnp.fft.ifft2(spectrum * (1j * (odd_x / safe_root))).real)
    channel_list.append(jnp.fft.ifft2(spectrum * (-full_y * full_y / safe_square)).real)
    channel_list.append(jnp.fft.ifft2(spectrum * (1j * (odd_y / safe_root))).real)
    channel_list.append(jnp.fft.ifft2(spectrum).real)
    gradient_grid = jnp.stack([item.astype(jnp.float32) for item in channel_list])
    weight_table = weight_rows(QLEV)
    tile_ids = jnp.arange(TILES, dtype=jnp.int32)
    frac_y = sample_frac[:, 0, :]
    frac_x = sample_frac[:, 1, :]
    base_y = jnp.where(frac_y < QLEV // 2, -1, 0).astype(jnp.int32)
    base_x = jnp.where(frac_x < QLEV // 2, -1, 0).astype(jnp.int32)
    tap_ids = jnp.arange(4, dtype=jnp.int32)
    row_first = tile_ids[:, None] * TROWS + sample_row + base_y - 1
    col_first = sample_col + base_x - 1
    row_ids = (row_first[:, :, None] + tap_ids) % NG
    col_ids = (col_first[:, :, None] + tap_ids) % NG
    weight_y = weight_table[frac_y]
    weight_x = weight_table[frac_x]
    gathered = gradient_grid[:, row_ids[:, :, :, None], col_ids[:, :, None, :]]
    interpolated = jnp.einsum('ctsab,tsa,tsb->cts', gathered, weight_y, weight_x)
    owner_ids = sample_owner[:, :, 0]
    owner_marks = (owner_ids[:, :, None] == jnp.arange(N_WIDE, dtype=jnp.int32)[None, None, :]).astype(jnp.int32)
    earlier = jnp.cumsum(owner_marks, axis=1) - owner_marks
    slot_ids = lax.optimization_barrier(jnp.sum(earlier * owner_marks, axis=2)).astype(jnp.int32)
    dest_tile = tile_ids[:, None] // N_WIDE * N_WIDE + owner_ids
    dest_col = tile_ids[:, None] % N_WIDE * CAP + slot_ids
    line_samples = jnp.zeros((6, TILES, N_WIDE * CAP), jnp.float32)
    line_samples = line_samples.at[:, dest_tile, dest_col].set(interpolated.astype(jnp.float32))
    return (gradient_grid, line_samples)
```

```python
import functools
import math

import jax
import jax.numpy as jnp
import ml_dtypes
import numpy as np
from jax import lax
from jax.experimental import pallas as pl
from jax.experimental.pallas import tpu as pltpu
from jax.sharding import PartitionSpec as P

RADIX = 128
QLEV = 16
HALF = 64
SLOTS = 16
FIELDS = 5
HIGH = lax.Precision.HIGHEST
VMEM_LIMIT = 56 * 1024 * 1024


def np_split(table):
    high = table.astype(np.float32).astype(ml_dtypes.bfloat16)
    low = (table - high.astype(np.float64)).astype(ml_dtypes.bfloat16)
    return jnp.asarray(high), jnp.asarray(low)


def f32(table):
    return jnp.asarray(np.asarray(table, np.float32))


def angles(left, right, period):
    return (np.outer(left, right) % period) * (2.0 * math.pi / period)


def lane_order():
    column = np.arange(256)
    wave = (column // 128) * HALF + column % HALF
    return wave, (column % 128) // HALF


def slot_zero_angles(grid_len):
    wave, part = lane_order()
    outer_len = grid_len // RADIX
    upper = wave >= HALF
    freq = np.where(upper, outer_len // 2 + outer_len * (wave - HALF), outer_len * wave)
    return wave, part, upper, angles(np.arange(RADIX), freq, grid_len)


def row_forward_tables(grid_len):
    outer_len = grid_len // RADIX
    theta = angles(np.arange(SLOTS), np.arange(outer_len), outer_len)
    first = np.zeros((2 * SLOTS, outer_len))
    first[0::2] = np.cos(theta)
    first[1::2] = -np.sin(theta)
    first[1] = np.cos(np.pi * np.arange(outer_len))
    kron = np.kron(first, np.eye(8))
    wave, part = lane_order()
    alpha = angles(np.arange(RADIX), wave, RADIX)
    base = np.concatenate(
        [
            np.where(part == 0, np.cos(alpha), -np.sin(alpha)),
            np.where(part == 0, np.sin(alpha), np.cos(alpha)),
        ]
    )
    wave, part, upper, alpha = slot_zero_angles(grid_len)
    table = np.where(part == 0, np.cos(alpha), -np.sin(alpha))
    top = np.where(upper, 0.0, table)
    top[:, (wave == 0) & (part == 1)] = np.cos(np.pi * np.arange(RADIX))[:, None]
    zero = np.concatenate([top, np.where(upper, table, 0.0)])
    beta = 2.0 * math.pi * np.arange(RADIX)[:, None] / grid_len * np.ones((1, 256))
    return kron, base, zero, np.cos(beta), np.sin(beta)


def row_inverse_tables(grid_len):
    outer_len = grid_len // RADIX
    theta = angles(np.arange(outer_len), np.arange(SLOTS), outer_len)
    last = np.zeros((outer_len, 2 * SLOTS))
    last[:, 0::2] = np.cos(theta)
    last[:, 1::2] = -np.sin(theta)
    last[:, 1] = np.cos(np.pi * np.arange(outer_len))
    kron = np.kron(last, np.eye(8))
    wave, part = lane_order()
    alpha = angles(wave, np.arange(RADIX), RADIX)
    real_row = (part == 0)[:, None]
    base = 2.0 * np.concatenate(
        [
            np.where(real_row, np.cos(alpha), -np.sin(alpha)),
            np.where(real_row, np.sin(alpha), np.cos(alpha)),
        ],
        axis=1,
    )
    wave, part, upper, alpha = slot_zero_angles(grid_len)
    table = 2.0 * np.where(part == 0, np.cos(alpha), -np.sin(alpha))
    left = np.where(upper, 0.0, table)
    left[:, (wave == 0) & (part == 0)] = 1.0
    left[:, (wave == 0) & (part == 1)] = np.cos(np.pi * np.arange(RADIX))[:, None]
    zero = np.concatenate([left.T, np.where(upper, table, 0.0).T], axis=1)
    beta = 2.0 * math.pi * np.arange(RADIX)[None, :] / grid_len
    return kron, base, zero, np.cos(beta), np.sin(beta)


def column_kron(outer_len, orient):
    theta = angles(np.arange(outer_len), np.arange(outer_len), outer_len)
    return np.concatenate(
        [np.kron(np.cos(theta), np.eye(8)), np.kron(orient * np.sin(theta), np.eye(8))], axis=1
    )


def split(value):
    high = value.astype(jnp.bfloat16)
    return high, (value - high.astype(jnp.float32)).astype(jnp.bfloat16)


def mm(left, right):
    return jnp.dot(left, right, preferred_element_type=jnp.float32)


def dot3(left, right):
    return mm(left[0], right[0]) + mm(left[0], right[1]) + mm(left[1], right[0])


def rotate(value):
    lane = lax.broadcasted_iota(jnp.int32, value.shape, 1)
    return jnp.where(lane < HALF, -1.0, 1.0) * pltpu.roll(value, HALF, 1)


def row_forward_kernel(chunks, x_ref, kh, kl, base, zero, cw, sw, *refs):
    outs = refs[:chunks]
    th, tl, rot, u_ref = refs[chunks:]
    rows = x_ref.shape[0]
    outer_len = x_ref.shape[1] // RADIX

    @pl.when(pl.program_id(0) == 0)
    def _():
        th[0], tl[0] = split(zero[...])
        rot[...] = base[...]
        for slot in range(1, SLOTS):
            top, low = rot[0:RADIX, :], rot[RADIX:, :]
            rot[0:RADIX, :] = cw[...] * top - sw[...] * low
            rot[RADIX:, :] = cw[...] * low + sw[...] * top
            th[slot], tl[slot] = split(rot[...])

    table = (kh[...], kl[...])

    def first(pair, carry):
        halves = [
            jnp.concatenate(
                [
                    x_ref[pl.ds(pair * 16 + 8 * side, 8), RADIX * a : RADIX * (a + 1)]
                    for a in range(outer_len)
                ],
                axis=0,
            )
            for side in range(2)
        ]
        u_ref[pair] = dot3(table, split(jnp.concatenate(halves, axis=1)))
        return carry

    lax.fori_loop(0, rows // 16, first, 0)
    for slot in range(SLOTS):
        parts = []
        for part in range(2):
            at = 16 * slot + 8 * part
            parts.append(
                jnp.concatenate(
                    [
                        u_ref[pair, at : at + 8, RADIX * side : RADIX * (side + 1)]
                        for pair in range(rows // 16)
                        for side in range(2)
                    ],
                    axis=0,
                )
            )
        result = dot3(split(jnp.concatenate(parts, axis=1)), (th[slot], tl[slot]))
        for side in range(2):
            block = 2 * slot + side
            outs[block % chunks][block // chunks] = result[:, RADIX * side : RADIX * (side + 1)]


def full_spec(shape):
    return pl.BlockSpec(shape, lambda *_: (0,) * len(shape))


def row_forward(field, wide_count):
    rows, grid_len = field.shape
    chunks = 2 * SLOTS // wide_count
    step = min(rows, 128)
    kron, base, zero, cw, sw = row_forward_tables(grid_len)
    tables = (*np_split(kron), f32(base), f32(zero), f32(cw), f32(sw))
    return pl.pallas_call(
        functools.partial(row_forward_kernel, chunks),
        grid=(rows // step,),
        in_specs=[pl.BlockSpec((step, grid_len), lambda i: (i, 0))]
        + [full_spec(item.shape) for item in tables],
        out_specs=[pl.BlockSpec((wide_count, step, RADIX), lambda i: (0, i, 0))] * chunks,
        out_shape=[jax.ShapeDtypeStruct((wide_count, rows, RADIX), jnp.float32)] * chunks,
        scratch_shapes=[
            pltpu.VMEM((SLOTS, 256, 256), jnp.bfloat16),
            pltpu.VMEM((SLOTS, 256, 256), jnp.bfloat16),
            pltpu.VMEM((256, 256), jnp.float32),
            pltpu.VMEM((step // 16, 256, 256), jnp.float32),
        ],
        compiler_params=pltpu.CompilerParams(vmem_limit_bytes=VMEM_LIMIT),
        cost_estimate=pl.CostEstimate(
            flops=12 * rows * grid_len * 256, bytes_accessed=8 * rows * grid_len, transcendentals=0
        ),
        name="row_forward",
    )(field, *tables)


def wave_y(first, shape, grid_len):
    outer_len = grid_len // RADIX
    index = first + outer_len * lax.broadcasted_iota(jnp.int32, shape, 0)
    signed = jnp.where(index < grid_len // 2, index, index - grid_len).astype(jnp.float32)
    full = signed * (2.0 * math.pi / grid_len)
    return full, jnp.where(index == grid_len // 2, 0.0, full)


def column_forward_kernel(
    grid_len, depth_ref, x_ref, kx_ref, kh, kl, ca, sa, cw, sw, out_ref, u_ref, c_ref, s_ref
):
    outer_len = grid_len // RADIX
    table = (kh[...], kl[...])

    def first(pair, carry):
        halves = [
            jnp.concatenate(
                [x_ref[pl.ds(a * RADIX + pair * 16 + 8 * side, 8), :] for a in range(outer_len)],
                axis=0,
            )
            for side in range(2)
        ]
        turned = [rotate(half) for half in halves]
        data = jnp.concatenate(
            [jnp.concatenate(halves, axis=1), jnp.concatenate(turned, axis=1)], axis=0
        )
        result = dot3(table, split(data))
        for k1 in range(outer_len):
            for side in range(2):
                u_ref[pl.ds(k1 * RADIX + pair * 16 + 8 * side, 8), :] = result[
                    8 * k1 : 8 * k1 + 8, RADIX * side : RADIX * (side + 1)
                ]
        return carry

    lax.fori_loop(0, RADIX // 16, first, 0)
    c_ref[...] = ca[...]
    s_ref[...] = sa[...]
    top, thick = depth_ref[0], depth_ref[1]

    def second(k1, carry):
        cosine, sine = c_ref[...], s_ref[...]
        table = split(jnp.concatenate([cosine, sine], axis=1))
        c_ref[...] = cosine * cw[...] - sine * sw[...]
        s_ref[...] = sine * cw[...] + cosine * sw[...]
        rows = pl.ds(pl.multiple_of(k1 * RADIX, RADIX), RADIX)
        data = u_ref[rows, :]
        result = dot3(table, split(jnp.concatenate([data, rotate(data)], axis=0)))
        full_y, _ = wave_y(k1, (RADIX, RADIX), grid_len)
        magnitude = jnp.sqrt(kx_ref[...] * kx_ref[...] + full_y * full_y)
        scale = (1.0 - jnp.exp(-magnitude * thick)) * jnp.exp(-magnitude * top)
        out_ref[rows, :] = result * (scale * (2.0 * math.pi / (grid_len * grid_len)))
        return carry

    lax.fori_loop(0, outer_len, second, 0, unroll=2)


def column_forward(block, wave_x, depths):
    grid_len = block.shape[0]
    outer_len = grid_len // RADIX
    alpha = angles(np.arange(RADIX), np.arange(RADIX), RADIX)
    beta = 2.0 * math.pi * np.arange(RADIX)[None, :] / grid_len
    tables = (
        *np_split(column_kron(outer_len, -1.0)),
        f32(np.cos(alpha)),
        f32(-np.sin(alpha)),
        f32(np.cos(beta)),
        f32(-np.sin(beta)),
    )
    square = (RADIX, RADIX)
    return pl.pallas_call(
        functools.partial(column_forward_kernel, grid_len),
        in_specs=[pl.BlockSpec(memory_space=pltpu.SMEM)]
        + [pl.BlockSpec(memory_space=pltpu.VMEM)] * (2 + len(tables)),
        out_specs=pl.BlockSpec(memory_space=pltpu.VMEM),
        out_shape=jax.ShapeDtypeStruct(block.shape, jnp.float32),
        scratch_shapes=[
            pltpu.VMEM((grid_len, RADIX), jnp.float32),
            pltpu.VMEM(square, jnp.float32),
            pltpu.VMEM(square, jnp.float32),
        ],
        compiler_params=pltpu.CompilerParams(vmem_limit_bytes=VMEM_LIMIT),
        cost_estimate=pl.CostEstimate(
            flops=24 * grid_len * RADIX * 256,
            bytes_accessed=8 * grid_len * RADIX,
            transcendentals=2 * grid_len * RADIX,
        ),
        name="column_forward",
    )(depths, block, wave_x, *tables)


def column_inverse_kernel(
    grid_len, tile_rows, special, flag_ref, s_in, kx_ref, kxo_ref, bh, bl, ca, sa, cw, sw, *refs
):
    if special:
        edge_ref, out_ref, v_ref, c_ref, s_ref = refs
    else:
        out_ref, v_ref, c_ref, s_ref = refs
    outer_len = grid_len // RADIX
    here = bh.shape[0] // 8
    c_ref[...] = ca[...]
    s_ref[...] = sa[...]

    def first(k1, carry):
        cosine, sine = c_ref[...], s_ref[...]
        table = split(jnp.concatenate([cosine, sine], axis=1))
        c_ref[...] = cosine * cw[...] - sine * sw[...]
        s_ref[...] = sine * cw[...] + cosine * sw[...]
        rows = pl.ds(pl.multiple_of(k1 * RADIX, RADIX), RADIX)
        full_y, odd_y = wave_y(k1, (RADIX, RADIX), grid_len)
        full_x, odd_x = kx_ref[...], kxo_ref[...]
        squared = full_x * full_x + full_y * full_y
        safe = jnp.where(squared > 0.0, squared, 1.0)
        root = lax.rsqrt(safe)
        inverse = root * root
        value = s_in[rows, :]
        turned = rotate(value)
        coef_xx = -full_x * full_x * inverse
        coef_xy = -odd_x * odd_y * inverse
        coef_yy = -full_y * full_y * inverse
        slope_x = odd_x * root
        slope_y = odd_y * root
        upper = [
            value * coef_xx,
            value * coef_xy,
            turned * slope_x,
            value * coef_yy,
            turned * slope_y,
        ]
        lower = [
            turned * coef_xx,
            turned * coef_xy,
            -value * slope_x,
            turned * coef_yy,
            -value * slope_y,
        ]
        data = jnp.concatenate(
            [jnp.concatenate(upper, axis=1), jnp.concatenate(lower, axis=1)], axis=0
        )
        v_ref[rows, :] = dot3(table, split(data))
        return carry

    lax.fori_loop(0, outer_len, first, 0)
    both = jnp.concatenate([bh[...], bl[...]], axis=0)
    span = 8 * here

    def second(group, carry):
        data = jnp.concatenate(
            [v_ref[pl.ds(k1 * RADIX + group * 8, 8), :] for k1 in range(outer_len)], axis=0
        )
        turned = jnp.concatenate(
            [rotate(data[:, RADIX * c : RADIX * (c + 1)]) for c in range(FIELDS)], axis=1
        )
        high, low = split(jnp.concatenate([data, turned], axis=0))
        stacked = mm(both, high)
        result = stacked[:span] + stacked[span:] + mm(bh[...], low)
        per_row = RADIX // tile_rows
        row = (group * 8) % tile_rows
        for a in range(here):
            dest = a * per_row + (group * 8) // tile_rows
            for c in range(FIELDS):
                piece = result[8 * a : 8 * a + 8, RADIX * c : RADIX * (c + 1)]
                if special:
                    lane = lax.broadcasted_iota(jnp.int32, piece.shape, 1)
                    edge = edge_ref[c, pl.ds(a * RADIX + group * 8, 8), :]
                    edge = jnp.where(lane < HALF, edge[:, 0:1], edge[:, 1:2])
                    piece = jnp.where((lane % HALF == 0) & (flag_ref[0] == 0), edge, piece)
                out_ref[dest, c, pl.ds(row, 8), :] = piece
        return carry

    lax.fori_loop(0, RADIX // 8, second, 0)


def column_inverse(block, wave_x, odd_x, share, flag, edge, wide_count, tile_rows):
    grid_len = block.shape[0]
    alpha = angles(np.arange(RADIX), np.arange(RADIX), RADIX)
    beta = 2.0 * math.pi * np.arange(RADIX)[:, None] / grid_len * np.ones((1, RADIX))
    tables = (
        *share,
        f32(np.cos(alpha)),
        f32(np.sin(alpha)),
        f32(np.cos(beta)),
        f32(np.sin(beta)),
    )
    if edge is not None:
        tables = tables + (edge,)
    square = (RADIX, RADIX)
    out_shape = (wide_count, FIELDS, tile_rows, RADIX)
    return pl.pallas_call(
        functools.partial(column_inverse_kernel, grid_len, tile_rows, edge is not None),
        in_specs=[pl.BlockSpec(memory_space=pltpu.SMEM)]
        + [pl.BlockSpec(memory_space=pltpu.VMEM)] * (3 + len(tables)),
        out_specs=pl.BlockSpec(memory_space=pltpu.VMEM),
        out_shape=jax.ShapeDtypeStruct(out_shape, jnp.float32),
        scratch_shapes=[
            pltpu.VMEM((grid_len, FIELDS * RADIX), jnp.float32),
            pltpu.VMEM(square, jnp.float32),
            pltpu.VMEM(square, jnp.float32),
        ],
        compiler_params=pltpu.CompilerParams(vmem_limit_bytes=VMEM_LIMIT),
        cost_estimate=pl.CostEstimate(
            flops=FIELDS * 18 * grid_len * RADIX * 256,
            bytes_accessed=4 * (grid_len * RADIX + math.prod(out_shape)),
            transcendentals=grid_len * RADIX,
        ),
        name="column_inverse",
    )(flag, block, wave_x, odd_x, *tables)


def row_inverse_kernel(chunks, *refs):
    ins = refs[:chunks]
    kh, kl, base, zero, cw, sw, out_ref, th, tl, rot, u_ref = refs[chunks:]
    rows = ins[0].shape[2]
    outer_len = out_ref.shape[2] // RADIX

    @pl.when(pl.program_id(0) == 0)
    def _():
        th[0], tl[0] = split(zero[...])
        rot[...] = base[...]
        for slot in range(1, SLOTS):
            left, right = rot[:, 0:RADIX], rot[:, RADIX:]
            rot[:, 0:RADIX] = cw[...] * left - sw[...] * right
            rot[:, RADIX:] = cw[...] * right + sw[...] * left
            th[slot], tl[slot] = split(rot[...])

    for slot in range(SLOTS):
        parts = []
        for side in range(2):
            block = 2 * slot + side
            item = ins[block % chunks][block // chunks]
            parts.append(item.reshape(FIELDS * rows, RADIX))
        u_ref[slot] = dot3(split(jnp.concatenate(parts, axis=1)), (th[slot], tl[slot]))

    table = (kh[...], kl[...])
    for c in range(FIELDS):

        def second(pair, carry):
            halves = []
            for side in range(2):
                at = pl.ds(c * rows + pair * 16 + 8 * side, 8)
                halves.append(
                    jnp.concatenate(
                        [
                            u_ref[slot, at, RADIX * part : RADIX * (part + 1)]
                            for slot in range(SLOTS)
                            for part in range(2)
                        ],
                        axis=0,
                    )
                )
            result = dot3(table, split(jnp.concatenate(halves, axis=1)))
            for a in range(outer_len):
                for side in range(2):
                    out_ref[
                        c, pl.ds(pair * 16 + 8 * side, 8), RADIX * a : RADIX * (a + 1)
                    ] = result[8 * a : 8 * a + 8, RADIX * side : RADIX * (side + 1)]
            return carry

        lax.fori_loop(0, rows // 16, second, 0)
    out_ref[FIELDS] = -(out_ref[0] + out_ref[3])


def row_inverse(blocks, grid_len):
    chunks = len(blocks)
    wide_count, _, rows, _ = blocks[0].shape
    step = min(rows, 32)
    kron, base, zero, cw, sw = row_inverse_tables(grid_len)
    tables = (*np_split(kron), f32(base), f32(zero), f32(cw), f32(sw))
    return pl.pallas_call(
        functools.partial(row_inverse_kernel, chunks),
        grid=(rows // step,),
        in_specs=[pl.BlockSpec((wide_count, FIELDS, step, RADIX), lambda i: (0, 0, i, 0))] * chunks
        + [full_spec(item.shape) for item in tables],
        out_specs=pl.BlockSpec((FIELDS + 1, step, grid_len), lambda i: (0, i, 0)),
        out_shape=jax.ShapeDtypeStruct((FIELDS + 1, rows, grid_len), jnp.float32),
        scratch_shapes=[
            pltpu.VMEM((SLOTS, 256, 256), jnp.bfloat16),
            pltpu.VMEM((SLOTS, 256, 256), jnp.bfloat16),
            pltpu.VMEM((256, 256), jnp.float32),
            pltpu.VMEM((SLOTS, FIELDS * step, 256), jnp.float32),
        ],
        compiler_params=pltpu.CompilerParams(vmem_limit_bytes=VMEM_LIMIT),
        cost_estimate=pl.CostEstimate(
            flops=12 * FIELDS * rows * grid_len * 256,
            bytes_accessed=44 * rows * grid_len,
            transcendentals=0,
        ),
        name="row_inverse",
    )(*blocks, *tables)


def interpolate_kernel(g_ref, halo_ref, wy_ref, col_ref, wx_ref, place_ref, out_ref, mask_ref):
    samples, grid_len = mask_ref.shape
    wide = 512

    @pl.when(pl.program_id(0) == 0)
    def _():
        for start in range(0, grid_len, wide):
            lane = start + lax.broadcasted_iota(jnp.int32, (samples, wide), 1)
            total = jnp.zeros((samples, wide), jnp.float32)
            for tap in range(4):
                total = total + jnp.where(
                    lane == col_ref[:, tap : tap + 1], wx_ref[:, tap : tap + 1], 0.0
                )
            mask_ref[:, start : start + wide] = total

    left = split(wy_ref[...])
    partial = jnp.zeros((samples, RADIX), jnp.float32)
    for start in range(0, grid_len, wide):
        at = slice(start, start + wide)
        data = jnp.concatenate([g_ref[0, :, at], halo_ref[0, :, at]], axis=0)
        product = dot3(left, split(data)) * mask_ref[:, at]
        for lane in range(0, wide, RADIX):
            partial = partial + product[:, lane : lane + RADIX]
    value = jnp.sum(partial, axis=1, keepdims=True)
    out_ref[0] = jnp.sum(value * place_ref[...], axis=0, keepdims=True)


def interpolate(gradient, halo, weight_y, col_ids, weight_x, placement):
    fields, rows, grid_len = gradient.shape
    samples, slot_total = placement.shape
    small = (weight_y, col_ids, weight_x, placement)
    return pl.pallas_call(
        interpolate_kernel,
        grid=(fields,),
        in_specs=[
            pl.BlockSpec((1, rows, grid_len), lambda i: (i, 0, 0)),
            pl.BlockSpec((1, 8, grid_len), lambda i: (i, 0, 0)),
        ]
        + [full_spec(item.shape) for item in small],
        out_specs=pl.BlockSpec((1, 1, slot_total), lambda i: (i, 0, 0)),
        out_shape=jax.ShapeDtypeStruct((fields, 1, slot_total), jnp.float32),
        scratch_shapes=[pltpu.VMEM((samples, grid_len), jnp.float32)],
        compiler_params=pltpu.CompilerParams(vmem_limit_bytes=VMEM_LIMIT),
        name="interpolate",
    )(gradient, halo, *small)


def product(formula, operand_a, operand_b):
    return jnp.einsum(formula, operand_a, operand_b, precision=HIGH)


def complex_product(formula, pair, table):
    return (
        product(formula, pair[0], table[0]) - product(formula, pair[1], table[1]),
        product(formula, pair[0], table[1]) + product(formula, pair[1], table[0]),
    )


def phase(row_count, col_count, period, orient):
    theta = angles(np.arange(row_count), np.arange(col_count), period)
    return f32(np.cos(theta)), f32(orient * np.sin(theta))


def times_table(pair, table):
    return (
        pair[0] * table[0] - pair[1] * table[1],
        pair[0] * table[1] + pair[1] * table[0],
    )


def edge_waves(grid_len):
    outer_len = grid_len // RADIX
    index = np.arange(outer_len)[:, None] + outer_len * np.arange(RADIX)[None, :]
    signed = np.where(index < grid_len // 2, index, index - grid_len).astype(np.float32)
    full_y = signed * np.float32(2.0 * math.pi / grid_len)
    odd_y = np.where(index == grid_len // 2, np.float32(0.0), full_y)
    return full_y, odd_y


def edge_forward(values, layer_top, layer_thick):
    grid_len = values.shape[1]
    outer_len = grid_len // RADIX
    columns = values.reshape(2, outer_len, RADIX)
    first = phase(outer_len, outer_len, outer_len, -1.0)
    pair = (product("zab,ka->zkb", columns, first[0]), product("zab,ka->zkb", columns, first[1]))
    pair = times_table(pair, phase(outer_len, RADIX, grid_len, -1.0))
    pair = complex_product("zkb,bc->zkc", pair, phase(RADIX, RADIX, RADIX, -1.0))
    full_y, _ = edge_waves(grid_len)
    magnitude = jnp.sqrt(
        jnp.asarray(np.stack([full_y * full_y, full_y * full_y + np.float32(math.pi) ** 2]))
    )
    scale = (
        2.0
        * math.pi
        / (grid_len * grid_len)
        * (1.0 - jnp.exp(-magnitude * layer_thick))
        * jnp.exp(-magnitude * layer_top)
    )
    return jnp.stack([pair[0] * scale, pair[1] * scale])


def edge_inverse(total, row_start, row_share):
    outer_len = total.shape[2]
    grid_len = outer_len * RADIX
    full_y, odd_y = edge_waves(grid_len)
    full_x = np.array([0.0, math.pi], np.float32)[:, None, None]
    squared = full_x * full_x + full_y * full_y
    safe = np.where(squared > 0.0, squared, np.float32(1.0))
    none = np.zeros_like(safe)
    plain = f32(np.stack([-full_x * full_x / safe, none, none, -full_y * full_y / safe, none]))
    turned = f32(np.stack([none, none, none, none, odd_y / np.sqrt(safe)]))
    pair = (total[0] * plain - total[1] * turned, total[1] * plain + total[0] * turned)
    pair = complex_product("fzkc,cb->fzkb", pair, phase(RADIX, RADIX, RADIX, 1.0))
    pair = times_table(pair, phase(outer_len, RADIX, grid_len, 1.0))
    last = phase(outer_len, outer_len, outer_len, 1.0)
    last = [lax.dynamic_slice_in_dim(item, row_start, row_share, 0) for item in last]
    real = product("fzkb,ak->fzab", pair[0], last[0]) - product("fzkb,ak->fzab", pair[1], last[1])
    return jnp.moveaxis(real.reshape(FIELDS, 2, row_share * RADIX), 1, 2)


def cubic_kernel(distance):
    near_part = (1.5 * distance - 2.5) * distance * distance + 1.0
    far_part = ((-0.5 * distance + 2.5) * distance - 4.0) * distance + 2.0
    return jnp.where(distance <= 1.0, near_part, jnp.where(distance < 2.0, far_part, 0.0))


def tap_weights(level):
    offset = (level.astype(jnp.float32) + 0.5) / QLEV - 0.5
    base = jnp.where(level < QLEV // 2, -1, 0).astype(jnp.int32)
    fraction = offset - base.astype(jnp.float32)
    taps = jnp.arange(4, dtype=jnp.int32)[None, :]
    weights = cubic_kernel(jnp.abs(fraction[:, None] - (taps.astype(jnp.float32) - 1.0)))
    return weights, base[:, None] - 1 + taps


def depth_sum(blocks):
    return [lax.psum(block, "depth") for block in blocks]


def per_device(density, layer_top, layer_thick, sample_row, sample_col, sample_frac, sample_owner):
    wide_count = lax.axis_size("wide")
    depth_count = lax.axis_size("depth")
    rows_here, grid_len = density.shape[1], density.shape[2]
    outer_len = grid_len // RADIX
    tile_rows = rows_here // depth_count
    chunks = 2 * SLOTS // wide_count
    wide_id, depth_id = lax.axis_index("wide"), lax.axis_index("depth")

    def exchange(block):
        return lax.all_to_all(block, "wide", split_axis=0, concat_axis=0, tiled=True)

    spectra = [exchange(item) for item in row_forward(density[0], wide_count)]
    columns = [item.reshape(grid_len, RADIX) for item in spectra]

    lane = jnp.arange(RADIX, dtype=jnp.int32)[None, :] % HALF
    waves = []
    for chunk in range(chunks):
        block = wide_id * chunks + chunk
        slot = block // 2
        place = (block % 2) * HALF + lane
        low = jnp.where(
            place < HALF, outer_len * place, outer_len // 2 + outer_len * (place - HALF)
        )
        index = jnp.where(slot == 0, low, slot + outer_len * place)
        signed = jnp.where(index < grid_len // 2, index, index - grid_len).astype(jnp.float32)
        waves.append(signed * (2.0 * math.pi / grid_len))

    depths = jnp.concatenate([layer_top, layer_thick])
    edge = edge_forward(
        jnp.stack([columns[0][:, 0], columns[0][:, HALF]]), layer_top[0], layer_thick[0]
    )
    summed = depth_sum([column_forward(c, w, depths) for c, w in zip(columns, waves)])
    row_share = outer_len // depth_count
    row_start = depth_id * row_share
    edge = edge_inverse(lax.psum(edge, "depth"), row_start, row_share)
    back = np_split(column_kron(outer_len, 1.0))
    share = [lax.dynamic_slice_in_dim(item, row_start * 8, row_share * 8, 0) for item in back]
    flag = wide_id.astype(jnp.int32).reshape(1)
    blocks = []
    for chunk in range(chunks):
        item = column_inverse(
            summed[chunk],
            waves[chunk],
            waves[chunk],
            share,
            flag,
            edge if chunk == 0 else None,
            wide_count,
            tile_rows,
        )
        blocks.append(exchange(item))
    gradient = row_inverse(blocks, grid_len)

    tiles = depth_count * wide_count
    forward = [(i, (i + 1) % tiles) for i in range(tiles)]
    backward = [(target, source) for source, target in forward]
    low = lax.ppermute(gradient[:, tile_rows - 2 :], ("depth", "wide"), forward)
    high = lax.ppermute(gradient[:, :2], ("depth", "wide"), backward)
    halo = jnp.concatenate(
        [low, high, jnp.zeros((FIELDS + 1, 4, grid_len), jnp.float32)], axis=1
    )

    taps_y, offset_y = tap_weights(sample_frac[0, 0])
    taps_x, offset_x = tap_weights(sample_frac[0, 1])
    row_ids = sample_row[0][:, None] + offset_y
    col_ids = (sample_col[0][:, None] + offset_x) % grid_len
    row_ids = jnp.where(
        row_ids < 0,
        row_ids + tile_rows + 2,
        jnp.where(row_ids >= tile_rows, row_ids + 2, row_ids),
    )
    row_marks = row_ids[:, :, None] == jnp.arange(tile_rows + 8, dtype=jnp.int32)
    weight_y = jnp.sum(jnp.where(row_marks, taps_y[:, :, None], 0.0), axis=1)
    sample_count = sample_row.shape[1]
    capacity = max(2 * sample_count // wide_count, 2)
    slot_total = wide_count * capacity
    owner_ids = sample_owner[0, :, 0]
    same = owner_ids[:, None] == owner_ids[None, :]
    order = jnp.arange(sample_count, dtype=jnp.int32)
    slot_ids = jnp.sum((same & (order[None, :] < order[:, None])).astype(jnp.int32), axis=1)
    target = owner_ids * capacity + slot_ids
    placement = (target[:, None] == jnp.arange(slot_total, dtype=jnp.int32)[None, :]).astype(
        jnp.float32
    )
    outgoing = interpolate(gradient, halo, weight_y, col_ids, taps_x, placement)
    outgoing = outgoing.reshape(FIELDS + 1, wide_count, capacity)
    arrived = lax.all_to_all(outgoing, "wide", split_axis=1, concat_axis=1, tiled=True)
    return (gradient, arrived.reshape(FIELDS + 1, 1, slot_total))


def solution(mesh):
    in_specs = (
        P("depth", "wide", None),
        P("depth"),
        P("depth"),
        P(("depth", "wide"), None),
        P(("depth", "wide"), None),
        P(("depth", "wide"), None, None),
        P(("depth", "wide"), None, None),
    )
    out_specs = (P(None, ("depth", "wide"), None), P(None, ("depth", "wide"), None))
    return jax.shard_map(
        per_device, mesh=mesh, in_specs=in_specs, out_specs=out_specs, check_vma=False
    )
```

```python
import functools
import math

import jax
import jax.numpy as jnp
import ml_dtypes
import numpy as np
from jax import lax
from jax.experimental import pallas as pl
from jax.experimental.pallas import tpu as pltpu
from jax.sharding import PartitionSpec as P

RADIX = 128
QLEV = 16
HALF = 64
SLOTS = 16
FIELDS = 5
EDGE_STEP = 2
HIGH = lax.Precision.HIGHEST
VMEM_LIMIT = 56 * 1024 * 1024


def np_split(table):
    high = table.astype(np.float32).astype(ml_dtypes.bfloat16)
    low = (table - high.astype(np.float64)).astype(ml_dtypes.bfloat16)
    return jnp.asarray(high), jnp.asarray(low)


def f32(table):
    return jnp.asarray(np.asarray(table, np.float32))


def angles(left, right, period):
    return (np.outer(left, right) % period) * (2.0 * math.pi / period)


def lane_order():
    column = np.arange(256)
    wave = (column // 128) * HALF + column % HALF
    return wave, (column % 128) // HALF


def slot_zero_angles(grid_len):
    wave, part = lane_order()
    outer_len = grid_len // RADIX
    upper = wave >= HALF
    freq = np.where(upper, outer_len // 2 + outer_len * (wave - HALF), outer_len * wave)
    return wave, part, upper, angles(np.arange(RADIX), freq, grid_len)


def row_forward_tables(grid_len):
    outer_len = grid_len // RADIX
    theta = angles(np.arange(SLOTS), np.arange(outer_len), outer_len)
    first = np.zeros((2 * SLOTS, outer_len))
    first[0::2] = np.cos(theta)
    first[1::2] = -np.sin(theta)
    first[1] = np.cos(np.pi * np.arange(outer_len))
    kron = np.kron(first, np.eye(8))
    wave, part = lane_order()
    alpha = angles(np.arange(RADIX), wave, RADIX)
    base = np.concatenate(
        [
            np.where(part == 0, np.cos(alpha), -np.sin(alpha)),
            np.where(part == 0, np.sin(alpha), np.cos(alpha)),
        ]
    )
    wave, part, upper, alpha = slot_zero_angles(grid_len)
    table = np.where(part == 0, np.cos(alpha), -np.sin(alpha))
    top = np.where(upper, 0.0, table)
    top[:, (wave == 0) & (part == 1)] = np.cos(np.pi * np.arange(RADIX))[:, None]
    zero = np.concatenate([top, np.where(upper, table, 0.0)])
    beta = 2.0 * math.pi * np.arange(RADIX)[:, None] / grid_len * np.ones((1, 256))
    return kron, base, zero, np.cos(beta), np.sin(beta)


def row_inverse_tables(grid_len):
    outer_len = grid_len // RADIX
    theta = angles(np.arange(outer_len), np.arange(SLOTS), outer_len)
    last = np.zeros((outer_len, 2 * SLOTS))
    last[:, 0::2] = np.cos(theta)
    last[:, 1::2] = -np.sin(theta)
    last[:, 1] = np.cos(np.pi * np.arange(outer_len))
    kron = np.kron(last, np.eye(8))
    wave, part = lane_order()
    alpha = angles(wave, np.arange(RADIX), RADIX)
    real_row = (part == 0)[:, None]
    base = 2.0 * np.concatenate(
        [
            np.where(real_row, np.cos(alpha), -np.sin(alpha)),
            np.where(real_row, np.sin(alpha), np.cos(alpha)),
        ],
        axis=1,
    )
    wave, part, upper, alpha = slot_zero_angles(grid_len)
    table = 2.0 * np.where(part == 0, np.cos(alpha), -np.sin(alpha))
    left = np.where(upper, 0.0, table)
    left[:, (wave == 0) & (part == 0)] = 1.0
    left[:, (wave == 0) & (part == 1)] = np.cos(np.pi * np.arange(RADIX))[:, None]
    zero = np.concatenate([left.T, np.where(upper, table, 0.0).T], axis=1)
    beta = 2.0 * math.pi * np.arange(RADIX)[None, :] / grid_len
    return kron, base, zero, np.cos(beta), np.sin(beta)


def column_kron(outer_len, orient):
    theta = angles(np.arange(outer_len), np.arange(outer_len), outer_len)
    return np.concatenate(
        [np.kron(np.cos(theta), np.eye(8)), np.kron(orient * np.sin(theta), np.eye(8))], axis=1
    )


def split(value):
    high = value.astype(jnp.bfloat16)
    return high, (value - high.astype(jnp.float32)).astype(jnp.bfloat16)


def mm(left, right):
    return jnp.dot(left, right, preferred_element_type=jnp.float32)


def dot3(left, right):
    rows = left[0].shape[0]
    both = mm(jnp.concatenate(left, axis=0), right[0])
    return both[:rows] + both[rows:] + mm(left[0], right[1])


def rotate(value):
    lane = lax.broadcasted_iota(jnp.int32, value.shape, 1)
    return jnp.where(lane < HALF, -1.0, 1.0) * pltpu.roll(value, HALF, 1)


def row_forward_kernel(chunks, x_ref, kh, kl, base, zero, cw, sw, *refs):
    outs = refs[:chunks]
    th, tl, rot, u_ref = refs[chunks:]
    rows = x_ref.shape[0]
    outer_len = x_ref.shape[1] // RADIX

    @pl.when(pl.program_id(0) == 0)
    def _():
        th[0], tl[0] = split(zero[...])
        rot[...] = base[...]
        for slot in range(1, SLOTS):
            top, low = rot[0:RADIX, :], rot[RADIX:, :]
            rot[0:RADIX, :] = cw[...] * top - sw[...] * low
            rot[RADIX:, :] = cw[...] * low + sw[...] * top
            th[slot], tl[slot] = split(rot[...])

    table = (kh[...], kl[...])

    def first(pair, carry):
        halves = [
            jnp.concatenate(
                [
                    x_ref[pl.ds(pair * 16 + 8 * side, 8), RADIX * a : RADIX * (a + 1)]
                    for a in range(outer_len)
                ],
                axis=0,
            )
            for side in range(2)
        ]
        u_ref[pair] = dot3(table, split(jnp.concatenate(halves, axis=1)))
        return carry

    lax.fori_loop(0, rows // 16, first, 0)
    for slot in range(SLOTS):
        parts = []
        for part in range(2):
            at = 16 * slot + 8 * part
            parts.append(
                jnp.concatenate(
                    [
                        u_ref[pair, at : at + 8, RADIX * side : RADIX * (side + 1)]
                        for pair in range(rows // 16)
                        for side in range(2)
                    ],
                    axis=0,
                )
            )
        result = dot3(split(jnp.concatenate(parts, axis=1)), (th[slot], tl[slot]))
        for side in range(2):
            block = 2 * slot + side
            outs[block % chunks][block // chunks] = result[:, RADIX * side : RADIX * (side + 1)]


def full_spec(shape):
    return pl.BlockSpec(shape, lambda *_: (0,) * len(shape))


def row_forward(field, wide_count):
    rows, grid_len = field.shape
    chunks = 2 * SLOTS // wide_count
    step = min(rows, 128)
    kron, base, zero, cw, sw = row_forward_tables(grid_len)
    tables = (*np_split(kron), f32(base), f32(zero), f32(cw), f32(sw))
    return pl.pallas_call(
        functools.partial(row_forward_kernel, chunks),
        grid=(rows // step,),
        in_specs=[pl.BlockSpec((step, grid_len), lambda i: (i, 0))]
        + [full_spec(item.shape) for item in tables],
        out_specs=[pl.BlockSpec((wide_count, step, RADIX), lambda i: (0, i, 0))] * chunks,
        out_shape=[jax.ShapeDtypeStruct((wide_count, rows, RADIX), jnp.float32)] * chunks,
        scratch_shapes=[
            pltpu.VMEM((SLOTS, 256, 256), jnp.bfloat16),
            pltpu.VMEM((SLOTS, 256, 256), jnp.bfloat16),
            pltpu.VMEM((256, 256), jnp.float32),
            pltpu.VMEM((step // 16, 256, 256), jnp.float32),
        ],
        compiler_params=pltpu.CompilerParams(vmem_limit_bytes=VMEM_LIMIT),
        cost_estimate=pl.CostEstimate(
            flops=12 * rows * grid_len * 256, bytes_accessed=8 * rows * grid_len, transcendentals=0
        ),
        name="row_forward",
    )(field, *tables)


def wave_y(first, shape, grid_len):
    outer_len = grid_len // RADIX
    index = first + outer_len * lax.broadcasted_iota(jnp.int32, shape, 0)
    signed = jnp.where(index < grid_len // 2, index, index - grid_len).astype(jnp.float32)
    full = signed * (2.0 * math.pi / grid_len)
    return full, jnp.where(index == grid_len // 2, 0.0, full)


def column_forward_kernel(
    grid_len, depth_ref, x_ref, kx_ref, kh, kl, ca, sa, cw, sw, low_ref, high_ref, *scratch
):
    u_ref, c_ref, s_ref = scratch
    outer_len = grid_len // RADIX
    table = (kh[...], kl[...])

    def first(pair, carry):
        halves = [
            jnp.concatenate(
                [x_ref[pl.ds(a * RADIX + pair * 16 + 8 * side, 8), :] for a in range(outer_len)],
                axis=0,
            )
            for side in range(2)
        ]
        turned = [rotate(half) for half in halves]
        data = jnp.concatenate(
            [jnp.concatenate(halves, axis=1), jnp.concatenate(turned, axis=1)], axis=0
        )
        result = dot3(table, split(data))
        for k1 in range(outer_len):
            for side in range(2):
                u_ref[pl.ds(k1 * RADIX + pair * 16 + 8 * side, 8), :] = result[
                    8 * k1 : 8 * k1 + 8, RADIX * side : RADIX * (side + 1)
                ]
        return carry

    lax.fori_loop(0, RADIX // 16, first, 0)
    c_ref[...] = ca[...]
    s_ref[...] = sa[...]
    top, thick = depth_ref[0], depth_ref[1]

    middle = outer_len // 2

    def second(out_ref, start, step, carry):
        k1 = start + step
        cosine, sine = c_ref[...], s_ref[...]
        table = split(jnp.concatenate([cosine, sine], axis=1))
        c_ref[...] = cosine * cw[...] - sine * sw[...]
        s_ref[...] = sine * cw[...] + cosine * sw[...]
        rows = pl.ds(pl.multiple_of(k1 * RADIX, RADIX), RADIX)
        data = u_ref[rows, :]
        result = dot3(table, split(jnp.concatenate([data, rotate(data)], axis=0)))
        full_y, _ = wave_y(k1, (RADIX, RADIX), grid_len)
        magnitude = jnp.sqrt(kx_ref[...] * kx_ref[...] + full_y * full_y)
        scale = (1.0 - jnp.exp(-magnitude * thick)) * jnp.exp(-magnitude * top)
        out_ref[pl.ds(pl.multiple_of(step * RADIX, RADIX), RADIX), :] = result * (
            scale * (2.0 * math.pi / (grid_len * grid_len))
        )
        return carry

    lax.fori_loop(0, middle, functools.partial(second, low_ref, 0), 0, unroll=2)
    lax.fori_loop(0, middle, functools.partial(second, high_ref, middle), 0, unroll=2)


def column_forward(block, wave_x, depths):
    grid_len = block.shape[0]
    outer_len = grid_len // RADIX
    alpha = angles(np.arange(RADIX), np.arange(RADIX), RADIX)
    beta = 2.0 * math.pi * np.arange(RADIX)[None, :] / grid_len
    tables = (
        *np_split(column_kron(outer_len, -1.0)),
        f32(np.cos(alpha)),
        f32(-np.sin(alpha)),
        f32(np.cos(beta)),
        f32(-np.sin(beta)),
    )
    square = (RADIX, RADIX)
    return pl.pallas_call(
        functools.partial(column_forward_kernel, grid_len),
        in_specs=[pl.BlockSpec(memory_space=pltpu.SMEM)]
        + [pl.BlockSpec(memory_space=pltpu.VMEM)] * (2 + len(tables)),
        out_specs=[pl.BlockSpec(memory_space=pltpu.VMEM)] * 2,
        out_shape=[jax.ShapeDtypeStruct((grid_len // 2, RADIX), jnp.float32)] * 2,
        scratch_shapes=[
            pltpu.VMEM((grid_len, RADIX), jnp.float32),
            pltpu.VMEM(square, jnp.float32),
            pltpu.VMEM(square, jnp.float32),
        ],
        compiler_params=pltpu.CompilerParams(vmem_limit_bytes=VMEM_LIMIT),
        cost_estimate=pl.CostEstimate(
            flops=100 * grid_len * RADIX * 256,
            bytes_accessed=8 * grid_len * RADIX,
            transcendentals=2 * grid_len * RADIX,
        ),
        name="column_forward",
    )(depths, block, wave_x, *tables)


def column_inverse_kernel(
    grid_len, tile_rows, start, count, special, added, keys, flag_ref, kx_ref, kxo_ref, *refs
):
    moves = [refs[0:1]]
    at = 1
    for group in keys:
        moves.append(refs[at : at + len(group)])
        at += len(group)
    refs, (held, arrived) = refs[at:-2], refs[-2:]
    for slot, (group, sources) in enumerate(zip(((),) + keys, moves)):
        for position, source in enumerate(sources):
            fetch = pltpu.make_async_copy(source, held.at[slot], arrived.at[slot])
            if slot == 0:
                fetch.start()
            elif position == 0:
                others = [flag_ref[1] != key for key in group[1:]]
                pl.when(functools.reduce(jnp.logical_and, others, flag_ref[1] >= 0))(fetch.start)
            else:
                pl.when(flag_ref[1] == group[position])(fetch.start)
    bh, bl, ca, sa, cw, sw = refs[:6]
    edge_ref = refs[6] if special else None
    sum_ref = refs[6 + special] if added else None
    out_ref, v_ref, c_ref, s_ref = refs[6 + special + added :]
    here = bh.shape[0] // 8
    c_ref[...] = ca[...]
    s_ref[...] = sa[...]

    def first(step, carry):
        cosine, sine = c_ref[...], s_ref[...]
        table = split(jnp.concatenate([cosine, sine], axis=1))
        c_ref[...] = cosine * cw[...] - sine * sw[...]
        s_ref[...] = sine * cw[...] + cosine * sw[...]
        full_y, odd_y = wave_y(start + step, (RADIX, RADIX), grid_len)
        full_x, odd_x = kx_ref[...], kxo_ref[...]
        squared = full_x * full_x + full_y * full_y
        safe = jnp.where(squared > 0.0, squared, 1.0)
        root = lax.rsqrt(safe)
        inverse = root * root
        rows = pl.ds(pl.multiple_of(step * RADIX, RADIX), RADIX)
        value = held[0, rows, :] + held[1, rows, :] + held[2, rows, :]
        turned = rotate(value)
        coef_xx = -full_x * full_x * inverse
        coef_xy = -odd_x * odd_y * inverse
        coef_yy = -full_y * full_y * inverse
        slope_x = odd_x * root
        slope_y = odd_y * root
        upper = [
            value * coef_xx,
            value * coef_xy,
            turned * slope_x,
            value * coef_yy,
            turned * slope_y,
        ]
        lower = [
            turned * coef_xx,
            turned * coef_xy,
            -value * slope_x,
            turned * coef_yy,
            -value * slope_y,
        ]
        data = jnp.concatenate(
            [jnp.concatenate(upper, axis=1), jnp.concatenate(lower, axis=1)], axis=0
        )
        v_ref[rows, :] = dot3(table, split(data))
        return carry

    for slot, sources in enumerate(moves):
        pltpu.make_async_copy(sources[0], held.at[slot], arrived.at[slot]).wait()
    lax.fori_loop(0, count, first, 0)
    both = jnp.concatenate([bh[...], bl[...]], axis=0)
    span = 8 * here

    def second(group, carry):
        data = jnp.concatenate(
            [v_ref[pl.ds(k1 * RADIX + group * 8, 8), :] for k1 in range(count)], axis=0
        )
        turned = jnp.concatenate(
            [rotate(data[:, RADIX * c : RADIX * (c + 1)]) for c in range(FIELDS)], axis=1
        )
        high, low = split(jnp.concatenate([data, turned], axis=0))
        stacked = mm(both, high)
        result = stacked[:span] + stacked[span:] + mm(bh[...], low)
        per_row = RADIX // tile_rows
        row = (group * 8) % tile_rows
        for a in range(here):
            dest = a * per_row + (group * 8) // tile_rows
            for c in range(FIELDS):
                piece = result[8 * a : 8 * a + 8, RADIX * c : RADIX * (c + 1)]
                if added:
                    piece = piece + sum_ref[dest, c, pl.ds(row, 8), :]
                if special:
                    lane = lax.broadcasted_iota(jnp.int32, piece.shape, 1)
                    edge = edge_ref[c, pl.ds(a * RADIX + group * 8, 8), :]
                    edge = jnp.where(lane < HALF, edge[:, 0:1], edge[:, 1:2])
                    piece = jnp.where((lane % HALF == 0) & (flag_ref[0] == 0), edge, piece)
                out_ref[dest, c, pl.ds(row, 8), :] = piece
        return carry

    lax.fori_loop(0, RADIX // 8, second, 0)


def column_inverse(part, start, wave_x, odd_x, place, edge, partial_sum, sizes):
    grid_len, wide_count, tile_rows = sizes
    flag, row_start, row_share = place
    piece, below, above = part
    count = piece.shape[0] // RADIX
    moved = [piece, *below.values(), *above.values()]
    outer_len = grid_len // RADIX
    alpha = angles(np.arange(RADIX), np.arange(RADIX), RADIX)
    beta = 2.0 * math.pi * np.arange(RADIX)[:, None] / grid_len * np.ones((1, RADIX))
    alpha = alpha + start * beta
    kron = column_kron(outer_len, 1.0)
    chosen = np.arange(start * 8, (start + count) * 8)
    kron = kron[:, np.concatenate([chosen, chosen + 8 * outer_len])]
    share = [
        lax.dynamic_slice_in_dim(item, row_start * 8, row_share * 8, 0) for item in np_split(kron)
    ]
    tables = [
        *share,
        f32(np.cos(alpha)),
        f32(np.sin(alpha)),
        f32(np.cos(beta)),
        f32(np.sin(beta)),
    ]
    extra = [item for item in (edge, partial_sum) if item is not None]
    operands = [*tables, *extra]
    plain = [pl.BlockSpec(memory_space=pltpu.VMEM)]
    square = (RADIX, RADIX)
    out_shape = (wide_count, FIELDS, tile_rows, RADIX)
    return pl.pallas_call(
        functools.partial(
            column_inverse_kernel,
            grid_len,
            tile_rows,
            start,
            count,
            int(edge is not None),
            int(partial_sum is not None),
            (tuple(below), tuple(above)),
        ),
        in_specs=[pl.BlockSpec(memory_space=pltpu.SMEM)]
        + plain * 2
        + [pl.BlockSpec(memory_space=pl.ANY)] * len(moved)
        + plain * len(operands),
        out_specs=pl.BlockSpec(memory_space=pltpu.VMEM),
        out_shape=jax.ShapeDtypeStruct(out_shape, jnp.float32),
        scratch_shapes=[
            pltpu.VMEM((count * RADIX, FIELDS * RADIX), jnp.float32),
            pltpu.VMEM(square, jnp.float32),
            pltpu.VMEM(square, jnp.float32),
            pltpu.VMEM((3, count * RADIX, RADIX), jnp.float32),
            pltpu.SemaphoreType.DMA((3,)),
        ],
        compiler_params=pltpu.CompilerParams(vmem_limit_bytes=VMEM_LIMIT),
        cost_estimate=pl.CostEstimate(
            flops=FIELDS * 45 * count * RADIX * RADIX * 256,
            bytes_accessed=4 * (count * RADIX * RADIX + math.prod(out_shape)),
            transcendentals=count * RADIX * RADIX,
        ),
        name="column_inverse",
    )(flag, wave_x, odd_x, *moved, *operands)


def row_inverse_kernel(chunks, *refs):
    ins = refs[:chunks]
    kh, kl, base, zero, cw, sw, out_ref, th, tl, rot, u_ref = refs[chunks:]
    rows = ins[0].shape[2]
    outer_len = out_ref.shape[2] // RADIX

    @pl.when(pl.program_id(0) == 0)
    def _():
        th[0], tl[0] = split(zero[...])
        rot[...] = base[...]
        for slot in range(1, SLOTS):
            left, right = rot[:, 0:RADIX], rot[:, RADIX:]
            rot[:, 0:RADIX] = cw[...] * left - sw[...] * right
            rot[:, RADIX:] = cw[...] * right + sw[...] * left
            th[slot], tl[slot] = split(rot[...])

    for slot in range(SLOTS):
        parts = []
        for side in range(2):
            block = 2 * slot + side
            item = ins[block % chunks][block // chunks]
            parts.append(item.reshape(FIELDS * rows, RADIX))
        u_ref[slot] = dot3(split(jnp.concatenate(parts, axis=1)), (th[slot], tl[slot]))

    table = (kh[...], kl[...])
    for c in range(FIELDS):

        def second(pair, carry):
            halves = []
            for side in range(2):
                at = pl.ds(c * rows + pair * 16 + 8 * side, 8)
                halves.append(
                    jnp.concatenate(
                        [
                            u_ref[slot, at, RADIX * part : RADIX * (part + 1)]
                            for slot in range(SLOTS)
                            for part in range(2)
                        ],
                        axis=0,
                    )
                )
            result = dot3(table, split(jnp.concatenate(halves, axis=1)))
            for a in range(outer_len):
                for side in range(2):
                    out_ref[
                        c, pl.ds(pair * 16 + 8 * side, 8), RADIX * a : RADIX * (a + 1)
                    ] = result[8 * a : 8 * a + 8, RADIX * side : RADIX * (side + 1)]
            return carry

        lax.fori_loop(0, rows // 16, second, 0)
    out_ref[FIELDS] = -(out_ref[0] + out_ref[3])


def row_inverse(blocks, grid_len):
    chunks = len(blocks)
    wide_count, _, rows, _ = blocks[0].shape
    step = min(rows, 32)
    kron, base, zero, cw, sw = row_inverse_tables(grid_len)
    tables = (*np_split(kron), f32(base), f32(zero), f32(cw), f32(sw))
    return pl.pallas_call(
        functools.partial(row_inverse_kernel, chunks),
        grid=(rows // step,),
        in_specs=[pl.BlockSpec((wide_count, FIELDS, step, RADIX), lambda i: (0, 0, i, 0))] * chunks
        + [full_spec(item.shape) for item in tables],
        out_specs=pl.BlockSpec((FIELDS + 1, step, grid_len), lambda i: (0, i, 0)),
        out_shape=jax.ShapeDtypeStruct((FIELDS + 1, rows, grid_len), jnp.float32),
        scratch_shapes=[
            pltpu.VMEM((SLOTS, 256, 256), jnp.bfloat16),
            pltpu.VMEM((SLOTS, 256, 256), jnp.bfloat16),
            pltpu.VMEM((256, 256), jnp.float32),
            pltpu.VMEM((SLOTS, FIELDS * step, 256), jnp.float32),
        ],
        compiler_params=pltpu.CompilerParams(vmem_limit_bytes=VMEM_LIMIT),
        cost_estimate=pl.CostEstimate(
            flops=12 * FIELDS * rows * grid_len * 256,
            bytes_accessed=44 * rows * grid_len,
            transcendentals=0,
        ),
        name="row_inverse",
    )(*blocks, *tables)


def interpolate_kernel(g_ref, halo_ref, wy_ref, col_ref, wx_ref, place_ref, out_ref, mask_ref):
    samples, grid_len = mask_ref.shape
    wide = 512

    @pl.when(pl.program_id(0) == 0)
    def _():
        for start in range(0, grid_len, wide):
            lane = start + lax.broadcasted_iota(jnp.int32, (samples, wide), 1)
            total = jnp.zeros((samples, wide), jnp.float32)
            for tap in range(4):
                total = total + jnp.where(
                    lane == col_ref[:, tap : tap + 1], wx_ref[:, tap : tap + 1], 0.0
                )
            mask_ref[:, start : start + wide] = total

    left = split(wy_ref[...])
    partial = jnp.zeros((samples, RADIX), jnp.float32)
    for start in range(0, grid_len, wide):
        at = slice(start, start + wide)
        data = jnp.concatenate([g_ref[0, :, at], halo_ref[0, :, at]], axis=0)
        product = dot3(left, split(data)) * mask_ref[:, at]
        for lane in range(0, wide, RADIX):
            partial = partial + product[:, lane : lane + RADIX]
    value = jnp.sum(partial, axis=1, keepdims=True)
    out_ref[0] = jnp.sum(value * place_ref[...], axis=0, keepdims=True)


def interpolate(gradient, halo, weight_y, col_ids, weight_x, placement):
    _, rows, grid_len = gradient.shape
    samples, slot_total = placement.shape
    small = (weight_y, col_ids, weight_x, placement)
    return pl.pallas_call(
        interpolate_kernel,
        grid=(FIELDS,),
        in_specs=[
            pl.BlockSpec((1, rows, grid_len), lambda i: (i, 0, 0)),
            pl.BlockSpec((1, 8, grid_len), lambda i: (i, 0, 0)),
        ]
        + [full_spec(item.shape) for item in small],
        out_specs=pl.BlockSpec((1, 1, slot_total), lambda i: (i, 0, 0)),
        out_shape=jax.ShapeDtypeStruct((FIELDS, 1, slot_total), jnp.float32),
        scratch_shapes=[pltpu.VMEM((samples, grid_len), jnp.float32)],
        compiler_params=pltpu.CompilerParams(vmem_limit_bytes=VMEM_LIMIT),
        name="interpolate",
    )(gradient, halo, *small)


def product(formula, operand_a, operand_b):
    return jnp.einsum(formula, operand_a, operand_b, precision=HIGH)


def complex_product(formula, pair, table):
    return (
        product(formula, pair[0], table[0]) - product(formula, pair[1], table[1]),
        product(formula, pair[0], table[1]) + product(formula, pair[1], table[0]),
    )


def phase(row_count, col_count, period, orient):
    theta = angles(np.arange(row_count), np.arange(col_count), period)
    return f32(np.cos(theta)), f32(orient * np.sin(theta))


def times_table(pair, table):
    return (
        pair[0] * table[0] - pair[1] * table[1],
        pair[0] * table[1] + pair[1] * table[0],
    )


def edge_waves(grid_len):
    outer_len = grid_len // RADIX
    index = np.arange(outer_len)[:, None] + outer_len * np.arange(RADIX)[None, :]
    signed = np.where(index < grid_len // 2, index, index - grid_len).astype(np.float32)
    full_y = signed * np.float32(2.0 * math.pi / grid_len)
    odd_y = np.where(index == grid_len // 2, np.float32(0.0), full_y)
    return full_y, odd_y


def edge_forward(values, layer_top, layer_thick):
    grid_len = values.shape[1]
    outer_len = grid_len // RADIX
    columns = values.reshape(2, outer_len, RADIX)
    first = phase(outer_len, outer_len, outer_len, -1.0)
    pair = (product("zab,ka->zkb", columns, first[0]), product("zab,ka->zkb", columns, first[1]))
    pair = times_table(pair, phase(outer_len, RADIX, grid_len, -1.0))
    pair = complex_product("zkb,bc->zkc", pair, phase(RADIX, RADIX, RADIX, -1.0))
    full_y, _ = edge_waves(grid_len)
    magnitude = jnp.sqrt(
        jnp.asarray(np.stack([full_y * full_y, full_y * full_y + np.float32(math.pi) ** 2]))
    )
    scale = (
        2.0
        * math.pi
        / (grid_len * grid_len)
        * (1.0 - jnp.exp(-magnitude * layer_thick))
        * jnp.exp(-magnitude * layer_top)
    )
    return jnp.stack([pair[0] * scale, pair[1] * scale])


def edge_inverse(total, row_start, row_share):
    outer_len = total.shape[2]
    grid_len = outer_len * RADIX
    full_y, odd_y = edge_waves(grid_len)
    full_x = np.array([0.0, math.pi], np.float32)[:, None, None]
    squared = full_x * full_x + full_y * full_y
    safe = np.where(squared > 0.0, squared, np.float32(1.0))
    none = np.zeros_like(safe)
    plain = f32(np.stack([-full_x * full_x / safe, none, none, -full_y * full_y / safe, none]))
    turned = f32(np.stack([none, none, none, none, odd_y / np.sqrt(safe)]))
    pair = (total[0] * plain - total[1] * turned, total[1] * plain + total[0] * turned)
    pair = complex_product("fzkc,cb->fzkb", pair, phase(RADIX, RADIX, RADIX, 1.0))
    pair = times_table(pair, phase(outer_len, RADIX, grid_len, 1.0))
    last = phase(outer_len, outer_len, outer_len, 1.0)
    last = [lax.dynamic_slice_in_dim(item, row_start, row_share, 0) for item in last]
    real = product("fzkb,ak->fzab", pair[0], last[0]) - product("fzkb,ak->fzab", pair[1], last[1])
    return jnp.moveaxis(real.reshape(FIELDS, 2, row_share * RADIX), 1, 2)


def cubic_kernel(distance):
    near_part = (1.5 * distance - 2.5) * distance * distance + 1.0
    far_part = ((-0.5 * distance + 2.5) * distance - 4.0) * distance + 2.0
    return jnp.where(distance <= 1.0, near_part, jnp.where(distance < 2.0, far_part, 0.0))


def tap_weights(level):
    offset = (level.astype(jnp.float32) + 0.5) / QLEV - 0.5
    base = jnp.where(level < QLEV // 2, -1, 0).astype(jnp.int32)
    fraction = offset - base.astype(jnp.float32)
    taps = jnp.arange(4, dtype=jnp.int32)[None, :]
    weights = cubic_kernel(jnp.abs(fraction[:, None] - (taps.astype(jnp.float32) - 1.0)))
    return weights, base[:, None] - 1 + taps


def choose(which, candidates):
    picked = None
    for key, value in candidates.items():
        picked = value if picked is None else jnp.where(which == key, value, picked)
    return picked


def depth_scan(pieces, jobs, total, aside):
    count = lax.axis_size("depth")
    here = lax.axis_index("depth")
    up = [(i, i + 1) for i in range(count - 1)]
    down = [(i + 1, i) for i in range(count - 1)]
    from_below, from_above = [], []

    def complete(index):
        below = {d: from_below[index + d - 1] for d in range(1, count)}
        above = {count - 1 - d: from_above[index + d - 1] for d in range(1, count)}
        return pieces[index], below, above

    for step in range(total + count - 2):
        live = [d for d in range(count - 1) if 0 <= step - d < total]
        rising = choose(here, {d: pieces[step - d] for d in live})
        falling = choose(here, {count - 1 - d: pieces[step - d] for d in live})
        if step:
            rising, falling = rising + from_below[-1], falling + from_above[-1]
        work = [jobs[step]] if step in jobs else []
        if step == aside[0]:
            work.append(aside[1:])
        keys = [key for _, key in work]
        rising, falling, keys = lax.optimization_barrier((rising, falling, keys))
        below = lax.ppermute(rising, "depth", up)
        above = lax.ppermute(falling, "depth", down)
        results = [task(key, complete) for (task, _), key in zip(work, keys)]
        below, above, _ = lax.optimization_barrier((below, above, results))
        from_below.append(below)
        from_above.append(above)
    return complete


def per_device(density, layer_top, layer_thick, sample_row, sample_col, sample_frac, sample_owner):
    wide_count = lax.axis_size("wide")
    depth_count = lax.axis_size("depth")
    rows_here, grid_len = density.shape[1], density.shape[2]
    outer_len = grid_len // RADIX
    tile_rows = rows_here // depth_count
    chunks = 2 * SLOTS // wide_count
    wide_id, depth_id = lax.axis_index("wide"), lax.axis_index("depth")

    def exchange(block):
        return lax.all_to_all(block, "wide", split_axis=0, concat_axis=0, tiled=True)

    spectra = [exchange(item) for item in row_forward(density[0], wide_count)]
    columns = [item.reshape(grid_len, RADIX) for item in spectra]

    lane = jnp.arange(RADIX, dtype=jnp.int32)[None, :] % HALF
    waves = []
    for chunk in range(chunks):
        block = wide_id * chunks + chunk
        slot = block // 2
        place = (block % 2) * HALF + lane
        low = jnp.where(
            place < HALF, outer_len * place, outer_len // 2 + outer_len * (place - HALF)
        )
        index = jnp.where(slot == 0, low, slot + outer_len * place)
        signed = jnp.where(index < grid_len // 2, index, index - grid_len).astype(jnp.float32)
        waves.append(signed * (2.0 * math.pi / grid_len))

    depths = jnp.concatenate([layer_top, layer_thick])
    edge = edge_forward(
        jnp.stack([columns[0][:, 0], columns[0][:, HALF]]), layer_top[0], layer_thick[0]
    )
    edge = lax.psum(edge, "depth")
    row_share = outer_len // depth_count
    row_start = depth_id * row_share
    place = (jnp.stack([wide_id, depth_id]).astype(jnp.int32), row_start, row_share)
    sizes = (grid_len, wide_count, tile_rows)
    pieces, blocks, partial_sums, edges = [], {}, {}, []

    def forward_job(chunk, wave, complete):
        pieces.extend(column_forward(columns[chunk], wave, depths))
        return pieces[-1]

    def edge_job(key, complete):
        edges.append(edge_inverse(key, row_start, row_share))
        return edges[0]

    def early_job(chunk, wave, complete):
        item = column_inverse(complete(2 * chunk), 0, wave, wave, place, None, None, sizes)
        partial_sums[chunk] = item
        return item

    def late_job(chunk, wave, complete):
        part = complete(2 * chunk + 1)
        special = edges[0] if chunk == 0 else None
        item = column_inverse(
            part, outer_len // 2, wave, wave, place, special, partial_sums[chunk], sizes
        )
        blocks[chunk] = exchange(item)
        return item

    forward_job(0, waves[0], None)
    jobs = {}
    last = chunks - 1
    for chunk in range(chunks):
        if chunk:
            jobs[chunk - 1] = (functools.partial(forward_job, chunk), waves[chunk])
        jobs[2 * chunk + depth_count - 1] = (functools.partial(early_job, chunk), waves[chunk])
        if chunk < last:
            jobs[2 * chunk + depth_count] = (functools.partial(late_job, chunk), waves[chunk])
    complete = depth_scan(pieces, jobs, 2 * chunks, (EDGE_STEP, edge_job, edge))
    late_job(last, waves[last], complete)
    blocks = [blocks[chunk] for chunk in range(chunks)]
    gradient = row_inverse(blocks, grid_len)

    tiles = depth_count * wide_count
    forward = [(i, (i + 1) % tiles) for i in range(tiles)]
    backward = [(target, source) for source, target in forward]
    low = lax.ppermute(gradient[:FIELDS, tile_rows - 2 :], ("depth", "wide"), forward)
    high = lax.ppermute(gradient[:FIELDS, :2], ("depth", "wide"), backward)
    halo = jnp.concatenate([low, high, jnp.zeros((FIELDS, 4, grid_len), jnp.float32)], axis=1)

    taps_y, offset_y = tap_weights(sample_frac[0, 0])
    taps_x, offset_x = tap_weights(sample_frac[0, 1])
    row_ids = sample_row[0][:, None] + offset_y
    col_ids = (sample_col[0][:, None] + offset_x) % grid_len
    row_ids = jnp.where(
        row_ids < 0,
        row_ids + tile_rows + 2,
        jnp.where(row_ids >= tile_rows, row_ids + 2, row_ids),
    )
    row_marks = row_ids[:, :, None] == jnp.arange(tile_rows + 8, dtype=jnp.int32)
    weight_y = jnp.sum(jnp.where(row_marks, taps_y[:, :, None], 0.0), axis=1)
    sample_count = sample_row.shape[1]
    capacity = max(2 * sample_count // wide_count, 2)
    slot_total = wide_count * capacity
    owner_ids = sample_owner[0, :, 0]
    same = owner_ids[:, None] == owner_ids[None, :]
    order = jnp.arange(sample_count, dtype=jnp.int32)
    slot_ids = jnp.sum((same & (order[None, :] < order[:, None])).astype(jnp.int32), axis=1)
    target = owner_ids * capacity + slot_ids
    placement = (target[:, None] == jnp.arange(slot_total, dtype=jnp.int32)[None, :]).astype(
        jnp.float32
    )
    outgoing = interpolate(gradient, halo, weight_y, col_ids, taps_x, placement)
    outgoing = outgoing.reshape(FIELDS, wide_count, capacity)
    arrived = lax.all_to_all(outgoing, "wide", split_axis=1, concat_axis=1, tiled=True)
    arrived = arrived.reshape(FIELDS, 1, slot_total)
    return (gradient, jnp.concatenate([arrived, -(arrived[0:1] + arrived[3:4])]))


def solution(mesh):
    in_specs = (
        P("depth", "wide", None),
        P("depth"),
        P("depth"),
        P(("depth", "wide"), None),
        P(("depth", "wide"), None),
        P(("depth", "wide"), None, None),
        P(("depth", "wide"), None, None),
    )
    out_specs = (P(None, ("depth", "wide"), None), P(None, ("depth", "wide"), None))
    return jax.shard_map(
        per_device, mesh=mesh, in_specs=in_specs, out_specs=out_specs, check_vma=False
    )
```

```python
import functools
import math

import jax
import jax.numpy as jnp
import ml_dtypes
import numpy as np
from jax import lax
from jax.experimental import pallas as pl
from jax.experimental.pallas import tpu as pltpu
from jax.sharding import PartitionSpec as P

RADIX = 128
QLEV = 16
HALF = 64
SLOTS = 16
FIELDS = 5
GROUPS = ((0, 1, 2, 3, 4),)
EVERY = tuple(range(FIELDS))
EDGE_STEP = 2
HIGH = lax.Precision.HIGHEST
VMEM_LIMIT = 56 * 1024 * 1024


def np_split(table):
    high = table.astype(np.float32).astype(ml_dtypes.bfloat16)
    low = (table - high.astype(np.float64)).astype(ml_dtypes.bfloat16)
    return jnp.asarray(high), jnp.asarray(low)


def f32(table):
    return jnp.asarray(np.asarray(table, np.float32))


def angles(left, right, period):
    return (np.outer(left, right) % period) * (2.0 * math.pi / period)


def lane_order():
    column = np.arange(256)
    wave = (column // 128) * HALF + column % HALF
    return wave, (column % 128) // HALF


def slot_zero_angles(grid_len):
    wave, part = lane_order()
    outer_len = grid_len // RADIX
    upper = wave >= HALF
    freq = np.where(upper, outer_len // 2 + outer_len * (wave - HALF), outer_len * wave)
    return wave, part, upper, angles(np.arange(RADIX), freq, grid_len)


def row_forward_tables(grid_len, slots):
    outer_len = grid_len // RADIX
    stride = slots[1] - slots[0]
    theta = angles(np.asarray(slots), np.arange(outer_len), outer_len)
    first = np.zeros((2 * len(slots), outer_len))
    first[0::2] = np.cos(theta)
    first[1::2] = -np.sin(theta)
    if slots[0] == 0:
        first[1] = np.cos(np.pi * np.arange(outer_len))
    kron = np.kron(first, np.eye(8))
    wave, part = lane_order()
    step = 2.0 * math.pi * np.arange(RADIX)[:, None] / grid_len * np.ones((1, 256))
    alpha = angles(np.arange(RADIX), wave, RADIX) + slots[0] * step
    base = np.concatenate(
        [
            np.where(part == 0, np.cos(alpha), -np.sin(alpha)),
            np.where(part == 0, np.sin(alpha), np.cos(alpha)),
        ]
    )
    wave, part, upper, alpha = slot_zero_angles(grid_len)
    table = np.where(part == 0, np.cos(alpha), -np.sin(alpha))
    top = np.where(upper, 0.0, table)
    top[:, (wave == 0) & (part == 1)] = np.cos(np.pi * np.arange(RADIX))[:, None]
    zero = np.concatenate([top, np.where(upper, table, 0.0)])
    return kron, base, zero if slots[0] == 0 else base, np.cos(stride * step), np.sin(stride * step)


def row_inverse_tables(grid_len):
    outer_len = grid_len // RADIX
    theta = angles(np.arange(outer_len), np.arange(SLOTS), outer_len)
    last = np.zeros((outer_len, 2 * SLOTS))
    last[:, 0::2] = np.cos(theta)
    last[:, 1::2] = -np.sin(theta)
    last[:, 1] = np.cos(np.pi * np.arange(outer_len))
    kron = np.kron(last, np.eye(8))
    wave, part = lane_order()
    alpha = angles(wave, np.arange(RADIX), RADIX)
    real_row = (part == 0)[:, None]
    base = 2.0 * np.concatenate(
        [
            np.where(real_row, np.cos(alpha), -np.sin(alpha)),
            np.where(real_row, np.sin(alpha), np.cos(alpha)),
        ],
        axis=1,
    )
    wave, part, upper, alpha = slot_zero_angles(grid_len)
    table = 2.0 * np.where(part == 0, np.cos(alpha), -np.sin(alpha))
    left = np.where(upper, 0.0, table)
    left[:, (wave == 0) & (part == 0)] = 1.0
    left[:, (wave == 0) & (part == 1)] = np.cos(np.pi * np.arange(RADIX))[:, None]
    zero = np.concatenate([left.T, np.where(upper, table, 0.0).T], axis=1)
    beta = 2.0 * math.pi * np.arange(RADIX)[None, :] / grid_len
    return kron, base, zero, np.cos(beta), np.sin(beta)


def column_kron(outer_len, orient):
    theta = angles(np.arange(outer_len), np.arange(outer_len), outer_len)
    return np.concatenate(
        [np.kron(np.cos(theta), np.eye(8)), np.kron(orient * np.sin(theta), np.eye(8))], axis=1
    )


def split(value):
    high = value.astype(jnp.bfloat16)
    return high, (value - high.astype(jnp.float32)).astype(jnp.bfloat16)


def mm(left, right):
    return jnp.dot(left, right, preferred_element_type=jnp.float32)


def dot3(left, right):
    rows = left[0].shape[0]
    both = mm(jnp.concatenate(left, axis=0), right[0])
    return both[:rows] + both[rows:] + mm(left[0], right[1])


def rotate(value):
    lane = lax.broadcasted_iota(jnp.int32, value.shape, 1)
    return jnp.where(lane < HALF, -1.0, 1.0) * pltpu.roll(value, HALF, 1)


def row_forward_kernel(chunks, slots, x_ref, kh, kl, base, zero, cw, sw, *refs):
    outs = refs[:-4]
    th, tl, rot, u_ref = refs[-4:]
    rows = x_ref.shape[0]
    outer_len = x_ref.shape[1] // RADIX

    @pl.when(pl.program_id(0) == 0)
    def _():
        th[0], tl[0] = split(zero[...])
        rot[...] = base[...]
        for slot in range(1, len(slots)):
            top, low = rot[0:RADIX, :], rot[RADIX:, :]
            rot[0:RADIX, :] = cw[...] * top - sw[...] * low
            rot[RADIX:, :] = cw[...] * low + sw[...] * top
            th[slot], tl[slot] = split(rot[...])

    table = (kh[...], kl[...])

    def first(pair, carry):
        halves = [
            jnp.concatenate(
                [
                    x_ref[pl.ds(pair * 16 + 8 * side, 8), RADIX * a : RADIX * (a + 1)]
                    for a in range(outer_len)
                ],
                axis=0,
            )
            for side in range(2)
        ]
        u_ref[pair] = dot3(table, split(jnp.concatenate(halves, axis=1)))
        return carry

    lax.fori_loop(0, rows // 16, first, 0, unroll=min(2, rows // 16))
    for slot in range(len(slots)):
        parts = []
        for part in range(2):
            at = 16 * slot + 8 * part
            parts.append(
                jnp.concatenate(
                    [
                        u_ref[pair, at : at + 8, RADIX * side : RADIX * (side + 1)]
                        for pair in range(rows // 16)
                        for side in range(2)
                    ],
                    axis=0,
                )
            )
        result = dot3(split(jnp.concatenate(parts, axis=1)), (th[slot], tl[slot]))
        for side in range(2):
            block = 2 * slots[slot] + side
            outs[block % chunks % len(outs)][block // chunks] = result[:, RADIX * side : RADIX * (side + 1)]


def full_spec(shape):
    return pl.BlockSpec(shape, lambda *_: (0,) * len(shape))


def row_forward(field, wide_count, slots):
    rows, grid_len = field.shape
    chunks = 2 * SLOTS // wide_count
    made = min(chunks, 2) if len(slots) < SLOTS else chunks
    step = min(rows, 128)
    kron, base, zero, cw, sw = row_forward_tables(grid_len, slots)
    tables = (*np_split(kron), f32(base), f32(zero), f32(cw), f32(sw))
    return pl.pallas_call(
        functools.partial(row_forward_kernel, chunks, slots),
        grid=(rows // step,),
        in_specs=[pl.BlockSpec((step, grid_len), lambda i: (i, 0))]
        + [full_spec(item.shape) for item in tables],
        out_specs=[pl.BlockSpec((wide_count, step, RADIX), lambda i: (0, i, 0))] * made,
        out_shape=[jax.ShapeDtypeStruct((wide_count, rows, RADIX), jnp.float32)] * made,
        scratch_shapes=[
            pltpu.VMEM((len(slots), 256, 256), jnp.bfloat16),
            pltpu.VMEM((len(slots), 256, 256), jnp.bfloat16),
            pltpu.VMEM((256, 256), jnp.float32),
            pltpu.VMEM((step // 16, 16 * len(slots), 256), jnp.float32),
        ],
        compiler_params=pltpu.CompilerParams(vmem_limit_bytes=VMEM_LIMIT),
        cost_estimate=pl.CostEstimate(
            flops=20 * len(slots) // SLOTS * rows * grid_len * 256, bytes_accessed=8 * rows * grid_len, transcendentals=0
        ),
        name="row_forward",
    )(field, *tables)


def wave_y(first, shape, grid_len):
    outer_len = grid_len // RADIX
    index = first + outer_len * lax.broadcasted_iota(jnp.int32, shape, 0)
    signed = jnp.where(index < grid_len // 2, index, index - grid_len).astype(jnp.float32)
    full = signed * (2.0 * math.pi / grid_len)
    return full, jnp.where(index == grid_len // 2, 0.0, full)


def column_forward_kernel(
    grid_len, depth_ref, x_ref, kx_ref, kh, kl, ca, sa, cw, sw, low_ref, high_ref, *scratch
):
    u_ref, c_ref, s_ref = scratch
    outer_len = grid_len // RADIX
    table = (kh[...], kl[...])

    def first(pair, carry):
        halves = [
            jnp.concatenate(
                [x_ref[pl.ds(a * RADIX + pair * 16 + 8 * side, 8), :] for a in range(outer_len)],
                axis=0,
            )
            for side in range(2)
        ]
        turned = [rotate(half) for half in halves]
        data = jnp.concatenate(
            [jnp.concatenate(halves, axis=1), jnp.concatenate(turned, axis=1)], axis=0
        )
        result = dot3(table, split(data))
        for k1 in range(outer_len):
            for side in range(2):
                u_ref[pl.ds(k1 * RADIX + pair * 16 + 8 * side, 8), :] = result[
                    8 * k1 : 8 * k1 + 8, RADIX * side : RADIX * (side + 1)
                ]
        return carry

    lax.fori_loop(0, RADIX // 16, first, 0, unroll=4)
    c_ref[...] = ca[...]
    s_ref[...] = sa[...]
    top, thick = depth_ref[0], depth_ref[1]

    middle = outer_len // 2

    def second(out_ref, start, step, carry):
        k1 = start + step
        cosine, sine = c_ref[...], s_ref[...]
        table = split(jnp.concatenate([cosine, sine], axis=1))
        c_ref[...] = cosine * cw[...] - sine * sw[...]
        s_ref[...] = sine * cw[...] + cosine * sw[...]
        rows = pl.ds(pl.multiple_of(k1 * RADIX, RADIX), RADIX)
        data = u_ref[rows, :]
        result = dot3(table, split(jnp.concatenate([data, rotate(data)], axis=0)))
        full_y, _ = wave_y(k1, (RADIX, RADIX), grid_len)
        magnitude = jnp.sqrt(kx_ref[...] * kx_ref[...] + full_y * full_y)
        scale = (1.0 - jnp.exp(-magnitude * thick)) * jnp.exp(-magnitude * top)
        out_ref[pl.ds(pl.multiple_of(step * RADIX, RADIX), RADIX), :] = result * (
            scale * (2.0 * math.pi / (grid_len * grid_len))
        )
        return carry

    lax.fori_loop(0, middle, functools.partial(second, low_ref, 0), 0, unroll=4)
    lax.fori_loop(0, middle, functools.partial(second, high_ref, middle), 0, unroll=4)


def column_forward(block, wave_x, depths):
    grid_len = block.shape[0]
    outer_len = grid_len // RADIX
    alpha = angles(np.arange(RADIX), np.arange(RADIX), RADIX)
    beta = 2.0 * math.pi * np.arange(RADIX)[None, :] / grid_len
    tables = (
        *np_split(column_kron(outer_len, -1.0)),
        f32(np.cos(alpha)),
        f32(-np.sin(alpha)),
        f32(np.cos(beta)),
        f32(-np.sin(beta)),
    )
    square = (RADIX, RADIX)
    return pl.pallas_call(
        functools.partial(column_forward_kernel, grid_len),
        in_specs=[pl.BlockSpec(memory_space=pltpu.SMEM)]
        + [pl.BlockSpec(memory_space=pltpu.VMEM)] * (2 + len(tables)),
        out_specs=[pl.BlockSpec(memory_space=pltpu.VMEM)] * 2,
        out_shape=[jax.ShapeDtypeStruct((grid_len // 2, RADIX), jnp.float32)] * 2,
        scratch_shapes=[
            pltpu.VMEM((grid_len, RADIX), jnp.float32),
            pltpu.VMEM(square, jnp.float32),
            pltpu.VMEM(square, jnp.float32),
        ],
        compiler_params=pltpu.CompilerParams(vmem_limit_bytes=VMEM_LIMIT),
        cost_estimate=pl.CostEstimate(
            flops=100 * grid_len * RADIX * 256,
            bytes_accessed=8 * grid_len * RADIX,
            transcendentals=2 * grid_len * RADIX,
        ),
        name="column_forward",
    )(depths, block, wave_x, *tables)


def column_inverse_kernel(
    grid_len, tile_rows, start, count, special, added, keys, fields, flag_ref, kx_ref, kxo_ref, *refs
):
    keys = tuple(group for group in keys if group)
    moves = [refs[0:1]]
    at = 1
    for group in keys:
        moves.append(refs[at : at + len(group)])
        at += len(group)
    refs, (held, arrived) = refs[at:-2], refs[-2:]
    for slot, (group, sources) in enumerate(zip(((),) + keys, moves)):
        for position, source in enumerate(sources):
            fetch = pltpu.make_async_copy(source, held.at[slot], arrived.at[slot])
            if slot == 0:
                fetch.start()
            elif position == 0:
                others = [flag_ref[1] != key for key in group[1:]]
                pl.when(functools.reduce(jnp.logical_and, others, flag_ref[1] >= 0))(fetch.start)
            else:
                pl.when(flag_ref[1] == group[position])(fetch.start)
    bh, bl, ca, sa, cw, sw = refs[:6]
    edge_ref = refs[6] if special else None
    sum_ref = refs[6 + special] if added else None
    out_ref, v_ref, c_ref, s_ref = refs[6 + special + added :]
    here = bh.shape[0] // 8
    c_ref[...] = ca[...]
    s_ref[...] = sa[...]

    def first(step, carry):
        cosine, sine = c_ref[...], s_ref[...]
        table = split(jnp.concatenate([cosine, sine], axis=1))
        c_ref[...] = cosine * cw[...] - sine * sw[...]
        s_ref[...] = sine * cw[...] + cosine * sw[...]
        full_y, odd_y = wave_y(start + step, (RADIX, RADIX), grid_len)
        full_x, odd_x = kx_ref[...], kxo_ref[...]
        squared = full_x * full_x + full_y * full_y
        safe = jnp.where(squared > 0.0, squared, 1.0)
        root = lax.rsqrt(safe)
        inverse = root * root
        rows = pl.ds(pl.multiple_of(step * RADIX, RADIX), RADIX)
        value = held[0, rows, :]
        for slot in range(1, held.shape[0]):
            value = value + held[slot, rows, :]
        turned = rotate(value)
        coef_xx = -full_x * full_x * inverse
        coef_xy = -odd_x * odd_y * inverse
        coef_yy = -full_y * full_y * inverse
        slope_x = odd_x * root
        slope_y = odd_y * root
        upper = [
            value * coef_xx,
            value * coef_xy,
            turned * slope_x,
            value * coef_yy,
            turned * slope_y,
        ]
        lower = [
            turned * coef_xx,
            turned * coef_xy,
            -value * slope_x,
            turned * coef_yy,
            -value * slope_y,
        ]
        upper = jnp.concatenate([upper[c] for c in fields], axis=1)
        lower = jnp.concatenate([lower[c] for c in fields], axis=1)
        data = jnp.concatenate([upper, lower], axis=0)
        v_ref[rows, :] = dot3(table, split(data))
        return carry

    for slot, sources in enumerate(moves):
        pltpu.make_async_copy(sources[0], held.at[slot], arrived.at[slot]).wait()
    lax.fori_loop(0, count, first, 0, unroll=8)
    both = jnp.concatenate([bh[...], bl[...]], axis=0)
    span = 8 * here

    def second(group, carry):
        data = jnp.concatenate(
            [v_ref[pl.ds(k1 * RADIX + group * 8, 8), :] for k1 in range(count)], axis=0
        )
        turned = jnp.concatenate(
            [rotate(data[:, RADIX * c : RADIX * (c + 1)]) for c in range(len(fields))], axis=1
        )
        high, low = split(jnp.concatenate([data, turned], axis=0))
        stacked = mm(both, high)
        result = stacked[:span] + stacked[span:] + mm(bh[...], low)
        per_row = RADIX // tile_rows
        row = (group * 8) % tile_rows
        for a in range(here):
            dest = a * per_row + (group * 8) // tile_rows
            for spot, c in enumerate(fields):
                piece = result[8 * a : 8 * a + 8, RADIX * spot : RADIX * (spot + 1)]
                if added:
                    piece = piece + sum_ref[dest, c, pl.ds(row, 8), :]
                if special:
                    lane = lax.broadcasted_iota(jnp.int32, piece.shape, 1)
                    edge = edge_ref[c, pl.ds(a * RADIX + group * 8, 8), :]
                    edge = jnp.where(lane < HALF, edge[:, 0:1], edge[:, 1:2])
                    piece = jnp.where((lane % HALF == 0) & (flag_ref[0] == 0), edge, piece)
                out_ref[dest, spot, pl.ds(row, 8), :] = piece
        return carry

    lax.fori_loop(0, RADIX // 8, second, 0, unroll=8)


def column_inverse(part, start, wave_x, odd_x, place, edge, partial_sum, sizes, fields):
    grid_len, wide_count, tile_rows = sizes
    flag, row_start, row_share = place
    piece, below, above = part
    count = piece.shape[0] // RADIX
    moved = [piece, *below.values(), *above.values()]
    outer_len = grid_len // RADIX
    alpha = angles(np.arange(RADIX), np.arange(RADIX), RADIX)
    beta = 2.0 * math.pi * np.arange(RADIX)[:, None] / grid_len * np.ones((1, RADIX))
    alpha = alpha + start * beta
    kron = column_kron(outer_len, 1.0)
    chosen = np.arange(start * 8, (start + count) * 8)
    kron = kron[:, np.concatenate([chosen, chosen + 8 * outer_len])]
    share = [
        lax.dynamic_slice_in_dim(item, row_start * 8, row_share * 8, 0) for item in np_split(kron)
    ]
    tables = [
        *share,
        f32(np.cos(alpha)),
        f32(np.sin(alpha)),
        f32(np.cos(beta)),
        f32(np.sin(beta)),
    ]
    extra = [item for item in (edge, partial_sum) if item is not None]
    operands = [*tables, *extra]
    plain = [pl.BlockSpec(memory_space=pltpu.VMEM)]
    square = (RADIX, RADIX)
    out_shape = (wide_count, len(fields), tile_rows, RADIX)
    return pl.pallas_call(
        functools.partial(
            column_inverse_kernel,
            grid_len,
            tile_rows,
            start,
            count,
            int(edge is not None),
            int(partial_sum is not None),
            (tuple(below), tuple(above)),
            fields,
        ),
        in_specs=[pl.BlockSpec(memory_space=pltpu.SMEM)]
        + plain * 2
        + [pl.BlockSpec(memory_space=pl.ANY)] * len(moved)
        + plain * len(operands),
        out_specs=pl.BlockSpec(memory_space=pltpu.VMEM),
        out_shape=jax.ShapeDtypeStruct(out_shape, jnp.float32),
        scratch_shapes=[
            pltpu.VMEM((count * RADIX, len(fields) * RADIX), jnp.float32),
            pltpu.VMEM(square, jnp.float32),
            pltpu.VMEM(square, jnp.float32),
            pltpu.VMEM((3 if below else 1, count * RADIX, RADIX), jnp.float32),
            pltpu.SemaphoreType.DMA((3 if below else 1,)),
        ],
        compiler_params=pltpu.CompilerParams(vmem_limit_bytes=VMEM_LIMIT),
        cost_estimate=pl.CostEstimate(
            flops=len(fields) * 45 * count * RADIX * RADIX * 256,
            bytes_accessed=4 * (count * RADIX * RADIX + math.prod(out_shape)),
            transcendentals=count * RADIX * RADIX,
        ),
        name="column_inverse",
    )(flag, wave_x, odd_x, *moved, *operands)


def row_inverse_kernel(chunks, fields, *refs):
    ins, refs = refs[: chunks * fields], refs[chunks * fields :]
    kh, kl, base, zero, cw, sw = refs[:6]
    trace_ref = refs[6] if len(refs) == 14 else None
    out_ref, top_ref, bottom_ref, th, tl, rot, u_ref = refs[-7:]
    rows = ins[0].shape[2]
    outer_len = out_ref.shape[2] // RADIX

    @pl.when(pl.program_id(0) == 0)
    def _():
        th[0], tl[0] = split(zero[...])
        rot[...] = base[...]
        for slot in range(1, SLOTS):
            left, right = rot[:, 0:RADIX], rot[:, RADIX:]
            rot[:, 0:RADIX] = cw[...] * left - sw[...] * right
            rot[:, RADIX:] = cw[...] * right + sw[...] * left
            th[slot], tl[slot] = split(rot[...])

    for slot in range(SLOTS):
        parts = []
        for side in range(2):
            block = 2 * slot + side
            parts.append(
                jnp.concatenate(
                    [ins[c * chunks + block % chunks][block // chunks, 0] for c in range(fields)],
                    axis=0,
                )
            )
        u_ref[slot] = dot3(split(jnp.concatenate(parts, axis=1)), (th[slot], tl[slot]))

    table = (kh[...], kl[...])
    for c in range(fields):

        def second(pair, carry):
            halves = []
            for side in range(2):
                at = pl.ds(c * rows + pair * 16 + 8 * side, 8)
                halves.append(
                    jnp.concatenate(
                        [
                            u_ref[slot, at, RADIX * part : RADIX * (part + 1)]
                            for slot in range(SLOTS)
                            for part in range(2)
                        ],
                        axis=0,
                    )
                )
            result = dot3(table, split(jnp.concatenate(halves, axis=1)))
            for a in range(outer_len):
                for side in range(2):
                    out_ref[
                        c, pl.ds(pair * 16 + 8 * side, 8), RADIX * a : RADIX * (a + 1)
                    ] = result[8 * a : 8 * a + 8, RADIX * side : RADIX * (side + 1)]
            return carry

        lax.fori_loop(0, rows // 16, second, 0, unroll=min(2, rows // 16))
    if trace_ref is not None:
        out_ref[fields] = -(trace_ref[0] + out_ref[0])
    elif fields == FIELDS:
        out_ref[fields] = -(out_ref[0] + out_ref[3])

    @pl.when(pl.program_id(0) == 0)
    def _():
        top_ref[...] = out_ref[:, 0:8, :]

    @pl.when(pl.program_id(0) == pl.num_programs(0) - 1)
    def _():
        bottom_ref[...] = out_ref[:, rows - 8 : rows, :]


def row_inverse(pieces, grid_len, earlier):
    fields, chunks = len(pieces), len(pieces[0])
    wide_count, _, rows, _ = pieces[0][0][0].shape
    step = min(rows, 32 if fields == FIELDS else 64)
    made = FIELDS + 1 if fields == FIELDS else 3
    kron, base, zero, cw, sw = row_inverse_tables(grid_len)
    tables = (*np_split(kron), f32(base), f32(zero), f32(cw), f32(sw))
    specs, operands = [], []
    for per_chunk in pieces:
        for array, index in per_chunk:
            specs.append(
                pl.BlockSpec((wide_count, 1, step, RADIX), lambda i, index=index: (0, index, i, 0))
            )
            operands.append(array)
    specs += [full_spec(item.shape) for item in tables]
    operands += tables
    aliases = {}
    if earlier is not None:
        aliases = {len(operands): 0}
        specs.append(pl.BlockSpec((1, step, grid_len), lambda i: (0, i, 0)))
        operands.append(earlier)
    group = 0 if earlier is None else 1
    edge = jax.ShapeDtypeStruct((made, 8, grid_len), jnp.float32)
    return pl.pallas_call(
        functools.partial(row_inverse_kernel, chunks, fields),
        grid=(rows // step,),
        in_specs=specs,
        out_specs=[pl.BlockSpec((made, step, grid_len), lambda i: (group, i, 0))]
        + [full_spec(edge.shape)] * 2,
        out_shape=[jax.ShapeDtypeStruct((FIELDS + 1, rows, grid_len), jnp.float32), edge, edge],
        scratch_shapes=[
            pltpu.VMEM((SLOTS, 256, 256), jnp.bfloat16),
            pltpu.VMEM((SLOTS, 256, 256), jnp.bfloat16),
            pltpu.VMEM((256, 256), jnp.float32),
            pltpu.VMEM((SLOTS, fields * step, 256), jnp.float32),
        ],
        input_output_aliases=aliases,
        compiler_params=pltpu.CompilerParams(vmem_limit_bytes=VMEM_LIMIT),
        cost_estimate=pl.CostEstimate(
            flops=12 * fields * rows * grid_len * 256,
            bytes_accessed=8 * fields * rows * grid_len,
            transcendentals=0,
        ),
        name="row_inverse",
    )(*operands)


def mask_kernel(col_ref, wx_ref, mask_ref):
    samples, wide = mask_ref.shape
    lane = pl.program_id(0) * wide + lax.broadcasted_iota(jnp.int32, (samples, wide), 1)
    total = jnp.zeros((samples, wide), jnp.float32)
    for tap in range(4):
        here = lane == col_ref[:, tap : tap + 1]
        total = total + jnp.where(here, wx_ref[:, tap : tap + 1], 0.0)
    mask_ref[...] = total


def column_mask(col_ids, weight_x, grid_len):
    samples = col_ids.shape[0]
    wide = 512
    return pl.pallas_call(
        mask_kernel,
        grid=(grid_len // wide,),
        in_specs=[full_spec(col_ids.shape), full_spec(weight_x.shape)],
        out_specs=pl.BlockSpec((samples, wide), lambda i: (0, i)),
        out_shape=jax.ShapeDtypeStruct((samples, grid_len), jnp.float32),
        name="column_mask",
    )(col_ids, weight_x)


def interpolate_kernel(g_ref, halo_ref, wy_ref, mask_ref, place_ref, out_ref):
    samples, grid_len = mask_ref.shape
    wide = 512
    left = split(wy_ref[...])
    partial = jnp.zeros((samples, RADIX), jnp.float32)
    for start in range(0, grid_len, wide):
        at = slice(start, start + wide)
        data = jnp.concatenate([g_ref[0, :, at], halo_ref[0, :, at]], axis=0)
        product = dot3(left, split(data)) * mask_ref[:, at]
        for lane in range(0, wide, RADIX):
            partial = partial + product[:, lane : lane + RADIX]
    value = jnp.sum(partial, axis=1, keepdims=True)
    out_ref[0] = jnp.sum(value * place_ref[...], axis=0, keepdims=True)


def interpolate(gradient, halo, group, weight_y, mask, placement):
    _, rows, grid_len = gradient.shape
    slot_total = placement.shape[1]
    small = (weight_y, mask, placement)
    return pl.pallas_call(
        interpolate_kernel,
        grid=(len(group),),
        in_specs=[
            pl.BlockSpec((1, rows, grid_len), lambda i: (i + group[0], 0, 0)),
            pl.BlockSpec((1, 8, grid_len), lambda i: (i, 0, 0)),
        ]
        + [full_spec(item.shape) for item in small],
        out_specs=pl.BlockSpec((1, 1, slot_total), lambda i: (i, 0, 0)),
        out_shape=jax.ShapeDtypeStruct((len(group), 1, slot_total), jnp.float32),
        compiler_params=pltpu.CompilerParams(vmem_limit_bytes=VMEM_LIMIT),
        name="interpolate",
    )(gradient, halo, *small)


def product(formula, operand_a, operand_b):
    return jnp.einsum(formula, operand_a, operand_b, precision=HIGH)


def complex_product(formula, pair, table):
    return (
        product(formula, pair[0], table[0]) - product(formula, pair[1], table[1]),
        product(formula, pair[0], table[1]) + product(formula, pair[1], table[0]),
    )


def phase(row_count, col_count, period, orient):
    theta = angles(np.arange(row_count), np.arange(col_count), period)
    return f32(np.cos(theta)), f32(orient * np.sin(theta))


def times_table(pair, table):
    return (
        pair[0] * table[0] - pair[1] * table[1],
        pair[0] * table[1] + pair[1] * table[0],
    )


def edge_waves(grid_len):
    outer_len = grid_len // RADIX
    index = np.arange(outer_len)[:, None] + outer_len * np.arange(RADIX)[None, :]
    signed = np.where(index < grid_len // 2, index, index - grid_len).astype(np.float32)
    full_y = signed * np.float32(2.0 * math.pi / grid_len)
    odd_y = np.where(index == grid_len // 2, np.float32(0.0), full_y)
    return full_y, odd_y


def edge_forward(values, layer_top, layer_thick):
    grid_len = values.shape[1]
    outer_len = grid_len // RADIX
    columns = values.reshape(2, outer_len, RADIX)
    first = phase(outer_len, outer_len, outer_len, -1.0)
    pair = (product("zab,ka->zkb", columns, first[0]), product("zab,ka->zkb", columns, first[1]))
    pair = times_table(pair, phase(outer_len, RADIX, grid_len, -1.0))
    pair = complex_product("zkb,bc->zkc", pair, phase(RADIX, RADIX, RADIX, -1.0))
    full_y, _ = edge_waves(grid_len)
    magnitude = jnp.sqrt(
        jnp.asarray(np.stack([full_y * full_y, full_y * full_y + np.float32(math.pi) ** 2]))
    )
    scale = (
        2.0
        * math.pi
        / (grid_len * grid_len)
        * (1.0 - jnp.exp(-magnitude * layer_thick))
        * jnp.exp(-magnitude * layer_top)
    )
    return jnp.stack([pair[0] * scale, pair[1] * scale])


def edge_inverse(total, row_start, row_share):
    outer_len = total.shape[2]
    grid_len = outer_len * RADIX
    full_y, odd_y = edge_waves(grid_len)
    full_x = np.array([0.0, math.pi], np.float32)[:, None, None]
    squared = full_x * full_x + full_y * full_y
    safe = np.where(squared > 0.0, squared, np.float32(1.0))
    none = np.zeros_like(safe)
    plain = f32(np.stack([-full_x * full_x / safe, none, none, -full_y * full_y / safe, none]))
    turned = f32(np.stack([none, none, none, none, odd_y / np.sqrt(safe)]))
    pair = (total[0] * plain - total[1] * turned, total[1] * plain + total[0] * turned)
    pair = complex_product("fzkc,cb->fzkb", pair, phase(RADIX, RADIX, RADIX, 1.0))
    pair = times_table(pair, phase(outer_len, RADIX, grid_len, 1.0))
    last = phase(outer_len, outer_len, outer_len, 1.0)
    last = [lax.dynamic_slice_in_dim(item, row_start, row_share, 0) for item in last]
    real = product("fzkb,ak->fzab", pair[0], last[0]) - product("fzkb,ak->fzab", pair[1], last[1])
    return jnp.moveaxis(real.reshape(FIELDS, 2, row_share * RADIX), 1, 2)


def cubic_kernel(distance):
    near_part = (1.5 * distance - 2.5) * distance * distance + 1.0
    far_part = ((-0.5 * distance + 2.5) * distance - 4.0) * distance + 2.0
    return jnp.where(distance <= 1.0, near_part, jnp.where(distance < 2.0, far_part, 0.0))


def tap_weights(level):
    offset = (level.astype(jnp.float32) + 0.5) / QLEV - 0.5
    base = jnp.where(level < QLEV // 2, -1, 0).astype(jnp.int32)
    fraction = offset - base.astype(jnp.float32)
    taps = jnp.arange(4, dtype=jnp.int32)[None, :]
    weights = cubic_kernel(jnp.abs(fraction[:, None] - (taps.astype(jnp.float32) - 1.0)))
    return weights, base[:, None] - 1 + taps


def choose(which, candidates):
    picked = None
    for key, value in candidates.items():
        picked = value if picked is None else jnp.where(which == key, value, picked)
    return picked


def depth_scan(pieces, jobs, total):
    count = lax.axis_size("depth")
    here = lax.axis_index("depth")
    up = [(i, i + 1) for i in range(count - 1)]
    down = [(i + 1, i) for i in range(count - 1)]
    from_below, from_above = [], []

    def complete(index):
        below = {d: from_below[index + d - 1] for d in range(1, count)}
        above = {count - 1 - d: from_above[index + d - 1] for d in range(1, count)}
        return pieces[index], below, above

    for step in range(total + count - 2):
        live = [d for d in range(count - 1) if 0 <= step - d < total]
        rising = choose(here, {d: pieces[step - d] for d in live})
        falling = choose(here, {count - 1 - d: pieces[step - d] for d in live})
        if step:
            rising, falling = rising + from_below[-1], falling + from_above[-1]
        work = jobs.get(step, [])
        keys = [key for _, key in work]
        rising, falling, keys = lax.optimization_barrier((rising, falling, keys))
        below = lax.ppermute(rising, "depth", up)
        above = lax.ppermute(falling, "depth", down)
        results = []
        for (task, _), key in zip(work, keys):
            if results:
                key, _ = lax.optimization_barrier((key, results[-1]))
            results.append(task(key, complete))
        below, above, _ = lax.optimization_barrier((below, above, results))
        from_below.append(below)
        from_above.append(above)
    return complete


def per_device(density, layer_top, layer_thick, sample_row, sample_col, sample_frac, sample_owner):
    wide_count = lax.axis_size("wide")
    depth_count = lax.axis_size("depth")
    rows_here, grid_len = density.shape[1], density.shape[2]
    outer_len = grid_len // RADIX
    tile_rows = rows_here // depth_count
    chunks = 2 * SLOTS // wide_count
    wide_id, depth_id = lax.axis_index("wide"), lax.axis_index("depth")

    def exchange(block):
        return lax.all_to_all(block, "wide", split_axis=0, concat_axis=0, tiled=True)

    groups = [range(0, SLOTS, 2), range(1, SLOTS, 2)] if chunks == 4 else [range(SLOTS)]
    spectra, field = [], density[0]
    for group in groups:
        made = row_forward(field, wide_count, tuple(group))
        spectra += [exchange(item) for item in made]
        field, _ = lax.optimization_barrier((field, made[0]))
    columns = [item.reshape(grid_len, RADIX) for item in spectra]

    lane = jnp.arange(RADIX, dtype=jnp.int32)[None, :] % HALF
    waves = []
    for chunk in range(chunks):
        block = wide_id * chunks + chunk
        slot = block // 2
        place = (block % 2) * HALF + lane
        low = jnp.where(
            place < HALF, outer_len * place, outer_len // 2 + outer_len * (place - HALF)
        )
        index = jnp.where(slot == 0, low, slot + outer_len * place)
        signed = jnp.where(index < grid_len // 2, index, index - grid_len).astype(jnp.float32)
        waves.append(signed * (2.0 * math.pi / grid_len))

    depths = jnp.concatenate([layer_top, layer_thick])
    edge = edge_forward(
        jnp.stack([columns[0][:, 0], columns[0][:, HALF]]), layer_top[0], layer_thick[0]
    )
    edge = lax.psum(edge, "depth")
    row_share = outer_len // depth_count
    row_start = depth_id * row_share
    place = (jnp.stack([wide_id, depth_id]).astype(jnp.int32), row_start, row_share)
    sizes = (grid_len, wide_count, tile_rows)
    taps_y, offset_y = tap_weights(sample_frac[0, 0])
    taps_x, offset_x = tap_weights(sample_frac[0, 1])
    row_ids = sample_row[0][:, None] + offset_y
    col_ids = (sample_col[0][:, None] + offset_x) % grid_len
    row_ids = jnp.where(
        row_ids < 0,
        row_ids + tile_rows + 2,
        jnp.where(row_ids >= tile_rows, row_ids + 2, row_ids),
    )
    row_marks = row_ids[:, :, None] == jnp.arange(tile_rows + 8, dtype=jnp.int32)
    weight_y = jnp.sum(jnp.where(row_marks, taps_y[:, :, None], 0.0), axis=1)
    sample_count = sample_row.shape[1]
    capacity = max(2 * sample_count // wide_count, 2)
    slot_total = wide_count * capacity
    owner_ids = sample_owner[0, :, 0]
    same = owner_ids[:, None] == owner_ids[None, :]
    order = jnp.arange(sample_count, dtype=jnp.int32)
    slot_ids = jnp.sum((same & (order[None, :] < order[:, None])).astype(jnp.int32), axis=1)
    target = owner_ids * capacity + slot_ids
    placement = (target[:, None] == jnp.arange(slot_total, dtype=jnp.int32)[None, :]).astype(
        jnp.float32
    )
    pieces, blocks, partial_sums, edges = [], {}, {}, []

    def forward_job(chunk, wave, complete):
        pieces.extend(column_forward(columns[chunk], wave, depths))
        return pieces[-1]

    def edge_job(key, complete):
        edges.append(edge_inverse(key[0], row_start, row_share))
        edges.append(column_mask(key[1], taps_x, grid_len))
        return edges

    def early_job(chunk, wave, complete):
        item = column_inverse(complete(2 * chunk), 0, wave, wave, place, None, None, sizes, EVERY)
        partial_sums[chunk] = item
        return item

    def late_job(chunk, wave, complete, groups=(EVERY,)):
        part = complete(2 * chunk + 1)
        special = edges[0] if chunk == 0 else None
        for group in groups:
            item = column_inverse(
                part, outer_len // 2, wave, wave, place, special, partial_sums[chunk], sizes, group
            )
            moved = exchange(item)
            for spot, c in enumerate(group):
                blocks[c, chunk] = (moved, spot)
            if group != groups[-1]:
                wave, _ = lax.optimization_barrier((wave, item))
        return item

    forward_job(0, waves[0], None)
    jobs = {}
    last = chunks - 1

    def plan(step, task, chunk):
        jobs.setdefault(step, []).append((functools.partial(task, chunk), waves[chunk]))

    for chunk in range(1, chunks):
        plan(chunk - 1, forward_job, chunk)
    for chunk in range(chunks):
        plan(2 * chunk + depth_count - 1, early_job, chunk)
        if chunk != last:
            plan(2 * chunk + depth_count, late_job, chunk)
    jobs.setdefault(EDGE_STEP, []).append((edge_job, (edge, col_ids)))
    complete = depth_scan(pieces, jobs, 2 * chunks)
    late_job(last, waves[last], complete, GROUPS)

    tiles = depth_count * wide_count
    forward = [(i, (i + 1) % tiles) for i in range(tiles)]
    backward = [(target, source) for source, target in forward]
    gradient, halos = None, []
    for group in GROUPS:
        ready = [[blocks[c, chunk] for chunk in range(chunks)] for c in group]
        gradient, top, bottom = row_inverse(ready, grid_len, gradient)
        used = len(group)
        gradient, bottom, top = lax.optimization_barrier(
            (gradient, bottom[:used, 6:], top[:used, :2])
        )
        low = lax.ppermute(bottom, ("depth", "wide"), forward)
        high = lax.ppermute(top, ("depth", "wide"), backward)
        halos.append(
            jnp.concatenate([low, high, jnp.zeros((used, 4, grid_len), jnp.float32)], axis=1)
        )

    outgoing = [
        interpolate(gradient, halo, group, weight_y, edges[1], placement)
        for group, halo in zip(GROUPS, halos)
    ]
    outgoing = jnp.concatenate(outgoing)
    outgoing = outgoing.reshape(FIELDS, wide_count, capacity)
    arrived = lax.all_to_all(outgoing, "wide", split_axis=1, concat_axis=1, tiled=True)
    arrived = arrived.reshape(FIELDS, 1, slot_total)
    return (gradient, jnp.concatenate([arrived, -(arrived[0:1] + arrived[3:4])]))


def solution(mesh):
    in_specs = (
        P("depth", "wide", None),
        P("depth"),
        P("depth"),
        P(("depth", "wide"), None),
        P(("depth", "wide"), None),
        P(("depth", "wide"), None, None),
        P(("depth", "wide"), None, None),
    )
    out_specs = (P(None, ("depth", "wide"), None), P(None, ("depth", "wide"), None))
    return jax.shard_map(
        per_device, mesh=mesh, in_specs=in_specs, out_specs=out_specs, check_vma=False
    )
```

```python
import functools
import math

import jax
import jax.numpy as jnp
import ml_dtypes
import numpy as np
from jax import lax
from jax.experimental import pallas as pl
from jax.experimental.pallas import tpu as pltpu
from jax.sharding import PartitionSpec as P

RADIX = 128
QLEV = 16
HALF = 64
SLOTS = 16
FIELDS = 5
GROUPS = ((0, 1, 2, 3, 4),)
EVERY = tuple(range(FIELDS))
EDGE_STEP = 2
HIGH = lax.Precision.HIGHEST
VMEM_LIMIT = 56 * 1024 * 1024


def np_split(table):
    high = table.astype(np.float32).astype(ml_dtypes.bfloat16)
    low = (table - high.astype(np.float64)).astype(ml_dtypes.bfloat16)
    return jnp.asarray(high), jnp.asarray(low)


def f32(table):
    return jnp.asarray(np.asarray(table, np.float32))


def angles(left, right, period):
    return (np.outer(left, right) % period) * (2.0 * math.pi / period)


def lane_order():
    column = np.arange(256)
    wave = (column // 128) * HALF + column % HALF
    return wave, (column % 128) // HALF


def slot_zero_angles(grid_len):
    wave, part = lane_order()
    outer_len = grid_len // RADIX
    upper = wave >= HALF
    freq = np.where(upper, outer_len // 2 + outer_len * (wave - HALF), outer_len * wave)
    return wave, part, upper, angles(np.arange(RADIX), freq, grid_len)


def row_forward_tables(grid_len, slots):
    outer_len = grid_len // RADIX
    stride = slots[1] - slots[0]
    theta = angles(np.asarray(slots), np.arange(outer_len), outer_len)
    first = np.zeros((2 * len(slots), outer_len))
    first[0::2] = np.cos(theta)
    first[1::2] = -np.sin(theta)
    if slots[0] == 0:
        first[1] = np.cos(np.pi * np.arange(outer_len))
    kron = np.kron(first, np.eye(8))
    wave, part = lane_order()
    step = 2.0 * math.pi * np.arange(RADIX)[:, None] / grid_len * np.ones((1, 256))
    alpha = angles(np.arange(RADIX), wave, RADIX) + slots[0] * step
    base = np.concatenate(
        [
            np.where(part == 0, np.cos(alpha), -np.sin(alpha)),
            np.where(part == 0, np.sin(alpha), np.cos(alpha)),
        ]
    )
    wave, part, upper, alpha = slot_zero_angles(grid_len)
    table = np.where(part == 0, np.cos(alpha), -np.sin(alpha))
    top = np.where(upper, 0.0, table)
    top[:, (wave == 0) & (part == 1)] = np.cos(np.pi * np.arange(RADIX))[:, None]
    zero = np.concatenate([top, np.where(upper, table, 0.0)])
    return kron, base, zero if slots[0] == 0 else base, np.cos(stride * step), np.sin(stride * step)


def row_inverse_tables(grid_len):
    outer_len = grid_len // RADIX
    theta = angles(np.arange(outer_len), np.arange(SLOTS), outer_len)
    last = np.zeros((outer_len, 2 * SLOTS))
    last[:, 0::2] = np.cos(theta)
    last[:, 1::2] = -np.sin(theta)
    last[:, 1] = np.cos(np.pi * np.arange(outer_len))
    kron = np.kron(last, np.eye(8))
    wave, part = lane_order()
    alpha = angles(wave, np.arange(RADIX), RADIX)
    real_row = (part == 0)[:, None]
    base = 2.0 * np.concatenate(
        [
            np.where(real_row, np.cos(alpha), -np.sin(alpha)),
            np.where(real_row, np.sin(alpha), np.cos(alpha)),
        ],
        axis=1,
    )
    wave, part, upper, alpha = slot_zero_angles(grid_len)
    table = 2.0 * np.where(part == 0, np.cos(alpha), -np.sin(alpha))
    left = np.where(upper, 0.0, table)
    left[:, (wave == 0) & (part == 0)] = 1.0
    left[:, (wave == 0) & (part == 1)] = np.cos(np.pi * np.arange(RADIX))[:, None]
    zero = np.concatenate([left.T, np.where(upper, table, 0.0).T], axis=1)
    beta = 2.0 * math.pi * np.arange(RADIX)[None, :] / grid_len
    return kron, base, zero, np.cos(beta), np.sin(beta)


def column_kron(outer_len, orient):
    theta = angles(np.arange(outer_len), np.arange(outer_len), outer_len)
    return np.concatenate(
        [np.kron(np.cos(theta), np.eye(8)), np.kron(orient * np.sin(theta), np.eye(8))], axis=1
    )


def split(value):
    high = value.astype(jnp.bfloat16)
    return high, (value - high.astype(jnp.float32)).astype(jnp.bfloat16)


def mm(left, right):
    return jnp.dot(left, right, preferred_element_type=jnp.float32)


def dot3(left, right):
    rows = left[0].shape[0]
    both = mm(jnp.concatenate(left, axis=0), right[0])
    return both[:rows] + both[rows:] + mm(left[0], right[1])


def rotate(value):
    lane = lax.broadcasted_iota(jnp.int32, value.shape, 1)
    return jnp.where(lane < HALF, -1.0, 1.0) * pltpu.roll(value, HALF, 1)


def row_forward_kernel(chunks, slots, x_ref, kh, kl, base, zero, cw, sw, *refs):
    outs = refs[:-4]
    th, tl, rot, u_ref = refs[-4:]
    rows = x_ref.shape[0]
    outer_len = x_ref.shape[1] // RADIX

    @pl.when(pl.program_id(0) == 0)
    def _():
        th[0], tl[0] = split(zero[...])
        rot[...] = base[...]
        for slot in range(1, len(slots)):
            top, low = rot[0:RADIX, :], rot[RADIX:, :]
            rot[0:RADIX, :] = cw[...] * top - sw[...] * low
            rot[RADIX:, :] = cw[...] * low + sw[...] * top
            th[slot], tl[slot] = split(rot[...])

    table = (kh[...], kl[...])

    def first(pair, carry):
        halves = [
            jnp.concatenate(
                [
                    x_ref[pl.ds(pair * 16 + 8 * side, 8), RADIX * a : RADIX * (a + 1)]
                    for a in range(outer_len)
                ],
                axis=0,
            )
            for side in range(2)
        ]
        u_ref[pair] = dot3(table, split(jnp.concatenate(halves, axis=1)))
        return carry

    lax.fori_loop(0, rows // 16, first, 0, unroll=min(2, rows // 16))
    for slot in range(len(slots)):
        parts = []
        for part in range(2):
            at = 16 * slot + 8 * part
            parts.append(
                jnp.concatenate(
                    [
                        u_ref[pair, at : at + 8, RADIX * side : RADIX * (side + 1)]
                        for pair in range(rows // 16)
                        for side in range(2)
                    ],
                    axis=0,
                )
            )
        result = dot3(split(jnp.concatenate(parts, axis=1)), (th[slot], tl[slot]))
        for side in range(2):
            block = 2 * slots[slot] + side
            outs[block % chunks % len(outs)][block // chunks] = result[:, RADIX * side : RADIX * (side + 1)]


def full_spec(shape):
    return pl.BlockSpec(shape, lambda *_: (0,) * len(shape))


def row_forward(field, wide_count, slots):
    rows, grid_len = field.shape
    chunks = 2 * SLOTS // wide_count
    made = min(chunks, 2) if len(slots) < SLOTS else chunks
    step = min(rows, 128)
    kron, base, zero, cw, sw = row_forward_tables(grid_len, slots)
    tables = (*np_split(kron), f32(base), f32(zero), f32(cw), f32(sw))
    return pl.pallas_call(
        functools.partial(row_forward_kernel, chunks, slots),
        grid=(rows // step,),
        in_specs=[pl.BlockSpec((step, grid_len), lambda i: (i, 0))]
        + [full_spec(item.shape) for item in tables],
        out_specs=[pl.BlockSpec((wide_count, step, RADIX), lambda i: (0, i, 0))] * made,
        out_shape=[jax.ShapeDtypeStruct((wide_count, rows, RADIX), jnp.float32)] * made,
        scratch_shapes=[
            pltpu.VMEM((len(slots), 256, 256), jnp.bfloat16),
            pltpu.VMEM((len(slots), 256, 256), jnp.bfloat16),
            pltpu.VMEM((256, 256), jnp.float32),
            pltpu.VMEM((step // 16, 16 * len(slots), 256), jnp.float32),
        ],
        compiler_params=pltpu.CompilerParams(vmem_limit_bytes=VMEM_LIMIT),
        cost_estimate=pl.CostEstimate(
            flops=20 * len(slots) // SLOTS * rows * grid_len * 256, bytes_accessed=8 * rows * grid_len, transcendentals=0
        ),
        name="row_forward",
    )(field, *tables)


def wave_y(first, shape, grid_len):
    outer_len = grid_len // RADIX
    index = first + outer_len * lax.broadcasted_iota(jnp.int32, shape, 0)
    signed = jnp.where(index < grid_len // 2, index, index - grid_len).astype(jnp.float32)
    full = signed * (2.0 * math.pi / grid_len)
    return full, jnp.where(index == grid_len // 2, 0.0, full)


def column_forward_kernel(
    grid_len, depth_ref, x_ref, kx_ref, kh, kl, ca, sa, cw, sw, low_ref, high_ref, *scratch
):
    u_ref, c_ref, s_ref = scratch
    outer_len = grid_len // RADIX
    table = (kh[...], kl[...])

    def first(pair, carry):
        halves = [
            jnp.concatenate(
                [x_ref[pl.ds(a * RADIX + pair * 16 + 8 * side, 8), :] for a in range(outer_len)],
                axis=0,
            )
            for side in range(2)
        ]
        turned = [rotate(half) for half in halves]
        data = jnp.concatenate(
            [jnp.concatenate(halves, axis=1), jnp.concatenate(turned, axis=1)], axis=0
        )
        result = dot3(table, split(data))
        for k1 in range(outer_len):
            for side in range(2):
                u_ref[pl.ds(k1 * RADIX + pair * 16 + 8 * side, 8), :] = result[
                    8 * k1 : 8 * k1 + 8, RADIX * side : RADIX * (side + 1)
                ]
        return carry

    lax.fori_loop(0, RADIX // 16, first, 0, unroll=4)
    c_ref[...] = ca[...]
    s_ref[...] = sa[...]
    top, thick = depth_ref[0], depth_ref[1]

    middle = outer_len // 2

    def second(out_ref, start, step, carry):
        k1 = start + step
        cosine, sine = c_ref[...], s_ref[...]
        table = split(jnp.concatenate([cosine, sine], axis=1))
        c_ref[...] = cosine * cw[...] - sine * sw[...]
        s_ref[...] = sine * cw[...] + cosine * sw[...]
        rows = pl.ds(pl.multiple_of(k1 * RADIX, RADIX), RADIX)
        data = u_ref[rows, :]
        result = dot3(table, split(jnp.concatenate([data, rotate(data)], axis=0)))
        full_y, _ = wave_y(k1, (RADIX, RADIX), grid_len)
        magnitude = jnp.sqrt(kx_ref[...] * kx_ref[...] + full_y * full_y)
        scale = (1.0 - jnp.exp(-magnitude * thick)) * jnp.exp(-magnitude * top)
        out_ref[pl.ds(pl.multiple_of(step * RADIX, RADIX), RADIX), :] = result * (
            scale * (2.0 * math.pi / (grid_len * grid_len))
        )
        return carry

    lax.fori_loop(0, middle, functools.partial(second, low_ref, 0), 0, unroll=4)
    lax.fori_loop(0, middle, functools.partial(second, high_ref, middle), 0, unroll=4)


def column_forward(block, wave_x, depths):
    grid_len = block.shape[0]
    outer_len = grid_len // RADIX
    alpha = angles(np.arange(RADIX), np.arange(RADIX), RADIX)
    beta = 2.0 * math.pi * np.arange(RADIX)[None, :] / grid_len
    tables = (
        *np_split(column_kron(outer_len, -1.0)),
        f32(np.cos(alpha)),
        f32(-np.sin(alpha)),
        f32(np.cos(beta)),
        f32(-np.sin(beta)),
    )
    square = (RADIX, RADIX)
    return pl.pallas_call(
        functools.partial(column_forward_kernel, grid_len),
        in_specs=[pl.BlockSpec(memory_space=pltpu.SMEM)]
        + [pl.BlockSpec(memory_space=pltpu.VMEM)] * (2 + len(tables)),
        out_specs=[pl.BlockSpec(memory_space=pltpu.VMEM)] * 2,
        out_shape=[jax.ShapeDtypeStruct((grid_len // 2, RADIX), jnp.float32)] * 2,
        scratch_shapes=[
            pltpu.VMEM((grid_len, RADIX), jnp.float32),
            pltpu.VMEM(square, jnp.float32),
            pltpu.VMEM(square, jnp.float32),
        ],
        compiler_params=pltpu.CompilerParams(vmem_limit_bytes=VMEM_LIMIT),
        cost_estimate=pl.CostEstimate(
            flops=100 * grid_len * RADIX * 256,
            bytes_accessed=8 * grid_len * RADIX,
            transcendentals=2 * grid_len * RADIX,
        ),
        name="column_forward",
    )(depths, block, wave_x, *tables)


def column_inverse_kernel(
    grid_len, tile_rows, start, count, special, added, keys, fields, flag_ref, kx_ref, kxo_ref, *refs
):
    keys = tuple(group for group in keys if group)
    moves = [refs[0:1]]
    at = 1
    for group in keys:
        moves.append(refs[at : at + len(group)])
        at += len(group)
    refs, (held, arrived) = refs[at:-2], refs[-2:]
    for slot, (group, sources) in enumerate(zip(((),) + keys, moves)):
        for position, source in enumerate(sources):
            fetch = pltpu.make_async_copy(source, held.at[slot], arrived.at[slot])
            if slot == 0:
                fetch.start()
            elif position == 0:
                others = [flag_ref[1] != key for key in group[1:]]
                pl.when(functools.reduce(jnp.logical_and, others, flag_ref[1] >= 0))(fetch.start)
            else:
                pl.when(flag_ref[1] == group[position])(fetch.start)
    bh, bl, ca, sa, cw, sw = refs[:6]
    edge_ref = refs[6] if special else None
    sum_ref = refs[6 + special] if added else None
    out_ref, v_ref, c_ref, s_ref = refs[6 + special + added :]
    here = bh.shape[0] // 8
    c_ref[...] = ca[...]
    s_ref[...] = sa[...]

    def first(step, carry):
        cosine, sine = c_ref[...], s_ref[...]
        table = split(jnp.concatenate([cosine, sine], axis=1))
        c_ref[...] = cosine * cw[...] - sine * sw[...]
        s_ref[...] = sine * cw[...] + cosine * sw[...]
        full_y, odd_y = wave_y(start + step, (RADIX, RADIX), grid_len)
        full_x, odd_x = kx_ref[...], kxo_ref[...]
        squared = full_x * full_x + full_y * full_y
        safe = jnp.where(squared > 0.0, squared, 1.0)
        root = lax.rsqrt(safe)
        inverse = root * root
        rows = pl.ds(pl.multiple_of(step * RADIX, RADIX), RADIX)
        value = held[0, rows, :]
        for slot in range(1, held.shape[0]):
            value = value + held[slot, rows, :]
        turned = rotate(value)
        coef_xx = -full_x * full_x * inverse
        coef_xy = -odd_x * odd_y * inverse
        coef_yy = -full_y * full_y * inverse
        slope_x = odd_x * root
        slope_y = odd_y * root
        upper = [
            value * coef_xx,
            value * coef_xy,
            turned * slope_x,
            value * coef_yy,
            turned * slope_y,
        ]
        lower = [
            turned * coef_xx,
            turned * coef_xy,
            -value * slope_x,
            turned * coef_yy,
            -value * slope_y,
        ]
        upper = jnp.concatenate([upper[c] for c in fields], axis=1)
        lower = jnp.concatenate([lower[c] for c in fields], axis=1)
        data = jnp.concatenate([upper, lower], axis=0)
        v_ref[rows, :] = dot3(table, split(data))
        return carry

    for slot, sources in enumerate(moves):
        pltpu.make_async_copy(sources[0], held.at[slot], arrived.at[slot]).wait()
    lax.fori_loop(0, count, first, 0, unroll=8)
    both = jnp.concatenate([bh[...], bl[...]], axis=0)
    span = 8 * here

    def second(group, carry):
        data = jnp.concatenate(
            [v_ref[pl.ds(k1 * RADIX + group * 8, 8), :] for k1 in range(count)], axis=0
        )
        turned = jnp.concatenate(
            [rotate(data[:, RADIX * c : RADIX * (c + 1)]) for c in range(len(fields))], axis=1
        )
        high, low = split(jnp.concatenate([data, turned], axis=0))
        stacked = mm(both, high)
        result = stacked[:span] + stacked[span:] + mm(bh[...], low)
        per_row = RADIX // tile_rows
        row = (group * 8) % tile_rows
        for a in range(here):
            dest = a * per_row + (group * 8) // tile_rows
            for spot, c in enumerate(fields):
                piece = result[8 * a : 8 * a + 8, RADIX * spot : RADIX * (spot + 1)]
                if added:
                    piece = piece + sum_ref[dest, c, pl.ds(row, 8), :]
                if special:
                    lane = lax.broadcasted_iota(jnp.int32, piece.shape, 1)
                    edge = edge_ref[c, pl.ds(a * RADIX + group * 8, 8), :]
                    edge = jnp.where(lane < HALF, edge[:, 0:1], edge[:, 1:2])
                    piece = jnp.where((lane % HALF == 0) & (flag_ref[0] == 0), edge, piece)
                out_ref[dest, spot, pl.ds(row, 8), :] = piece
        return carry

    lax.fori_loop(0, RADIX // 8, second, 0, unroll=8)


def column_inverse(part, start, wave_x, odd_x, place, edge, partial_sum, sizes, fields):
    grid_len, wide_count, tile_rows = sizes
    flag, row_start, row_share = place
    piece, below, above = part
    count = piece.shape[0] // RADIX
    moved = [piece, *below.values(), *above.values()]
    outer_len = grid_len // RADIX
    alpha = angles(np.arange(RADIX), np.arange(RADIX), RADIX)
    beta = 2.0 * math.pi * np.arange(RADIX)[:, None] / grid_len * np.ones((1, RADIX))
    alpha = alpha + start * beta
    kron = column_kron(outer_len, 1.0)
    chosen = np.arange(start * 8, (start + count) * 8)
    kron = kron[:, np.concatenate([chosen, chosen + 8 * outer_len])]
    share = [
        lax.dynamic_slice_in_dim(item, row_start * 8, row_share * 8, 0) for item in np_split(kron)
    ]
    tables = [
        *share,
        f32(np.cos(alpha)),
        f32(np.sin(alpha)),
        f32(np.cos(beta)),
        f32(np.sin(beta)),
    ]
    extra = [item for item in (edge, partial_sum) if item is not None]
    operands = [*tables, *extra]
    plain = [pl.BlockSpec(memory_space=pltpu.VMEM)]
    square = (RADIX, RADIX)
    out_shape = (wide_count, len(fields), tile_rows, RADIX)
    return pl.pallas_call(
        functools.partial(
            column_inverse_kernel,
            grid_len,
            tile_rows,
            start,
            count,
            int(edge is not None),
            int(partial_sum is not None),
            (tuple(below), tuple(above)),
            fields,
        ),
        in_specs=[pl.BlockSpec(memory_space=pltpu.SMEM)]
        + plain * 2
        + [pl.BlockSpec(memory_space=pl.ANY)] * len(moved)
        + plain * len(operands),
        out_specs=pl.BlockSpec(memory_space=pltpu.VMEM),
        out_shape=jax.ShapeDtypeStruct(out_shape, jnp.float32),
        scratch_shapes=[
            pltpu.VMEM((count * RADIX, len(fields) * RADIX), jnp.float32),
            pltpu.VMEM(square, jnp.float32),
            pltpu.VMEM(square, jnp.float32),
            pltpu.VMEM((3 if below else 1, count * RADIX, RADIX), jnp.float32),
            pltpu.SemaphoreType.DMA((3 if below else 1,)),
        ],
        compiler_params=pltpu.CompilerParams(vmem_limit_bytes=VMEM_LIMIT),
        cost_estimate=pl.CostEstimate(
            flops=len(fields) * 45 * count * RADIX * RADIX * 256,
            bytes_accessed=4 * (count * RADIX * RADIX + math.prod(out_shape)),
            transcendentals=count * RADIX * RADIX,
        ),
        name="column_inverse",
    )(flag, wave_x, odd_x, *moved, *operands)


def row_inverse_kernel(chunks, fields, *refs):
    ins, refs = refs[: chunks * fields], refs[chunks * fields :]
    kh, kl, base, zero, cw, sw = refs[:6]
    trace_ref = refs[6] if len(refs) == 14 else None
    out_ref, top_ref, bottom_ref, th, tl, rot, u_ref = refs[-7:]
    rows = ins[0].shape[2]
    outer_len = out_ref.shape[2] // RADIX

    @pl.when(pl.program_id(0) == 0)
    def _():
        th[0], tl[0] = split(zero[...])
        rot[...] = base[...]
        for slot in range(1, SLOTS):
            left, right = rot[:, 0:RADIX], rot[:, RADIX:]
            rot[:, 0:RADIX] = cw[...] * left - sw[...] * right
            rot[:, RADIX:] = cw[...] * right + sw[...] * left
            th[slot], tl[slot] = split(rot[...])

    for slot in range(SLOTS):
        parts = []
        for side in range(2):
            block = 2 * slot + side
            parts.append(
                jnp.concatenate(
                    [ins[c * chunks + block % chunks][block // chunks, 0] for c in range(fields)],
                    axis=0,
                )
            )
        u_ref[slot] = dot3(split(jnp.concatenate(parts, axis=1)), (th[slot], tl[slot]))

    table = (kh[...], kl[...])
    for c in range(fields):

        def second(pair, carry):
            halves = []
            for side in range(2):
                at = pl.ds(c * rows + pair * 16 + 8 * side, 8)
                halves.append(
                    jnp.concatenate(
                        [
                            u_ref[slot, at, RADIX * part : RADIX * (part + 1)]
                            for slot in range(SLOTS)
                            for part in range(2)
                        ],
                        axis=0,
                    )
                )
            result = dot3(table, split(jnp.concatenate(halves, axis=1)))
            for a in range(outer_len):
                for side in range(2):
                    out_ref[
                        c, pl.ds(pair * 16 + 8 * side, 8), RADIX * a : RADIX * (a + 1)
                    ] = result[8 * a : 8 * a + 8, RADIX * side : RADIX * (side + 1)]
            return carry

        lax.fori_loop(0, rows // 16, second, 0, unroll=min(2, rows // 16))
    if trace_ref is not None:
        out_ref[fields] = -(trace_ref[0] + out_ref[0])
    elif fields == FIELDS:
        out_ref[fields] = -(out_ref[0] + out_ref[3])

    @pl.when(pl.program_id(0) == 0)
    def _():
        top_ref[...] = out_ref[:, 0:8, :]

    @pl.when(pl.program_id(0) == pl.num_programs(0) - 1)
    def _():
        bottom_ref[...] = out_ref[:, rows - 8 : rows, :]


def row_inverse(pieces, grid_len, earlier):
    fields, chunks = len(pieces), len(pieces[0])
    wide_count, _, rows, _ = pieces[0][0][0].shape
    step = min(rows, 32 if fields == FIELDS else 64)
    made = FIELDS + 1 if fields == FIELDS else 3
    kron, base, zero, cw, sw = row_inverse_tables(grid_len)
    tables = (*np_split(kron), f32(base), f32(zero), f32(cw), f32(sw))
    specs, operands = [], []
    for per_chunk in pieces:
        for array, index in per_chunk:
            specs.append(
                pl.BlockSpec((wide_count, 1, step, RADIX), lambda i, index=index: (0, index, i, 0))
            )
            operands.append(array)
    specs += [full_spec(item.shape) for item in tables]
    operands += tables
    aliases = {}
    if earlier is not None:
        aliases = {len(operands): 0}
        specs.append(pl.BlockSpec((1, step, grid_len), lambda i: (0, i, 0)))
        operands.append(earlier)
    group = 0 if earlier is None else 1
    edge = jax.ShapeDtypeStruct((made, 8, grid_len), jnp.float32)
    return pl.pallas_call(
        functools.partial(row_inverse_kernel, chunks, fields),
        grid=(rows // step,),
        in_specs=specs,
        out_specs=[pl.BlockSpec((made, step, grid_len), lambda i: (group, i, 0))]
        + [full_spec(edge.shape)] * 2,
        out_shape=[jax.ShapeDtypeStruct((FIELDS + 1, rows, grid_len), jnp.float32), edge, edge],
        scratch_shapes=[
            pltpu.VMEM((SLOTS, 256, 256), jnp.bfloat16),
            pltpu.VMEM((SLOTS, 256, 256), jnp.bfloat16),
            pltpu.VMEM((256, 256), jnp.float32),
            pltpu.VMEM((SLOTS, fields * step, 256), jnp.float32),
        ],
        input_output_aliases=aliases,
        compiler_params=pltpu.CompilerParams(vmem_limit_bytes=VMEM_LIMIT),
        cost_estimate=pl.CostEstimate(
            flops=12 * fields * rows * grid_len * 256,
            bytes_accessed=8 * fields * rows * grid_len,
            transcendentals=0,
        ),
        name="row_inverse",
    )(*operands)


def mask_kernel(col_ref, wx_ref, mask_ref):
    samples, wide = mask_ref.shape
    lane = pl.program_id(0) * wide + lax.broadcasted_iota(jnp.int32, (samples, wide), 1)
    total = jnp.zeros((samples, wide), jnp.float32)
    for tap in range(4):
        here = lane == col_ref[:, tap : tap + 1]
        total = total + jnp.where(here, wx_ref[:, tap : tap + 1], 0.0)
    mask_ref[...] = total


def column_mask(col_ids, weight_x, grid_len):
    samples = col_ids.shape[0]
    wide = 512
    return pl.pallas_call(
        mask_kernel,
        grid=(grid_len // wide,),
        in_specs=[full_spec(col_ids.shape), full_spec(weight_x.shape)],
        out_specs=pl.BlockSpec((samples, wide), lambda i: (0, i)),
        out_shape=jax.ShapeDtypeStruct((samples, grid_len), jnp.float32),
        name="column_mask",
    )(col_ids, weight_x)


def interpolate_kernel(g_ref, halo_ref, wy_ref, mask_ref, place_ref, out_ref):
    samples, grid_len = mask_ref.shape
    wide = 512
    left = split(wy_ref[...])
    partial = jnp.zeros((samples, RADIX), jnp.float32)
    for start in range(0, grid_len, wide):
        at = slice(start, start + wide)
        data = jnp.concatenate([g_ref[0, :, at], halo_ref[0, :, at]], axis=0)
        product = dot3(left, split(data)) * mask_ref[:, at]
        for lane in range(0, wide, RADIX):
            partial = partial + product[:, lane : lane + RADIX]
    value = jnp.sum(partial, axis=1, keepdims=True)
    out_ref[0] = jnp.sum(value * place_ref[...], axis=0, keepdims=True)


def interpolate(gradient, halo, group, weight_y, mask, placement):
    _, rows, grid_len = gradient.shape
    slot_total = placement.shape[1]
    small = (weight_y, mask, placement)
    return pl.pallas_call(
        interpolate_kernel,
        grid=(len(group),),
        in_specs=[
            pl.BlockSpec((1, rows, grid_len), lambda i: (i + group[0], 0, 0)),
            pl.BlockSpec((1, 8, grid_len), lambda i: (i, 0, 0)),
        ]
        + [full_spec(item.shape) for item in small],
        out_specs=pl.BlockSpec((1, 1, slot_total), lambda i: (i, 0, 0)),
        out_shape=jax.ShapeDtypeStruct((len(group), 1, slot_total), jnp.float32),
        compiler_params=pltpu.CompilerParams(vmem_limit_bytes=VMEM_LIMIT),
        name="interpolate",
    )(gradient, halo, *small)


def product(formula, operand_a, operand_b):
    return jnp.einsum(formula, operand_a, operand_b, precision=HIGH)


def complex_product(formula, pair, table):
    return (
        product(formula, pair[0], table[0]) - product(formula, pair[1], table[1]),
        product(formula, pair[0], table[1]) + product(formula, pair[1], table[0]),
    )


def phase(row_count, col_count, period, orient):
    theta = angles(np.arange(row_count), np.arange(col_count), period)
    return f32(np.cos(theta)), f32(orient * np.sin(theta))


def times_table(pair, table):
    return (
        pair[0] * table[0] - pair[1] * table[1],
        pair[0] * table[1] + pair[1] * table[0],
    )


def edge_waves(grid_len):
    outer_len = grid_len // RADIX
    index = np.arange(outer_len)[:, None] + outer_len * np.arange(RADIX)[None, :]
    signed = np.where(index < grid_len // 2, index, index - grid_len).astype(np.float32)
    full_y = signed * np.float32(2.0 * math.pi / grid_len)
    odd_y = np.where(index == grid_len // 2, np.float32(0.0), full_y)
    return full_y, odd_y


def edge_forward(values, layer_top, layer_thick):
    grid_len = values.shape[1]
    outer_len = grid_len // RADIX
    columns = values.reshape(2, outer_len, RADIX)
    first = phase(outer_len, outer_len, outer_len, -1.0)
    pair = (product("zab,ka->zkb", columns, first[0]), product("zab,ka->zkb", columns, first[1]))
    pair = times_table(pair, phase(outer_len, RADIX, grid_len, -1.0))
    pair = complex_product("zkb,bc->zkc", pair, phase(RADIX, RADIX, RADIX, -1.0))
    full_y, _ = edge_waves(grid_len)
    magnitude = jnp.sqrt(
        jnp.asarray(np.stack([full_y * full_y, full_y * full_y + np.float32(math.pi) ** 2]))
    )
    scale = (
        2.0
        * math.pi
        / (grid_len * grid_len)
        * (1.0 - jnp.exp(-magnitude * layer_thick))
        * jnp.exp(-magnitude * layer_top)
    )
    return jnp.stack([pair[0] * scale, pair[1] * scale])


def edge_inverse(total, row_start, row_share):
    outer_len = total.shape[2]
    grid_len = outer_len * RADIX
    full_y, odd_y = edge_waves(grid_len)
    full_x = np.array([0.0, math.pi], np.float32)[:, None, None]
    squared = full_x * full_x + full_y * full_y
    safe = np.where(squared > 0.0, squared, np.float32(1.0))
    none = np.zeros_like(safe)
    plain = f32(np.stack([-full_x * full_x / safe, none, none, -full_y * full_y / safe, none]))
    turned = f32(np.stack([none, none, none, none, odd_y / np.sqrt(safe)]))
    pair = (total[0] * plain - total[1] * turned, total[1] * plain + total[0] * turned)
    pair = complex_product("fzkc,cb->fzkb", pair, phase(RADIX, RADIX, RADIX, 1.0))
    pair = times_table(pair, phase(outer_len, RADIX, grid_len, 1.0))
    last = phase(outer_len, outer_len, outer_len, 1.0)
    last = [lax.dynamic_slice_in_dim(item, row_start, row_share, 0) for item in last]
    real = product("fzkb,ak->fzab", pair[0], last[0]) - product("fzkb,ak->fzab", pair[1], last[1])
    return jnp.moveaxis(real.reshape(FIELDS, 2, row_share * RADIX), 1, 2)


def cubic_kernel(distance):
    near_part = (1.5 * distance - 2.5) * distance * distance + 1.0
    far_part = ((-0.5 * distance + 2.5) * distance - 4.0) * distance + 2.0
    return jnp.where(distance <= 1.0, near_part, jnp.where(distance < 2.0, far_part, 0.0))


def tap_weights(level):
    offset = (level.astype(jnp.float32) + 0.5) / QLEV - 0.5
    base = jnp.where(level < QLEV // 2, -1, 0).astype(jnp.int32)
    fraction = offset - base.astype(jnp.float32)
    taps = jnp.arange(4, dtype=jnp.int32)[None, :]
    weights = cubic_kernel(jnp.abs(fraction[:, None] - (taps.astype(jnp.float32) - 1.0)))
    return weights, base[:, None] - 1 + taps


def choose(which, candidates):
    picked = None
    for key, value in candidates.items():
        picked = value if picked is None else jnp.where(which == key, value, picked)
    return picked


def depth_scan(pieces, jobs, total):
    count = lax.axis_size("depth")
    here = lax.axis_index("depth")
    up = [(i, i + 1) for i in range(count - 1)]
    down = [(i + 1, i) for i in range(count - 1)]
    from_below, from_above = [], []

    def complete(index):
        below = {d: from_below[index + d - 1] for d in range(1, count)}
        above = {count - 1 - d: from_above[index + d - 1] for d in range(1, count)}
        return pieces[index], below, above

    for step in range(total + count - 2):
        live = [d for d in range(count - 1) if 0 <= step - d < total]
        rising = choose(here, {d: pieces[step - d] for d in live})
        falling = choose(here, {count - 1 - d: pieces[step - d] for d in live})
        if step:
            rising, falling = rising + from_below[-1], falling + from_above[-1]
        work = jobs.get(step, [])
        keys = [key for _, key in work]
        rising, falling, keys = lax.optimization_barrier((rising, falling, keys))
        below = lax.ppermute(rising, "depth", up)
        above = lax.ppermute(falling, "depth", down)
        results = [task(key, complete) for (task, _), key in zip(work, keys)]
        below, above, _ = lax.optimization_barrier((below, above, results))
        from_below.append(below)
        from_above.append(above)
    return complete


def per_device(density, layer_top, layer_thick, sample_row, sample_col, sample_frac, sample_owner):
    wide_count = lax.axis_size("wide")
    depth_count = lax.axis_size("depth")
    rows_here, grid_len = density.shape[1], density.shape[2]
    outer_len = grid_len // RADIX
    tile_rows = rows_here // depth_count
    chunks = 2 * SLOTS // wide_count
    wide_id, depth_id = lax.axis_index("wide"), lax.axis_index("depth")

    def exchange(block):
        return lax.all_to_all(block, "wide", split_axis=0, concat_axis=0, tiled=True)

    groups = [range(0, SLOTS, 2), range(1, SLOTS, 2)] if chunks == 4 else [range(SLOTS)]
    spectra, field = [], density[0]
    for group in groups:
        made = row_forward(field, wide_count, tuple(group))
        spectra += [exchange(item) for item in made]
        field, _ = lax.optimization_barrier((field, made[0]))
    columns = [item.reshape(grid_len, RADIX) for item in spectra]

    lane = jnp.arange(RADIX, dtype=jnp.int32)[None, :] % HALF
    waves = []
    for chunk in range(chunks):
        block = wide_id * chunks + chunk
        slot = block // 2
        place = (block % 2) * HALF + lane
        low = jnp.where(
            place < HALF, outer_len * place, outer_len // 2 + outer_len * (place - HALF)
        )
        index = jnp.where(slot == 0, low, slot + outer_len * place)
        signed = jnp.where(index < grid_len // 2, index, index - grid_len).astype(jnp.float32)
        waves.append(signed * (2.0 * math.pi / grid_len))

    depths = jnp.concatenate([layer_top, layer_thick])
    edge = edge_forward(
        jnp.stack([columns[0][:, 0], columns[0][:, HALF]]), layer_top[0], layer_thick[0]
    )
    edge = lax.psum(edge, "depth")
    row_share = outer_len // depth_count
    row_start = depth_id * row_share
    place = (jnp.stack([wide_id, depth_id]).astype(jnp.int32), row_start, row_share)
    sizes = (grid_len, wide_count, tile_rows)
    taps_y, offset_y = tap_weights(sample_frac[0, 0])
    taps_x, offset_x = tap_weights(sample_frac[0, 1])
    row_ids = sample_row[0][:, None] + offset_y
    col_ids = (sample_col[0][:, None] + offset_x) % grid_len
    row_ids = jnp.where(
        row_ids < 0,
        row_ids + tile_rows + 2,
        jnp.where(row_ids >= tile_rows, row_ids + 2, row_ids),
    )
    row_marks = row_ids[:, :, None] == jnp.arange(tile_rows + 8, dtype=jnp.int32)
    weight_y = jnp.sum(jnp.where(row_marks, taps_y[:, :, None], 0.0), axis=1)
    sample_count = sample_row.shape[1]
    capacity = max(2 * sample_count // wide_count, 2)
    slot_total = wide_count * capacity
    owner_ids = sample_owner[0, :, 0]
    same = owner_ids[:, None] == owner_ids[None, :]
    order = jnp.arange(sample_count, dtype=jnp.int32)
    slot_ids = jnp.sum((same & (order[None, :] < order[:, None])).astype(jnp.int32), axis=1)
    target = owner_ids * capacity + slot_ids
    placement = (target[:, None] == jnp.arange(slot_total, dtype=jnp.int32)[None, :]).astype(
        jnp.float32
    )
    pieces, blocks, partial_sums, edges = [], {}, {}, []

    def forward_job(chunk, wave, complete):
        pieces.extend(column_forward(columns[chunk], wave, depths))
        return pieces[-1]

    def edge_job(key, complete):
        edges.append(edge_inverse(key[0], row_start, row_share))
        edges.append(column_mask(key[1], taps_x, grid_len))
        return edges

    def early_job(chunk, wave, complete):
        item = column_inverse(complete(2 * chunk), 0, wave, wave, place, None, None, sizes, EVERY)
        partial_sums[chunk] = item
        return item

    def late_job(chunk, wave, complete, groups=(EVERY,)):
        part = complete(2 * chunk + 1)
        if chunk:
            wave, _ = lax.optimization_barrier((wave, blocks[0, chunk - 1][0]))
        special = edges[0] if chunk == 0 else None
        for group in groups:
            item = column_inverse(
                part, outer_len // 2, wave, wave, place, special, partial_sums[chunk], sizes, group
            )
            moved = exchange(item)
            for spot, c in enumerate(group):
                blocks[c, chunk] = (moved, spot)
            if group != groups[-1]:
                wave, _ = lax.optimization_barrier((wave, item))
        return item

    forward_job(0, waves[0], None)
    jobs = {}
    last = chunks - 1

    def plan(step, task, chunk):
        jobs.setdefault(step, []).append((functools.partial(task, chunk), waves[chunk]))

    for chunk in range(1, chunks):
        plan(chunk - 1, forward_job, chunk)
    for chunk in range(chunks):
        plan(2 * chunk + depth_count - 1, early_job, chunk)
        if chunk != last:
            plan(2 * chunk + depth_count, late_job, chunk)
    jobs.setdefault(EDGE_STEP, []).append((edge_job, (edge, col_ids)))
    complete = depth_scan(pieces, jobs, 2 * chunks)
    late_job(last, waves[last], complete, GROUPS)

    tiles = depth_count * wide_count
    forward = [(i, (i + 1) % tiles) for i in range(tiles)]
    backward = [(target, source) for source, target in forward]
    gradient, halos = None, []
    for group in GROUPS:
        ready = [[blocks[c, chunk] for chunk in range(chunks)] for c in group]
        gradient, top, bottom = row_inverse(ready, grid_len, gradient)
        used = len(group)
        gradient, bottom, top = lax.optimization_barrier(
            (gradient, bottom[:used, 6:], top[:used, :2])
        )
        low = lax.ppermute(bottom, ("depth", "wide"), forward)
        high = lax.ppermute(top, ("depth", "wide"), backward)
        halos.append(
            jnp.concatenate([low, high, jnp.zeros((used, 4, grid_len), jnp.float32)], axis=1)
        )

    outgoing = [
        interpolate(gradient, halo, group, weight_y, edges[1], placement)
        for group, halo in zip(GROUPS, halos)
    ]
    outgoing = jnp.concatenate(outgoing)
    outgoing = outgoing.reshape(FIELDS, wide_count, capacity)
    arrived = lax.all_to_all(outgoing, "wide", split_axis=1, concat_axis=1, tiled=True)
    arrived = arrived.reshape(FIELDS, 1, slot_total)
    return (gradient, jnp.concatenate([arrived, -(arrived[0:1] + arrived[3:4])]))


def solution(mesh):
    in_specs = (
        P("depth", "wide", None),
        P("depth"),
        P("depth"),
        P(("depth", "wide"), None),
        P(("depth", "wide"), None),
        P(("depth", "wide"), None, None),
        P(("depth", "wide"), None, None),
    )
    out_specs = (P(None, ("depth", "wide"), None), P(None, ("depth", "wide"), None))
    return jax.shard_map(
        per_device, mesh=mesh, in_specs=in_specs, out_specs=out_specs, check_vma=False
    )
```

```python
import functools
import math

import jax
import jax.numpy as jnp
import ml_dtypes
import numpy as np
from jax import lax
from jax.experimental import pallas as pl
from jax.experimental.pallas import tpu as pltpu
from jax.sharding import PartitionSpec as P

RADIX = 128
QLEV = 16
HALF = 64
SLOTS = 16
FIELDS = 5
GROUPS = ((0, 1, 2, 3, 4),)
EVERY = tuple(range(FIELDS))
EDGE_STEP = 2
EARLY, LATE, LAST = 2, 4, 8
HIGH = lax.Precision.HIGHEST
VMEM_LIMIT = 56 * 1024 * 1024


def np_split(table):
    high = table.astype(np.float32).astype(ml_dtypes.bfloat16)
    low = (table - high.astype(np.float64)).astype(ml_dtypes.bfloat16)
    return jnp.asarray(high), jnp.asarray(low)


def f32(table):
    return jnp.asarray(np.asarray(table, np.float32))


def angles(left, right, period):
    return (np.outer(left, right) % period) * (2.0 * math.pi / period)


def lane_order():
    column = np.arange(256)
    wave = (column // 128) * HALF + column % HALF
    return wave, (column % 128) // HALF


def slot_zero_angles(grid_len):
    wave, part = lane_order()
    outer_len = grid_len // RADIX
    upper = wave >= HALF
    freq = np.where(upper, outer_len // 2 + outer_len * (wave - HALF), outer_len * wave)
    return wave, part, upper, angles(np.arange(RADIX), freq, grid_len)


def row_forward_tables(grid_len, slots):
    outer_len = grid_len // RADIX
    stride = slots[1] - slots[0]
    theta = angles(np.asarray(slots), np.arange(outer_len), outer_len)
    first = np.zeros((2 * len(slots), outer_len))
    first[0::2] = np.cos(theta)
    first[1::2] = -np.sin(theta)
    if slots[0] == 0:
        first[1] = np.cos(np.pi * np.arange(outer_len))
    kron = np.kron(first, np.eye(8))
    wave, part = lane_order()
    step = 2.0 * math.pi * np.arange(RADIX)[:, None] / grid_len * np.ones((1, 256))
    alpha = angles(np.arange(RADIX), wave, RADIX) + slots[0] * step
    base = np.concatenate(
        [
            np.where(part == 0, np.cos(alpha), -np.sin(alpha)),
            np.where(part == 0, np.sin(alpha), np.cos(alpha)),
        ]
    )
    wave, part, upper, alpha = slot_zero_angles(grid_len)
    table = np.where(part == 0, np.cos(alpha), -np.sin(alpha))
    top = np.where(upper, 0.0, table)
    top[:, (wave == 0) & (part == 1)] = np.cos(np.pi * np.arange(RADIX))[:, None]
    zero = np.concatenate([top, np.where(upper, table, 0.0)])
    return kron, base, zero if slots[0] == 0 else base, np.cos(stride * step), np.sin(stride * step)


def row_inverse_tables(grid_len):
    outer_len = grid_len // RADIX
    theta = angles(np.arange(outer_len), np.arange(SLOTS), outer_len)
    last = np.zeros((outer_len, 2 * SLOTS))
    last[:, 0::2] = np.cos(theta)
    last[:, 1::2] = -np.sin(theta)
    last[:, 1] = np.cos(np.pi * np.arange(outer_len))
    kron = np.kron(last, np.eye(8))
    wave, part = lane_order()
    alpha = angles(wave, np.arange(RADIX), RADIX)
    real_row = (part == 0)[:, None]
    base = 2.0 * np.concatenate(
        [
            np.where(real_row, np.cos(alpha), -np.sin(alpha)),
            np.where(real_row, np.sin(alpha), np.cos(alpha)),
        ],
        axis=1,
    )
    wave, part, upper, alpha = slot_zero_angles(grid_len)
    table = 2.0 * np.where(part == 0, np.cos(alpha), -np.sin(alpha))
    left = np.where(upper, 0.0, table)
    left[:, (wave == 0) & (part == 0)] = 1.0
    left[:, (wave == 0) & (part == 1)] = np.cos(np.pi * np.arange(RADIX))[:, None]
    zero = np.concatenate([left.T, np.where(upper, table, 0.0).T], axis=1)
    beta = 2.0 * math.pi * np.arange(RADIX)[None, :] / grid_len
    return kron, base, zero, np.cos(beta), np.sin(beta)


def column_kron(outer_len, orient):
    theta = angles(np.arange(outer_len), np.arange(outer_len), outer_len)
    return np.concatenate(
        [np.kron(np.cos(theta), np.eye(8)), np.kron(orient * np.sin(theta), np.eye(8))], axis=1
    )


def split(value):
    high = value.astype(jnp.bfloat16)
    return high, (value - high.astype(jnp.float32)).astype(jnp.bfloat16)


def mm(left, right):
    return jnp.dot(left, right, preferred_element_type=jnp.float32)


def dot3(left, right):
    rows = left[0].shape[0]
    both = mm(jnp.concatenate(left, axis=0), right[0])
    return both[:rows] + both[rows:] + mm(left[0], right[1])


def rotate(value):
    lane = lax.broadcasted_iota(jnp.int32, value.shape, 1)
    return jnp.where(lane < HALF, -1.0, 1.0) * pltpu.roll(value, HALF, 1)


def row_forward_kernel(chunks, slots, x_ref, kh, kl, base, zero, cw, sw, *refs):
    outs = refs[:-4]
    th, tl, rot, u_ref = refs[-4:]
    rows = x_ref.shape[0]
    outer_len = x_ref.shape[1] // RADIX

    @pl.when(pl.program_id(0) == 0)
    def _():
        th[0], tl[0] = split(zero[...])
        rot[...] = base[...]
        for slot in range(1, len(slots)):
            top, low = rot[0:RADIX, :], rot[RADIX:, :]
            rot[0:RADIX, :] = cw[...] * top - sw[...] * low
            rot[RADIX:, :] = cw[...] * low + sw[...] * top
            th[slot], tl[slot] = split(rot[...])

    table = (kh[...], kl[...])

    def first(pair, carry):
        halves = [
            jnp.concatenate(
                [
                    x_ref[pl.ds(pair * 16 + 8 * side, 8), RADIX * a : RADIX * (a + 1)]
                    for a in range(outer_len)
                ],
                axis=0,
            )
            for side in range(2)
        ]
        u_ref[pair] = dot3(table, split(jnp.concatenate(halves, axis=1)))
        return carry

    lax.fori_loop(0, rows // 16, first, 0, unroll=min(2, rows // 16))
    for slot in range(len(slots)):
        parts = []
        for part in range(2):
            at = 16 * slot + 8 * part
            parts.append(
                jnp.concatenate(
                    [
                        u_ref[pair, at : at + 8, RADIX * side : RADIX * (side + 1)]
                        for pair in range(rows // 16)
                        for side in range(2)
                    ],
                    axis=0,
                )
            )
        result = dot3(split(jnp.concatenate(parts, axis=1)), (th[slot], tl[slot]))
        for side in range(2):
            block = 2 * slots[slot] + side
            outs[block % chunks % len(outs)][block // chunks] = result[:, RADIX * side : RADIX * (side + 1)]


def full_spec(shape):
    return pl.BlockSpec(shape, lambda *_: (0,) * len(shape))


def row_forward(field, wide_count, slots):
    rows, grid_len = field.shape
    chunks = 2 * SLOTS // wide_count
    made = min(chunks, 2) if len(slots) < SLOTS else chunks
    step = min(rows, 128)
    kron, base, zero, cw, sw = row_forward_tables(grid_len, slots)
    tables = (*np_split(kron), f32(base), f32(zero), f32(cw), f32(sw))
    return pl.pallas_call(
        functools.partial(row_forward_kernel, chunks, slots),
        grid=(rows // step,),
        in_specs=[pl.BlockSpec((step, grid_len), lambda i: (i, 0))]
        + [full_spec(item.shape) for item in tables],
        out_specs=[pl.BlockSpec((wide_count, step, RADIX), lambda i: (0, i, 0))] * made,
        out_shape=[jax.ShapeDtypeStruct((wide_count, rows, RADIX), jnp.float32)] * made,
        scratch_shapes=[
            pltpu.VMEM((len(slots), 256, 256), jnp.bfloat16),
            pltpu.VMEM((len(slots), 256, 256), jnp.bfloat16),
            pltpu.VMEM((256, 256), jnp.float32),
            pltpu.VMEM((step // 16, 16 * len(slots), 256), jnp.float32),
        ],
        compiler_params=pltpu.CompilerParams(vmem_limit_bytes=VMEM_LIMIT),
        cost_estimate=pl.CostEstimate(
            flops=20 * len(slots) // SLOTS * rows * grid_len * 256, bytes_accessed=8 * rows * grid_len, transcendentals=0
        ),
        name="row_forward",
    )(field, *tables)


def wave_y(first, shape, grid_len):
    outer_len = grid_len // RADIX
    index = first + outer_len * lax.broadcasted_iota(jnp.int32, shape, 0)
    signed = jnp.where(index < grid_len // 2, index, index - grid_len).astype(jnp.float32)
    full = signed * (2.0 * math.pi / grid_len)
    return full, jnp.where(index == grid_len // 2, 0.0, full)


def column_forward_kernel(
    grid_len, unroll, depth_ref, x_ref, kx_ref, kh, kl, ca, sa, cw, sw, low_ref, high_ref, *scratch
):
    u_ref, c_ref, s_ref = scratch
    outer_len = grid_len // RADIX
    table = (kh[...], kl[...])

    def first(pair, carry):
        halves = [
            jnp.concatenate(
                [x_ref[pl.ds(a * RADIX + pair * 16 + 8 * side, 8), :] for a in range(outer_len)],
                axis=0,
            )
            for side in range(2)
        ]
        turned = [rotate(half) for half in halves]
        data = jnp.concatenate(
            [jnp.concatenate(halves, axis=1), jnp.concatenate(turned, axis=1)], axis=0
        )
        result = dot3(table, split(data))
        for k1 in range(outer_len):
            for side in range(2):
                u_ref[pl.ds(k1 * RADIX + pair * 16 + 8 * side, 8), :] = result[
                    8 * k1 : 8 * k1 + 8, RADIX * side : RADIX * (side + 1)
                ]
        return carry

    lax.fori_loop(0, RADIX // 16, first, 0, unroll=unroll)
    c_ref[...] = ca[...]
    s_ref[...] = sa[...]
    top, thick = depth_ref[0], depth_ref[1]

    middle = outer_len // 2

    def second(out_ref, start, step, carry):
        k1 = start + step
        cosine, sine = c_ref[...], s_ref[...]
        table = split(jnp.concatenate([cosine, sine], axis=1))
        c_ref[...] = cosine * cw[...] - sine * sw[...]
        s_ref[...] = sine * cw[...] + cosine * sw[...]
        rows = pl.ds(pl.multiple_of(k1 * RADIX, RADIX), RADIX)
        data = u_ref[rows, :]
        result = dot3(table, split(jnp.concatenate([data, rotate(data)], axis=0)))
        full_y, _ = wave_y(k1, (RADIX, RADIX), grid_len)
        magnitude = jnp.sqrt(kx_ref[...] * kx_ref[...] + full_y * full_y)
        scale = (1.0 - jnp.exp(-magnitude * thick)) * jnp.exp(-magnitude * top)
        out_ref[pl.ds(pl.multiple_of(step * RADIX, RADIX), RADIX), :] = result * (
            scale * (2.0 * math.pi / (grid_len * grid_len))
        )
        return carry

    lax.fori_loop(0, middle, functools.partial(second, low_ref, 0), 0, unroll=unroll)
    lax.fori_loop(0, middle, functools.partial(second, high_ref, middle), 0, unroll=unroll)


def column_forward(block, wave_x, depths, unroll):
    grid_len = block.shape[0]
    outer_len = grid_len // RADIX
    alpha = angles(np.arange(RADIX), np.arange(RADIX), RADIX)
    beta = 2.0 * math.pi * np.arange(RADIX)[None, :] / grid_len
    tables = (
        *np_split(column_kron(outer_len, -1.0)),
        f32(np.cos(alpha)),
        f32(-np.sin(alpha)),
        f32(np.cos(beta)),
        f32(-np.sin(beta)),
    )
    square = (RADIX, RADIX)
    return pl.pallas_call(
        functools.partial(column_forward_kernel, grid_len, unroll),
        in_specs=[pl.BlockSpec(memory_space=pltpu.SMEM)]
        + [pl.BlockSpec(memory_space=pltpu.VMEM)] * (2 + len(tables)),
        out_specs=[pl.BlockSpec(memory_space=pltpu.VMEM)] * 2,
        out_shape=[jax.ShapeDtypeStruct((grid_len // 2, RADIX), jnp.float32)] * 2,
        scratch_shapes=[
            pltpu.VMEM((grid_len, RADIX), jnp.float32),
            pltpu.VMEM(square, jnp.float32),
            pltpu.VMEM(square, jnp.float32),
        ],
        compiler_params=pltpu.CompilerParams(vmem_limit_bytes=VMEM_LIMIT),
        cost_estimate=pl.CostEstimate(
            flops=100 * grid_len * RADIX * 256,
            bytes_accessed=8 * grid_len * RADIX,
            transcendentals=2 * grid_len * RADIX,
        ),
        name="column_forward",
    )(depths, block, wave_x, *tables)


def column_inverse_kernel(
    grid_len, tile_rows, unroll, start, count, special, added, keys, fields, flag_ref, kx_ref, kxo_ref, *refs
):
    keys = tuple(group for group in keys if group)
    moves = [refs[0:1]]
    at = 1
    for group in keys:
        moves.append(refs[at : at + len(group)])
        at += len(group)
    refs, (held, arrived) = refs[at:-2], refs[-2:]
    for slot, (group, sources) in enumerate(zip(((),) + keys, moves)):
        for position, source in enumerate(sources):
            fetch = pltpu.make_async_copy(source, held.at[slot], arrived.at[slot])
            if slot == 0:
                fetch.start()
            elif position == 0:
                others = [flag_ref[1] != key for key in group[1:]]
                pl.when(functools.reduce(jnp.logical_and, others, flag_ref[1] >= 0))(fetch.start)
            else:
                pl.when(flag_ref[1] == group[position])(fetch.start)
    bh, bl, ca, sa, cw, sw = refs[:6]
    edge_ref = refs[6] if special else None
    sum_ref = refs[6 + special] if added else None
    out_ref, v_ref, c_ref, s_ref = refs[6 + special + added :]
    here = bh.shape[0] // 8
    c_ref[...] = ca[...]
    s_ref[...] = sa[...]

    def first(step, carry):
        cosine, sine = c_ref[...], s_ref[...]
        table = split(jnp.concatenate([cosine, sine], axis=1))
        c_ref[...] = cosine * cw[...] - sine * sw[...]
        s_ref[...] = sine * cw[...] + cosine * sw[...]
        full_y, odd_y = wave_y(start + step, (RADIX, RADIX), grid_len)
        full_x, odd_x = kx_ref[...], kxo_ref[...]
        squared = full_x * full_x + full_y * full_y
        safe = jnp.where(squared > 0.0, squared, 1.0)
        root = lax.rsqrt(safe)
        inverse = root * root
        rows = pl.ds(pl.multiple_of(step * RADIX, RADIX), RADIX)
        value = held[0, rows, :]
        for slot in range(1, held.shape[0]):
            value = value + held[slot, rows, :]
        turned = rotate(value)
        coef_xx = -full_x * full_x * inverse
        coef_xy = -odd_x * odd_y * inverse
        coef_yy = -full_y * full_y * inverse
        slope_x = odd_x * root
        slope_y = odd_y * root
        upper = [
            value * coef_xx,
            value * coef_xy,
            turned * slope_x,
            value * coef_yy,
            turned * slope_y,
        ]
        lower = [
            turned * coef_xx,
            turned * coef_xy,
            -value * slope_x,
            turned * coef_yy,
            -value * slope_y,
        ]
        upper = jnp.concatenate([upper[c] for c in fields], axis=1)
        lower = jnp.concatenate([lower[c] for c in fields], axis=1)
        data = jnp.concatenate([upper, lower], axis=0)
        v_ref[rows, :] = dot3(table, split(data))
        return carry

    for slot, sources in enumerate(moves):
        pltpu.make_async_copy(sources[0], held.at[slot], arrived.at[slot]).wait()
    lax.fori_loop(0, count, first, 0, unroll=unroll)
    both = jnp.concatenate([bh[...], bl[...]], axis=0)
    span = 8 * here

    def second(group, carry):
        data = jnp.concatenate(
            [v_ref[pl.ds(k1 * RADIX + group * 8, 8), :] for k1 in range(count)], axis=0
        )
        turned = jnp.concatenate(
            [rotate(data[:, RADIX * c : RADIX * (c + 1)]) for c in range(len(fields))], axis=1
        )
        high, low = split(jnp.concatenate([data, turned], axis=0))
        stacked = mm(both, high)
        result = stacked[:span] + stacked[span:] + mm(bh[...], low)
        per_row = RADIX // tile_rows
        row = (group * 8) % tile_rows
        for a in range(here):
            dest = a * per_row + (group * 8) // tile_rows
            for spot, c in enumerate(fields):
                piece = result[8 * a : 8 * a + 8, RADIX * spot : RADIX * (spot + 1)]
                if added:
                    piece = piece + sum_ref[dest, c, pl.ds(row, 8), :]
                if special:
                    lane = lax.broadcasted_iota(jnp.int32, piece.shape, 1)
                    edge = edge_ref[c, pl.ds(a * RADIX + group * 8, 8), :]
                    edge = jnp.where(lane < HALF, edge[:, 0:1], edge[:, 1:2])
                    piece = jnp.where((lane % HALF == 0) & (flag_ref[0] == 0), edge, piece)
                out_ref[dest, spot, pl.ds(row, 8), :] = piece
        return carry

    lax.fori_loop(0, RADIX // 8, second, 0, unroll=unroll)


def column_inverse(part, start, wave_x, odd_x, place, edge, partial_sum, sizes, fields, unroll):
    grid_len, wide_count, tile_rows = sizes
    flag, row_start, row_share = place
    piece, below, above = part
    count = piece.shape[0] // RADIX
    moved = [piece, *below.values(), *above.values()]
    outer_len = grid_len // RADIX
    alpha = angles(np.arange(RADIX), np.arange(RADIX), RADIX)
    beta = 2.0 * math.pi * np.arange(RADIX)[:, None] / grid_len * np.ones((1, RADIX))
    alpha = alpha + start * beta
    kron = column_kron(outer_len, 1.0)
    chosen = np.arange(start * 8, (start + count) * 8)
    kron = kron[:, np.concatenate([chosen, chosen + 8 * outer_len])]
    share = [
        lax.dynamic_slice_in_dim(item, row_start * 8, row_share * 8, 0) for item in np_split(kron)
    ]
    tables = [
        *share,
        f32(np.cos(alpha)),
        f32(np.sin(alpha)),
        f32(np.cos(beta)),
        f32(np.sin(beta)),
    ]
    extra = [item for item in (edge, partial_sum) if item is not None]
    operands = [*tables, *extra]
    plain = [pl.BlockSpec(memory_space=pltpu.VMEM)]
    square = (RADIX, RADIX)
    out_shape = (wide_count, len(fields), tile_rows, RADIX)
    return pl.pallas_call(
        functools.partial(
            column_inverse_kernel,
            grid_len,
            tile_rows,
            unroll,
            start,
            count,
            int(edge is not None),
            int(partial_sum is not None),
            (tuple(below), tuple(above)),
            fields,
        ),
        in_specs=[pl.BlockSpec(memory_space=pltpu.SMEM)]
        + plain * 2
        + [pl.BlockSpec(memory_space=pl.ANY)] * len(moved)
        + plain * len(operands),
        out_specs=pl.BlockSpec(memory_space=pltpu.VMEM),
        out_shape=jax.ShapeDtypeStruct(out_shape, jnp.float32),
        scratch_shapes=[
            pltpu.VMEM((count * RADIX, len(fields) * RADIX), jnp.float32),
            pltpu.VMEM(square, jnp.float32),
            pltpu.VMEM(square, jnp.float32),
            pltpu.VMEM((3 if below else 1, count * RADIX, RADIX), jnp.float32),
            pltpu.SemaphoreType.DMA((3 if below else 1,)),
        ],
        compiler_params=pltpu.CompilerParams(vmem_limit_bytes=VMEM_LIMIT),
        cost_estimate=pl.CostEstimate(
            flops=len(fields) * 45 * count * RADIX * RADIX * 256,
            bytes_accessed=4 * (count * RADIX * RADIX + math.prod(out_shape)),
            transcendentals=count * RADIX * RADIX,
        ),
        name="column_inverse",
    )(flag, wave_x, odd_x, *moved, *operands)


def row_inverse_kernel(chunks, fields, *refs):
    ins, refs = refs[: chunks * fields], refs[chunks * fields :]
    kh, kl, base, zero, cw, sw = refs[:6]
    trace_ref = refs[6] if len(refs) == 14 else None
    out_ref, top_ref, bottom_ref, th, tl, rot, u_ref = refs[-7:]
    rows = ins[0].shape[2]
    outer_len = out_ref.shape[2] // RADIX

    @pl.when(pl.program_id(0) == 0)
    def _():
        th[0], tl[0] = split(zero[...])
        rot[...] = base[...]
        for slot in range(1, SLOTS):
            left, right = rot[:, 0:RADIX], rot[:, RADIX:]
            rot[:, 0:RADIX] = cw[...] * left - sw[...] * right
            rot[:, RADIX:] = cw[...] * right + sw[...] * left
            th[slot], tl[slot] = split(rot[...])

    for slot in range(SLOTS):
        parts = []
        for side in range(2):
            block = 2 * slot + side
            parts.append(
                jnp.concatenate(
                    [ins[c * chunks + block % chunks][block // chunks, 0] for c in range(fields)],
                    axis=0,
                )
            )
        u_ref[slot] = dot3(split(jnp.concatenate(parts, axis=1)), (th[slot], tl[slot]))

    table = (kh[...], kl[...])
    for c in range(fields):

        def second(pair, carry):
            halves = []
            for side in range(2):
                at = pl.ds(c * rows + pair * 16 + 8 * side, 8)
                halves.append(
                    jnp.concatenate(
                        [
                            u_ref[slot, at, RADIX * part : RADIX * (part + 1)]
                            for slot in range(SLOTS)
                            for part in range(2)
                        ],
                        axis=0,
                    )
                )
            result = dot3(table, split(jnp.concatenate(halves, axis=1)))
            for a in range(outer_len):
                for side in range(2):
                    out_ref[
                        c, pl.ds(pair * 16 + 8 * side, 8), RADIX * a : RADIX * (a + 1)
                    ] = result[8 * a : 8 * a + 8, RADIX * side : RADIX * (side + 1)]
            return carry

        lax.fori_loop(0, rows // 16, second, 0, unroll=min(2, rows // 16))
    if trace_ref is not None:
        out_ref[fields] = -(trace_ref[0] + out_ref[0])
    elif fields == FIELDS:
        out_ref[fields] = -(out_ref[0] + out_ref[3])

    @pl.when(pl.program_id(0) == 0)
    def _():
        top_ref[...] = out_ref[:, 0:8, :]

    @pl.when(pl.program_id(0) == pl.num_programs(0) - 1)
    def _():
        bottom_ref[...] = out_ref[:, rows - 8 : rows, :]


def row_inverse(pieces, grid_len, earlier):
    fields, chunks = len(pieces), len(pieces[0])
    wide_count, _, rows, _ = pieces[0][0][0].shape
    step = min(rows, 32 if fields == FIELDS else 64)
    made = FIELDS + 1 if fields == FIELDS else 3
    kron, base, zero, cw, sw = row_inverse_tables(grid_len)
    tables = (*np_split(kron), f32(base), f32(zero), f32(cw), f32(sw))
    specs, operands = [], []
    for per_chunk in pieces:
        for array, index in per_chunk:
            specs.append(
                pl.BlockSpec((wide_count, 1, step, RADIX), lambda i, index=index: (0, index, i, 0))
            )
            operands.append(array)
    specs += [full_spec(item.shape) for item in tables]
    operands += tables
    aliases = {}
    if earlier is not None:
        aliases = {len(operands): 0}
        specs.append(pl.BlockSpec((1, step, grid_len), lambda i: (0, i, 0)))
        operands.append(earlier)
    group = 0 if earlier is None else 1
    edge = jax.ShapeDtypeStruct((made, 8, grid_len), jnp.float32)
    return pl.pallas_call(
        functools.partial(row_inverse_kernel, chunks, fields),
        grid=(rows // step,),
        in_specs=specs,
        out_specs=[pl.BlockSpec((made, step, grid_len), lambda i: (group, i, 0))]
        + [full_spec(edge.shape)] * 2,
        out_shape=[jax.ShapeDtypeStruct((FIELDS + 1, rows, grid_len), jnp.float32), edge, edge],
        scratch_shapes=[
            pltpu.VMEM((SLOTS, 256, 256), jnp.bfloat16),
            pltpu.VMEM((SLOTS, 256, 256), jnp.bfloat16),
            pltpu.VMEM((256, 256), jnp.float32),
            pltpu.VMEM((SLOTS, fields * step, 256), jnp.float32),
        ],
        input_output_aliases=aliases,
        compiler_params=pltpu.CompilerParams(vmem_limit_bytes=VMEM_LIMIT),
        cost_estimate=pl.CostEstimate(
            flops=12 * fields * rows * grid_len * 256,
            bytes_accessed=8 * fields * rows * grid_len,
            transcendentals=0,
        ),
        name="row_inverse",
    )(*operands)


def mask_kernel(col_ref, wx_ref, mask_ref):
    samples, wide = mask_ref.shape
    lane = pl.program_id(0) * wide + lax.broadcasted_iota(jnp.int32, (samples, wide), 1)
    total = jnp.zeros((samples, wide), jnp.float32)
    for tap in range(4):
        here = lane == col_ref[:, tap : tap + 1]
        total = total + jnp.where(here, wx_ref[:, tap : tap + 1], 0.0)
    mask_ref[...] = total


def column_mask(col_ids, weight_x, grid_len):
    samples = col_ids.shape[0]
    wide = 512
    return pl.pallas_call(
        mask_kernel,
        grid=(grid_len // wide,),
        in_specs=[full_spec(col_ids.shape), full_spec(weight_x.shape)],
        out_specs=pl.BlockSpec((samples, wide), lambda i: (0, i)),
        out_shape=jax.ShapeDtypeStruct((samples, grid_len), jnp.float32),
        name="column_mask",
    )(col_ids, weight_x)


def interpolate_kernel(g_ref, halo_ref, wy_ref, mask_ref, place_ref, out_ref):
    samples, grid_len = mask_ref.shape
    wide = 512
    left = split(wy_ref[...])
    partial = jnp.zeros((samples, RADIX), jnp.float32)
    for start in range(0, grid_len, wide):
        at = slice(start, start + wide)
        data = jnp.concatenate([g_ref[0, :, at], halo_ref[0, :, at]], axis=0)
        product = dot3(left, split(data)) * mask_ref[:, at]
        for lane in range(0, wide, RADIX):
            partial = partial + product[:, lane : lane + RADIX]
    value = jnp.sum(partial, axis=1, keepdims=True)
    out_ref[0] = jnp.sum(value * place_ref[...], axis=0, keepdims=True)


def interpolate(gradient, halo, group, weight_y, mask, placement):
    _, rows, grid_len = gradient.shape
    slot_total = placement.shape[1]
    small = (weight_y, mask, placement)
    return pl.pallas_call(
        interpolate_kernel,
        grid=(len(group),),
        in_specs=[
            pl.BlockSpec((1, rows, grid_len), lambda i: (i + group[0], 0, 0)),
            pl.BlockSpec((1, 8, grid_len), lambda i: (i, 0, 0)),
        ]
        + [full_spec(item.shape) for item in small],
        out_specs=pl.BlockSpec((1, 1, slot_total), lambda i: (i, 0, 0)),
        out_shape=jax.ShapeDtypeStruct((len(group), 1, slot_total), jnp.float32),
        compiler_params=pltpu.CompilerParams(vmem_limit_bytes=VMEM_LIMIT),
        name="interpolate",
    )(gradient, halo, *small)


def product(formula, operand_a, operand_b):
    return jnp.einsum(formula, operand_a, operand_b, precision=HIGH)


def complex_product(formula, pair, table):
    return (
        product(formula, pair[0], table[0]) - product(formula, pair[1], table[1]),
        product(formula, pair[0], table[1]) + product(formula, pair[1], table[0]),
    )


def phase(row_count, col_count, period, orient):
    theta = angles(np.arange(row_count), np.arange(col_count), period)
    return f32(np.cos(theta)), f32(orient * np.sin(theta))


def times_table(pair, table):
    return (
        pair[0] * table[0] - pair[1] * table[1],
        pair[0] * table[1] + pair[1] * table[0],
    )


def edge_waves(grid_len):
    outer_len = grid_len // RADIX
    index = np.arange(outer_len)[:, None] + outer_len * np.arange(RADIX)[None, :]
    signed = np.where(index < grid_len // 2, index, index - grid_len).astype(np.float32)
    full_y = signed * np.float32(2.0 * math.pi / grid_len)
    odd_y = np.where(index == grid_len // 2, np.float32(0.0), full_y)
    return full_y, odd_y


def edge_forward(values, layer_top, layer_thick):
    grid_len = values.shape[1]
    outer_len = grid_len // RADIX
    columns = values.reshape(2, outer_len, RADIX)
    first = phase(outer_len, outer_len, outer_len, -1.0)
    pair = (product("zab,ka->zkb", columns, first[0]), product("zab,ka->zkb", columns, first[1]))
    pair = times_table(pair, phase(outer_len, RADIX, grid_len, -1.0))
    pair = complex_product("zkb,bc->zkc", pair, phase(RADIX, RADIX, RADIX, -1.0))
    full_y, _ = edge_waves(grid_len)
    magnitude = jnp.sqrt(
        jnp.asarray(np.stack([full_y * full_y, full_y * full_y + np.float32(math.pi) ** 2]))
    )
    scale = (
        2.0
        * math.pi
        / (grid_len * grid_len)
        * (1.0 - jnp.exp(-magnitude * layer_thick))
        * jnp.exp(-magnitude * layer_top)
    )
    return jnp.stack([pair[0] * scale, pair[1] * scale])


def edge_inverse(total, row_start, row_share):
    outer_len = total.shape[2]
    grid_len = outer_len * RADIX
    full_y, odd_y = edge_waves(grid_len)
    full_x = np.array([0.0, math.pi], np.float32)[:, None, None]
    squared = full_x * full_x + full_y * full_y
    safe = np.where(squared > 0.0, squared, np.float32(1.0))
    none = np.zeros_like(safe)
    plain = f32(np.stack([-full_x * full_x / safe, none, none, -full_y * full_y / safe, none]))
    turned = f32(np.stack([none, none, none, none, odd_y / np.sqrt(safe)]))
    pair = (total[0] * plain - total[1] * turned, total[1] * plain + total[0] * turned)
    pair = complex_product("fzkc,cb->fzkb", pair, phase(RADIX, RADIX, RADIX, 1.0))
    pair = times_table(pair, phase(outer_len, RADIX, grid_len, 1.0))
    last = phase(outer_len, outer_len, outer_len, 1.0)
    last = [lax.dynamic_slice_in_dim(item, row_start, row_share, 0) for item in last]
    real = product("fzkb,ak->fzab", pair[0], last[0]) - product("fzkb,ak->fzab", pair[1], last[1])
    return jnp.moveaxis(real.reshape(FIELDS, 2, row_share * RADIX), 1, 2)


def cubic_kernel(distance):
    near_part = (1.5 * distance - 2.5) * distance * distance + 1.0
    far_part = ((-0.5 * distance + 2.5) * distance - 4.0) * distance + 2.0
    return jnp.where(distance <= 1.0, near_part, jnp.where(distance < 2.0, far_part, 0.0))


def tap_weights(level):
    offset = (level.astype(jnp.float32) + 0.5) / QLEV - 0.5
    base = jnp.where(level < QLEV // 2, -1, 0).astype(jnp.int32)
    fraction = offset - base.astype(jnp.float32)
    taps = jnp.arange(4, dtype=jnp.int32)[None, :]
    weights = cubic_kernel(jnp.abs(fraction[:, None] - (taps.astype(jnp.float32) - 1.0)))
    return weights, base[:, None] - 1 + taps


def choose(which, candidates):
    picked = None
    for key, value in candidates.items():
        picked = value if picked is None else jnp.where(which == key, value, picked)
    return picked


def depth_scan(pieces, jobs, total):
    count = lax.axis_size("depth")
    here = lax.axis_index("depth")
    up = [(i, i + 1) for i in range(count - 1)]
    down = [(i + 1, i) for i in range(count - 1)]
    from_below, from_above = [], []

    def complete(index):
        below = {d: from_below[index + d - 1] for d in range(1, count)}
        above = {count - 1 - d: from_above[index + d - 1] for d in range(1, count)}
        return pieces[index], below, above

    for step in range(total + count - 2):
        live = [d for d in range(count - 1) if 0 <= step - d < total]
        rising = choose(here, {d: pieces[step - d] for d in live})
        falling = choose(here, {count - 1 - d: pieces[step - d] for d in live})
        if step:
            rising, falling = rising + from_below[-1], falling + from_above[-1]
        work = jobs.get(step, [])
        keys = [key for _, key in work]
        rising, falling, keys = lax.optimization_barrier((rising, falling, keys))
        below = lax.ppermute(rising, "depth", up)
        above = lax.ppermute(falling, "depth", down)
        results = [task(key, complete) for (task, _), key in zip(work, keys)]
        below, above, _ = lax.optimization_barrier((below, above, results))
        from_below.append(below)
        from_above.append(above)
    return complete


def per_device(density, layer_top, layer_thick, sample_row, sample_col, sample_frac, sample_owner):
    wide_count = lax.axis_size("wide")
    depth_count = lax.axis_size("depth")
    rows_here, grid_len = density.shape[1], density.shape[2]
    outer_len = grid_len // RADIX
    tile_rows = rows_here // depth_count
    chunks = 2 * SLOTS // wide_count
    wide_id, depth_id = lax.axis_index("wide"), lax.axis_index("depth")

    def exchange(block):
        return lax.all_to_all(block, "wide", split_axis=0, concat_axis=0, tiled=True)

    groups = [range(0, SLOTS, 2), range(1, SLOTS, 2)] if chunks == 4 else [range(SLOTS)]
    spectra, field = [], density[0]
    for group in groups:
        made = row_forward(field, wide_count, tuple(group))
        spectra += [exchange(item) for item in made]
        field, _ = lax.optimization_barrier((field, made[0]))
    columns = [item.reshape(grid_len, RADIX) for item in spectra]

    lane = jnp.arange(RADIX, dtype=jnp.int32)[None, :] % HALF
    waves = []
    for chunk in range(chunks):
        block = wide_id * chunks + chunk
        slot = block // 2
        place = (block % 2) * HALF + lane
        low = jnp.where(
            place < HALF, outer_len * place, outer_len // 2 + outer_len * (place - HALF)
        )
        index = jnp.where(slot == 0, low, slot + outer_len * place)
        signed = jnp.where(index < grid_len // 2, index, index - grid_len).astype(jnp.float32)
        waves.append(signed * (2.0 * math.pi / grid_len))

    depths = jnp.concatenate([layer_top, layer_thick])
    edge = edge_forward(
        jnp.stack([columns[0][:, 0], columns[0][:, HALF]]), layer_top[0], layer_thick[0]
    )
    edge = lax.psum(edge, "depth")
    row_share = outer_len // depth_count
    row_start = depth_id * row_share
    place = (jnp.stack([wide_id, depth_id]).astype(jnp.int32), row_start, row_share)
    sizes = (grid_len, wide_count, tile_rows)
    taps_y, offset_y = tap_weights(sample_frac[0, 0])
    taps_x, offset_x = tap_weights(sample_frac[0, 1])
    row_ids = sample_row[0][:, None] + offset_y
    col_ids = (sample_col[0][:, None] + offset_x) % grid_len
    row_ids = jnp.where(
        row_ids < 0,
        row_ids + tile_rows + 2,
        jnp.where(row_ids >= tile_rows, row_ids + 2, row_ids),
    )
    row_marks = row_ids[:, :, None] == jnp.arange(tile_rows + 8, dtype=jnp.int32)
    weight_y = jnp.sum(jnp.where(row_marks, taps_y[:, :, None], 0.0), axis=1)
    sample_count = sample_row.shape[1]
    capacity = max(2 * sample_count // wide_count, 2)
    slot_total = wide_count * capacity
    owner_ids = sample_owner[0, :, 0]
    same = owner_ids[:, None] == owner_ids[None, :]
    order = jnp.arange(sample_count, dtype=jnp.int32)
    slot_ids = jnp.sum((same & (order[None, :] < order[:, None])).astype(jnp.int32), axis=1)
    target = owner_ids * capacity + slot_ids
    placement = (target[:, None] == jnp.arange(slot_total, dtype=jnp.int32)[None, :]).astype(
        jnp.float32
    )
    pieces, blocks, partial_sums, edges = [], {}, {}, []

    def forward_job(chunk, wave, complete):
        pieces.extend(column_forward(columns[chunk], wave, depths, 2 if chunk else 4))
        return pieces[-1]

    def edge_job(key, complete):
        edges.append(edge_inverse(key[0], row_start, row_share))
        edges.append(column_mask(key[1], taps_x, grid_len))
        return edges

    def early_job(chunk, wave, complete):
        item = column_inverse(complete(2 * chunk), 0, wave, wave, place, None, None, sizes, EVERY, EARLY)
        partial_sums[chunk] = item
        return item

    def late_job(chunk, wave, complete, groups=(EVERY,)):
        part = complete(2 * chunk + 1)
        if chunk:
            wave, _ = lax.optimization_barrier((wave, blocks[0, chunk - 1][0]))
        special = edges[0] if chunk == 0 else None
        for group in groups:
            item = column_inverse(
                part,
                outer_len // 2,
                wave,
                wave,
                place,
                special,
                partial_sums[chunk],
                sizes,
                group,
                LAST if chunk == last else LATE,
            )
            moved = exchange(item)
            for spot, c in enumerate(group):
                blocks[c, chunk] = (moved, spot)
            if group != groups[-1]:
                wave, _ = lax.optimization_barrier((wave, item))
        return item

    forward_job(0, waves[0], None)
    jobs = {}
    last = chunks - 1

    def plan(step, task, chunk):
        jobs.setdefault(step, []).append((functools.partial(task, chunk), waves[chunk]))

    for chunk in range(1, chunks):
        plan(chunk - 1, forward_job, chunk)
    for chunk in range(chunks):
        plan(2 * chunk + depth_count - 1, early_job, chunk)
        if chunk != last:
            plan(2 * chunk + depth_count, late_job, chunk)
    jobs.setdefault(EDGE_STEP, []).append((edge_job, (edge, col_ids)))
    complete = depth_scan(pieces, jobs, 2 * chunks)
    late_job(last, waves[last], complete, GROUPS)

    tiles = depth_count * wide_count
    forward = [(i, (i + 1) % tiles) for i in range(tiles)]
    backward = [(target, source) for source, target in forward]
    gradient, halos = None, []
    for group in GROUPS:
        ready = [[blocks[c, chunk] for chunk in range(chunks)] for c in group]
        gradient, top, bottom = row_inverse(ready, grid_len, gradient)
        used = len(group)
        gradient, bottom, top = lax.optimization_barrier(
            (gradient, bottom[:used, 6:], top[:used, :2])
        )
        low = lax.ppermute(bottom, ("depth", "wide"), forward)
        high = lax.ppermute(top, ("depth", "wide"), backward)
        halos.append(
            jnp.concatenate([low, high, jnp.zeros((used, 4, grid_len), jnp.float32)], axis=1)
        )

    outgoing = [
        interpolate(gradient, halo, group, weight_y, edges[1], placement)
        for group, halo in zip(GROUPS, halos)
    ]
    outgoing = jnp.concatenate(outgoing)
    outgoing = outgoing.reshape(FIELDS, wide_count, capacity)
    arrived = lax.all_to_all(outgoing, "wide", split_axis=1, concat_axis=1, tiled=True)
    arrived = arrived.reshape(FIELDS, 1, slot_total)
    return (gradient, jnp.concatenate([arrived, -(arrived[0:1] + arrived[3:4])]))


def solution(mesh):
    in_specs = (
        P("depth", "wide", None),
        P("depth"),
        P("depth"),
        P(("depth", "wide"), None),
        P(("depth", "wide"), None),
        P(("depth", "wide"), None, None),
        P(("depth", "wide"), None, None),
    )
    out_specs = (P(None, ("depth", "wide"), None), P(None, ("depth", "wide"), None))
    return jax.shard_map(
        per_device, mesh=mesh, in_specs=in_specs, out_specs=out_specs, check_vma=False
    )
```

```python
import functools
import math

import jax
import jax.numpy as jnp
import ml_dtypes
import numpy as np
from jax import lax
from jax.experimental import pallas as pl
from jax.experimental.pallas import tpu as pltpu
from jax.sharding import PartitionSpec as P

RADIX = 128
QLEV = 16
HALF = 64
SLOTS = 16
FIELDS = 5
GROUPS = ((0, 1, 2, 3, 4),)
EVERY = tuple(range(FIELDS))
EDGE_STEP = 2
HIGH = lax.Precision.HIGHEST
VMEM_LIMIT = 56 * 1024 * 1024


def np_split(table):
    high = table.astype(np.float32).astype(ml_dtypes.bfloat16)
    low = (table - high.astype(np.float64)).astype(ml_dtypes.bfloat16)
    return jnp.asarray(high), jnp.asarray(low)


def f32(table):
    return jnp.asarray(np.asarray(table, np.float32))


def angles(left, right, period):
    return (np.outer(left, right) % period) * (2.0 * math.pi / period)


def lane_order():
    column = np.arange(256)
    wave = (column // 128) * HALF + column % HALF
    return wave, (column % 128) // HALF


def slot_zero_angles(grid_len):
    wave, part = lane_order()
    outer_len = grid_len // RADIX
    upper = wave >= HALF
    freq = np.where(upper, outer_len // 2 + outer_len * (wave - HALF), outer_len * wave)
    return wave, part, upper, angles(np.arange(RADIX), freq, grid_len)


def row_forward_tables(grid_len, slots):
    outer_len = grid_len // RADIX
    stride = slots[1] - slots[0]
    theta = angles(np.asarray(slots), np.arange(outer_len), outer_len)
    first = np.zeros((2 * len(slots), outer_len))
    first[0::2] = np.cos(theta)
    first[1::2] = -np.sin(theta)
    if slots[0] == 0:
        first[1] = np.cos(np.pi * np.arange(outer_len))
    kron = np.kron(first, np.eye(8))
    wave, part = lane_order()
    step = 2.0 * math.pi * np.arange(RADIX)[:, None] / grid_len * np.ones((1, 256))
    alpha = angles(np.arange(RADIX), wave, RADIX) + slots[0] * step
    base = np.concatenate(
        [
            np.where(part == 0, np.cos(alpha), -np.sin(alpha)),
            np.where(part == 0, np.sin(alpha), np.cos(alpha)),
        ]
    )
    wave, part, upper, alpha = slot_zero_angles(grid_len)
    table = np.where(part == 0, np.cos(alpha), -np.sin(alpha))
    top = np.where(upper, 0.0, table)
    top[:, (wave == 0) & (part == 1)] = np.cos(np.pi * np.arange(RADIX))[:, None]
    zero = np.concatenate([top, np.where(upper, table, 0.0)])
    return kron, base, zero if slots[0] == 0 else base, np.cos(stride * step), np.sin(stride * step)


def row_inverse_tables(grid_len):
    outer_len = grid_len // RADIX
    theta = angles(np.arange(outer_len), np.arange(SLOTS), outer_len)
    last = np.zeros((outer_len, 2 * SLOTS))
    last[:, 0::2] = np.cos(theta)
    last[:, 1::2] = -np.sin(theta)
    last[:, 1] = np.cos(np.pi * np.arange(outer_len))
    kron = np.kron(last, np.eye(8))
    wave, part = lane_order()
    alpha = angles(wave, np.arange(RADIX), RADIX)
    real_row = (part == 0)[:, None]
    base = 2.0 * np.concatenate(
        [
            np.where(real_row, np.cos(alpha), -np.sin(alpha)),
            np.where(real_row, np.sin(alpha), np.cos(alpha)),
        ],
        axis=1,
    )
    wave, part, upper, alpha = slot_zero_angles(grid_len)
    table = 2.0 * np.where(part == 0, np.cos(alpha), -np.sin(alpha))
    left = np.where(upper, 0.0, table)
    left[:, (wave == 0) & (part == 0)] = 1.0
    left[:, (wave == 0) & (part == 1)] = np.cos(np.pi * np.arange(RADIX))[:, None]
    zero = np.concatenate([left.T, np.where(upper, table, 0.0).T], axis=1)
    beta = 2.0 * math.pi * np.arange(RADIX)[None, :] / grid_len
    return kron, base, zero, np.cos(beta), np.sin(beta)


def column_kron(outer_len, orient):
    theta = angles(np.arange(outer_len), np.arange(outer_len), outer_len)
    return np.concatenate(
        [np.kron(np.cos(theta), np.eye(8)), np.kron(orient * np.sin(theta), np.eye(8))], axis=1
    )


def split(value):
    high = value.astype(jnp.bfloat16)
    return high, (value - high.astype(jnp.float32)).astype(jnp.bfloat16)


def mm(left, right):
    return jnp.dot(left, right, preferred_element_type=jnp.float32)


def dot3(left, right):
    rows = left[0].shape[0]
    both = mm(jnp.concatenate(left, axis=0), right[0])
    return both[:rows] + both[rows:] + mm(left[0], right[1])


def rotate(value):
    lane = lax.broadcasted_iota(jnp.int32, value.shape, 1)
    return jnp.where(lane < HALF, -1.0, 1.0) * pltpu.roll(value, HALF, 1)


def row_forward_kernel(chunks, slots, x_ref, kh, kl, base, zero, cw, sw, *refs):
    outs = refs[:-4]
    th, tl, rot, u_ref = refs[-4:]
    rows = x_ref.shape[0]
    outer_len = x_ref.shape[1] // RADIX

    @pl.when(pl.program_id(0) == 0)
    def _():
        th[0], tl[0] = split(zero[...])
        rot[...] = base[...]
        for slot in range(1, len(slots)):
            top, low = rot[0:RADIX, :], rot[RADIX:, :]
            rot[0:RADIX, :] = cw[...] * top - sw[...] * low
            rot[RADIX:, :] = cw[...] * low + sw[...] * top
            th[slot], tl[slot] = split(rot[...])

    table = (kh[...], kl[...])

    def first(pair, carry):
        halves = [
            jnp.concatenate(
                [
                    x_ref[pl.ds(pair * 16 + 8 * side, 8), RADIX * a : RADIX * (a + 1)]
                    for a in range(outer_len)
                ],
                axis=0,
            )
            for side in range(2)
        ]
        u_ref[pair] = dot3(table, split(jnp.concatenate(halves, axis=1)))
        return carry

    lax.fori_loop(0, rows // 16, first, 0, unroll=min(2, rows // 16))
    for slot in range(len(slots)):
        parts = []
        for part in range(2):
            at = 16 * slot + 8 * part
            parts.append(
                jnp.concatenate(
                    [
                        u_ref[pair, at : at + 8, RADIX * side : RADIX * (side + 1)]
                        for pair in range(rows // 16)
                        for side in range(2)
                    ],
                    axis=0,
                )
            )
        result = dot3(split(jnp.concatenate(parts, axis=1)), (th[slot], tl[slot]))
        for side in range(2):
            block = 2 * slots[slot] + side
            outs[block % chunks % len(outs)][block // chunks] = result[:, RADIX * side : RADIX * (side + 1)]


def full_spec(shape):
    return pl.BlockSpec(shape, lambda *_: (0,) * len(shape))


def row_forward(field, wide_count, slots):
    rows, grid_len = field.shape
    chunks = 2 * SLOTS // wide_count
    made = min(chunks, 2) if len(slots) < SLOTS else chunks
    step = min(rows, 128)
    kron, base, zero, cw, sw = row_forward_tables(grid_len, slots)
    tables = (*np_split(kron), f32(base), f32(zero), f32(cw), f32(sw))
    return pl.pallas_call(
        functools.partial(row_forward_kernel, chunks, slots),
        grid=(rows // step,),
        in_specs=[pl.BlockSpec((step, grid_len), lambda i: (i, 0))]
        + [full_spec(item.shape) for item in tables],
        out_specs=[pl.BlockSpec((wide_count, step, RADIX), lambda i: (0, i, 0))] * made,
        out_shape=[jax.ShapeDtypeStruct((wide_count, rows, RADIX), jnp.float32)] * made,
        scratch_shapes=[
            pltpu.VMEM((len(slots), 256, 256), jnp.bfloat16),
            pltpu.VMEM((len(slots), 256, 256), jnp.bfloat16),
            pltpu.VMEM((256, 256), jnp.float32),
            pltpu.VMEM((step // 16, 16 * len(slots), 256), jnp.float32),
        ],
        compiler_params=pltpu.CompilerParams(vmem_limit_bytes=VMEM_LIMIT),
        cost_estimate=pl.CostEstimate(
            flops=20 * len(slots) // SLOTS * rows * grid_len * 256, bytes_accessed=8 * rows * grid_len, transcendentals=0
        ),
        name="row_forward",
    )(field, *tables)


def wave_y(first, shape, grid_len):
    outer_len = grid_len // RADIX
    index = first + outer_len * lax.broadcasted_iota(jnp.int32, shape, 0)
    signed = jnp.where(index < grid_len // 2, index, index - grid_len).astype(jnp.float32)
    full = signed * (2.0 * math.pi / grid_len)
    return full, jnp.where(index == grid_len // 2, 0.0, full)


def column_forward_kernel(
    grid_len, depth_ref, x_ref, kx_ref, kh, kl, ca, sa, cw, sw, low_ref, high_ref, *scratch
):
    u_ref, c_ref, s_ref = scratch
    outer_len = grid_len // RADIX
    table = (kh[...], kl[...])

    def first(pair, carry):
        halves = [
            jnp.concatenate(
                [x_ref[pl.ds(a * RADIX + pair * 16 + 8 * side, 8), :] for a in range(outer_len)],
                axis=0,
            )
            for side in range(2)
        ]
        turned = [rotate(half) for half in halves]
        data = jnp.concatenate(
            [jnp.concatenate(halves, axis=1), jnp.concatenate(turned, axis=1)], axis=0
        )
        result = dot3(table, split(data))
        for k1 in range(outer_len):
            for side in range(2):
                u_ref[pl.ds(k1 * RADIX + pair * 16 + 8 * side, 8), :] = result[
                    8 * k1 : 8 * k1 + 8, RADIX * side : RADIX * (side + 1)
                ]
        return carry

    lax.fori_loop(0, RADIX // 16, first, 0, unroll=4)
    c_ref[...] = ca[...]
    s_ref[...] = sa[...]
    top, thick = depth_ref[0], depth_ref[1]

    middle = outer_len // 2

    def second(out_ref, start, step, carry):
        k1 = start + step
        cosine, sine = c_ref[...], s_ref[...]
        table = split(jnp.concatenate([cosine, sine], axis=1))
        c_ref[...] = cosine * cw[...] - sine * sw[...]
        s_ref[...] = sine * cw[...] + cosine * sw[...]
        rows = pl.ds(pl.multiple_of(k1 * RADIX, RADIX), RADIX)
        data = u_ref[rows, :]
        result = dot3(table, split(jnp.concatenate([data, rotate(data)], axis=0)))
        full_y, _ = wave_y(k1, (RADIX, RADIX), grid_len)
        magnitude = jnp.sqrt(kx_ref[...] * kx_ref[...] + full_y * full_y)
        scale = (1.0 - jnp.exp(-magnitude * thick)) * jnp.exp(-magnitude * top)
        out_ref[pl.ds(pl.multiple_of(step * RADIX, RADIX), RADIX), :] = result * (
            scale * (2.0 * math.pi / (grid_len * grid_len))
        )
        return carry

    lax.fori_loop(0, middle, functools.partial(second, low_ref, 0), 0, unroll=4)
    lax.fori_loop(0, middle, functools.partial(second, high_ref, middle), 0, unroll=4)


def column_forward(block, wave_x, depths):
    grid_len = block.shape[0]
    outer_len = grid_len // RADIX
    alpha = angles(np.arange(RADIX), np.arange(RADIX), RADIX)
    beta = 2.0 * math.pi * np.arange(RADIX)[None, :] / grid_len
    tables = (
        *np_split(column_kron(outer_len, -1.0)),
        f32(np.cos(alpha)),
        f32(-np.sin(alpha)),
        f32(np.cos(beta)),
        f32(-np.sin(beta)),
    )
    square = (RADIX, RADIX)
    return pl.pallas_call(
        functools.partial(column_forward_kernel, grid_len),
        in_specs=[pl.BlockSpec(memory_space=pltpu.SMEM)]
        + [pl.BlockSpec(memory_space=pltpu.VMEM)] * (2 + len(tables)),
        out_specs=[pl.BlockSpec(memory_space=pltpu.VMEM)] * 2,
        out_shape=[jax.ShapeDtypeStruct((grid_len // 2, RADIX), jnp.float32)] * 2,
        scratch_shapes=[
            pltpu.VMEM((grid_len, RADIX), jnp.float32),
            pltpu.VMEM(square, jnp.float32),
            pltpu.VMEM(square, jnp.float32),
        ],
        compiler_params=pltpu.CompilerParams(vmem_limit_bytes=VMEM_LIMIT),
        cost_estimate=pl.CostEstimate(
            flops=100 * grid_len * RADIX * 256,
            bytes_accessed=8 * grid_len * RADIX,
            transcendentals=2 * grid_len * RADIX,
        ),
        name="column_forward",
    )(depths, block, wave_x, *tables)


def column_inverse_kernel(
    grid_len, tile_rows, start, count, special, added, keys, fields, flag_ref, kx_ref, kxo_ref, *refs
):
    keys = tuple(group for group in keys if group)
    moves = [refs[0:1]]
    at = 1
    for group in keys:
        moves.append(refs[at : at + len(group)])
        at += len(group)
    refs, (held, arrived) = refs[at:-2], refs[-2:]
    for slot, (group, sources) in enumerate(zip(((),) + keys, moves)):
        for position, source in enumerate(sources):
            fetch = pltpu.make_async_copy(source, held.at[slot], arrived.at[slot])
            if slot == 0:
                fetch.start()
            elif position == 0:
                others = [flag_ref[1] != key for key in group[1:]]
                pl.when(functools.reduce(jnp.logical_and, others, flag_ref[1] >= 0))(fetch.start)
            else:
                pl.when(flag_ref[1] == group[position])(fetch.start)
    bh, bl, ca, sa, cw, sw = refs[:6]
    edge_ref = refs[6] if special else None
    sum_ref = refs[6 + special] if added else None
    out_ref, v_ref, c_ref, s_ref = refs[6 + special + added :]
    here = bh.shape[0] // 8
    c_ref[...] = ca[...]
    s_ref[...] = sa[...]

    def first(step, carry):
        cosine, sine = c_ref[...], s_ref[...]
        table = split(jnp.concatenate([cosine, sine], axis=1))
        c_ref[...] = cosine * cw[...] - sine * sw[...]
        s_ref[...] = sine * cw[...] + cosine * sw[...]
        full_y, odd_y = wave_y(start + step, (RADIX, RADIX), grid_len)
        full_x, odd_x = kx_ref[...], kxo_ref[...]
        squared = full_x * full_x + full_y * full_y
        safe = jnp.where(squared > 0.0, squared, 1.0)
        root = lax.rsqrt(safe)
        inverse = root * root
        rows = pl.ds(pl.multiple_of(step * RADIX, RADIX), RADIX)
        value = held[0, rows, :]
        for slot in range(1, held.shape[0]):
            value = value + held[slot, rows, :]
        turned = rotate(value)
        coef_xx = -full_x * full_x * inverse
        coef_xy = -odd_x * odd_y * inverse
        coef_yy = -full_y * full_y * inverse
        slope_x = odd_x * root
        slope_y = odd_y * root
        upper = [
            value * coef_xx,
            value * coef_xy,
            turned * slope_x,
            value * coef_yy,
            turned * slope_y,
        ]
        lower = [
            turned * coef_xx,
            turned * coef_xy,
            -value * slope_x,
            turned * coef_yy,
            -value * slope_y,
        ]
        upper = jnp.concatenate([upper[c] for c in fields], axis=1)
        lower = jnp.concatenate([lower[c] for c in fields], axis=1)
        data = jnp.concatenate([upper, lower], axis=0)
        v_ref[rows, :] = dot3(table, split(data))
        return carry

    for slot, sources in enumerate(moves):
        pltpu.make_async_copy(sources[0], held.at[slot], arrived.at[slot]).wait()
    lax.fori_loop(0, count, first, 0, unroll=8)
    both = jnp.concatenate([bh[...], bl[...]], axis=0)
    span = 8 * here

    def second(group, carry):
        data = jnp.concatenate(
            [v_ref[pl.ds(k1 * RADIX + group * 8, 8), :] for k1 in range(count)], axis=0
        )
        turned = jnp.concatenate(
            [rotate(data[:, RADIX * c : RADIX * (c + 1)]) for c in range(len(fields))], axis=1
        )
        high, low = split(jnp.concatenate([data, turned], axis=0))
        stacked = mm(both, high)
        result = stacked[:span] + stacked[span:] + mm(bh[...], low)
        per_row = RADIX // tile_rows
        row = (group * 8) % tile_rows
        for a in range(here):
            dest = a * per_row + (group * 8) // tile_rows
            for spot, c in enumerate(fields):
                piece = result[8 * a : 8 * a + 8, RADIX * spot : RADIX * (spot + 1)]
                if added:
                    piece = piece + sum_ref[dest, c, pl.ds(row, 8), :]
                if special:
                    lane = lax.broadcasted_iota(jnp.int32, piece.shape, 1)
                    edge = edge_ref[c, pl.ds(a * RADIX + group * 8, 8), :]
                    edge = jnp.where(lane < HALF, edge[:, 0:1], edge[:, 1:2])
                    piece = jnp.where((lane % HALF == 0) & (flag_ref[0] == 0), edge, piece)
                out_ref[dest, spot, pl.ds(row, 8), :] = piece
        return carry

    lax.fori_loop(0, RADIX // 8, second, 0, unroll=8)


def column_inverse(part, start, wave_x, odd_x, place, edge, partial_sum, sizes, fields):
    grid_len, wide_count, tile_rows = sizes
    flag, row_start, row_share = place
    piece, below, above = part
    count = piece.shape[0] // RADIX
    moved = [piece, *below.values(), *above.values()]
    outer_len = grid_len // RADIX
    alpha = angles(np.arange(RADIX), np.arange(RADIX), RADIX)
    beta = 2.0 * math.pi * np.arange(RADIX)[:, None] / grid_len * np.ones((1, RADIX))
    alpha = alpha + start * beta
    kron = column_kron(outer_len, 1.0)
    chosen = np.arange(start * 8, (start + count) * 8)
    kron = kron[:, np.concatenate([chosen, chosen + 8 * outer_len])]
    share = [
        lax.dynamic_slice_in_dim(item, row_start * 8, row_share * 8, 0) for item in np_split(kron)
    ]
    tables = [
        *share,
        f32(np.cos(alpha)),
        f32(np.sin(alpha)),
        f32(np.cos(beta)),
        f32(np.sin(beta)),
    ]
    extra = [item for item in (edge, partial_sum) if item is not None]
    operands = [*tables, *extra]
    plain = [pl.BlockSpec(memory_space=pltpu.VMEM)]
    square = (RADIX, RADIX)
    out_shape = (wide_count, len(fields), tile_rows, RADIX)
    return pl.pallas_call(
        functools.partial(
            column_inverse_kernel,
            grid_len,
            tile_rows,
            start,
            count,
            int(edge is not None),
            int(partial_sum is not None),
            (tuple(below), tuple(above)),
            fields,
        ),
        in_specs=[pl.BlockSpec(memory_space=pltpu.SMEM)]
        + plain * 2
        + [pl.BlockSpec(memory_space=pl.ANY)] * len(moved)
        + plain * len(operands),
        out_specs=pl.BlockSpec(memory_space=pltpu.VMEM),
        out_shape=jax.ShapeDtypeStruct(out_shape, jnp.float32),
        scratch_shapes=[
            pltpu.VMEM((count * RADIX, len(fields) * RADIX), jnp.float32),
            pltpu.VMEM(square, jnp.float32),
            pltpu.VMEM(square, jnp.float32),
            pltpu.VMEM((3 if below else 1, count * RADIX, RADIX), jnp.float32),
            pltpu.SemaphoreType.DMA((3 if below else 1,)),
        ],
        compiler_params=pltpu.CompilerParams(vmem_limit_bytes=VMEM_LIMIT),
        cost_estimate=pl.CostEstimate(
            flops=len(fields) * 45 * count * RADIX * RADIX * 256,
            bytes_accessed=4 * (count * RADIX * RADIX + math.prod(out_shape)),
            transcendentals=count * RADIX * RADIX,
        ),
        name="column_inverse",
    )(flag, wave_x, odd_x, *moved, *operands)


def row_inverse_kernel(chunks, fields, *refs):
    ins, refs = refs[: chunks * fields], refs[chunks * fields :]
    kh, kl, base, zero, cw, sw = refs[:6]
    trace_ref = refs[6] if len(refs) == 14 else None
    out_ref, top_ref, bottom_ref, th, tl, rot, u_ref = refs[-7:]
    rows = ins[0].shape[2]
    outer_len = out_ref.shape[2] // RADIX

    @pl.when(pl.program_id(0) == 0)
    def _():
        th[0], tl[0] = split(zero[...])
        rot[...] = base[...]
        for slot in range(1, SLOTS):
            left, right = rot[:, 0:RADIX], rot[:, RADIX:]
            rot[:, 0:RADIX] = cw[...] * left - sw[...] * right
            rot[:, RADIX:] = cw[...] * right + sw[...] * left
            th[slot], tl[slot] = split(rot[...])

    for slot in range(SLOTS):
        parts = []
        for side in range(2):
            block = 2 * slot + side
            parts.append(
                jnp.concatenate(
                    [ins[c * chunks + block % chunks][block // chunks, 0] for c in range(fields)],
                    axis=0,
                )
            )
        u_ref[slot] = dot3(split(jnp.concatenate(parts, axis=1)), (th[slot], tl[slot]))

    table = (kh[...], kl[...])
    for c in range(fields):

        def second(pair, carry):
            halves = []
            for side in range(2):
                at = pl.ds(c * rows + pair * 16 + 8 * side, 8)
                halves.append(
                    jnp.concatenate(
                        [
                            u_ref[slot, at, RADIX * part : RADIX * (part + 1)]
                            for slot in range(SLOTS)
                            for part in range(2)
                        ],
                        axis=0,
                    )
                )
            result = dot3(table, split(jnp.concatenate(halves, axis=1)))
            for a in range(outer_len):
                for side in range(2):
                    out_ref[
                        c, pl.ds(pair * 16 + 8 * side, 8), RADIX * a : RADIX * (a + 1)
                    ] = result[8 * a : 8 * a + 8, RADIX * side : RADIX * (side + 1)]
            return carry

        lax.fori_loop(0, rows // 16, second, 0, unroll=min(4, rows // 16))
    if trace_ref is not None:
        out_ref[fields] = -(trace_ref[0] + out_ref[0])
    elif fields == FIELDS:
        out_ref[fields] = -(out_ref[0] + out_ref[3])

    @pl.when(pl.program_id(0) == 0)
    def _():
        top_ref[...] = out_ref[:, 0:8, :]

    @pl.when(pl.program_id(0) == pl.num_programs(0) - 1)
    def _():
        bottom_ref[...] = out_ref[:, rows - 8 : rows, :]


def row_inverse(pieces, grid_len, earlier):
    fields, chunks = len(pieces), len(pieces[0])
    wide_count, _, rows, _ = pieces[0][0][0].shape
    step = min(rows, 64)
    made = FIELDS + 1 if fields == FIELDS else 3
    kron, base, zero, cw, sw = row_inverse_tables(grid_len)
    tables = (*np_split(kron), f32(base), f32(zero), f32(cw), f32(sw))
    specs, operands = [], []
    for per_chunk in pieces:
        for array, index in per_chunk:
            specs.append(
                pl.BlockSpec((wide_count, 1, step, RADIX), lambda i, index=index: (0, index, i, 0))
            )
            operands.append(array)
    specs += [full_spec(item.shape) for item in tables]
    operands += tables
    aliases = {}
    if earlier is not None:
        aliases = {len(operands): 0}
        specs.append(pl.BlockSpec((1, step, grid_len), lambda i: (0, i, 0)))
        operands.append(earlier)
    group = 0 if earlier is None else 1
    edge = jax.ShapeDtypeStruct((made, 8, grid_len), jnp.float32)
    return pl.pallas_call(
        functools.partial(row_inverse_kernel, chunks, fields),
        grid=(rows // step,),
        in_specs=specs,
        out_specs=[pl.BlockSpec((made, step, grid_len), lambda i: (group, i, 0))]
        + [full_spec(edge.shape)] * 2,
        out_shape=[jax.ShapeDtypeStruct((FIELDS + 1, rows, grid_len), jnp.float32), edge, edge],
        scratch_shapes=[
            pltpu.VMEM((SLOTS, 256, 256), jnp.bfloat16),
            pltpu.VMEM((SLOTS, 256, 256), jnp.bfloat16),
            pltpu.VMEM((256, 256), jnp.float32),
            pltpu.VMEM((SLOTS, fields * step, 256), jnp.float32),
        ],
        input_output_aliases=aliases,
        compiler_params=pltpu.CompilerParams(vmem_limit_bytes=VMEM_LIMIT),
        cost_estimate=pl.CostEstimate(
            flops=12 * fields * rows * grid_len * 256,
            bytes_accessed=8 * fields * rows * grid_len,
            transcendentals=0,
        ),
        name="row_inverse",
    )(*operands)


def mask_kernel(col_ref, wx_ref, mask_ref):
    samples, wide = mask_ref.shape
    lane = pl.program_id(0) * wide + lax.broadcasted_iota(jnp.int32, (samples, wide), 1)
    total = jnp.zeros((samples, wide), jnp.float32)
    for tap in range(4):
        here = lane == col_ref[:, tap : tap + 1]
        total = total + jnp.where(here, wx_ref[:, tap : tap + 1], 0.0)
    mask_ref[...] = total


def column_mask(col_ids, weight_x, grid_len):
    samples = col_ids.shape[0]
    wide = 512
    return pl.pallas_call(
        mask_kernel,
        grid=(grid_len // wide,),
        in_specs=[full_spec(col_ids.shape), full_spec(weight_x.shape)],
        out_specs=pl.BlockSpec((samples, wide), lambda i: (0, i)),
        out_shape=jax.ShapeDtypeStruct((samples, grid_len), jnp.float32),
        name="column_mask",
    )(col_ids, weight_x)


def interpolate_kernel(g_ref, halo_ref, wy_ref, mask_ref, place_ref, out_ref):
    samples, grid_len = mask_ref.shape
    wide = 512
    left = split(wy_ref[...])
    partial = jnp.zeros((samples, RADIX), jnp.float32)
    for start in range(0, grid_len, wide):
        at = slice(start, start + wide)
        data = jnp.concatenate([g_ref[0, :, at], halo_ref[0, :, at]], axis=0)
        product = dot3(left, split(data)) * mask_ref[:, at]
        for lane in range(0, wide, RADIX):
            partial = partial + product[:, lane : lane + RADIX]
    value = jnp.sum(partial, axis=1, keepdims=True)
    out_ref[0] = jnp.sum(value * place_ref[...], axis=0, keepdims=True)


def interpolate(gradient, halo, group, weight_y, mask, placement):
    _, rows, grid_len = gradient.shape
    slot_total = placement.shape[1]
    small = (weight_y, mask, placement)
    return pl.pallas_call(
        interpolate_kernel,
        grid=(len(group),),
        in_specs=[
            pl.BlockSpec((1, rows, grid_len), lambda i: (i + group[0], 0, 0)),
            pl.BlockSpec((1, 8, grid_len), lambda i: (i, 0, 0)),
        ]
        + [full_spec(item.shape) for item in small],
        out_specs=pl.BlockSpec((1, 1, slot_total), lambda i: (i, 0, 0)),
        out_shape=jax.ShapeDtypeStruct((len(group), 1, slot_total), jnp.float32),
        compiler_params=pltpu.CompilerParams(vmem_limit_bytes=VMEM_LIMIT),
        name="interpolate",
    )(gradient, halo, *small)


def product(formula, operand_a, operand_b):
    return jnp.einsum(formula, operand_a, operand_b, precision=HIGH)


def complex_product(formula, pair, table):
    return (
        product(formula, pair[0], table[0]) - product(formula, pair[1], table[1]),
        product(formula, pair[0], table[1]) + product(formula, pair[1], table[0]),
    )


def phase(row_count, col_count, period, orient):
    theta = angles(np.arange(row_count), np.arange(col_count), period)
    return f32(np.cos(theta)), f32(orient * np.sin(theta))


def times_table(pair, table):
    return (
        pair[0] * table[0] - pair[1] * table[1],
        pair[0] * table[1] + pair[1] * table[0],
    )


def edge_waves(grid_len):
    outer_len = grid_len // RADIX
    index = np.arange(outer_len)[:, None] + outer_len * np.arange(RADIX)[None, :]
    signed = np.where(index < grid_len // 2, index, index - grid_len).astype(np.float32)
    full_y = signed * np.float32(2.0 * math.pi / grid_len)
    odd_y = np.where(index == grid_len // 2, np.float32(0.0), full_y)
    return full_y, odd_y


def edge_forward(values, layer_top, layer_thick):
    grid_len = values.shape[1]
    outer_len = grid_len // RADIX
    columns = values.reshape(2, outer_len, RADIX)
    first = phase(outer_len, outer_len, outer_len, -1.0)
    pair = (product("zab,ka->zkb", columns, first[0]), product("zab,ka->zkb", columns, first[1]))
    pair = times_table(pair, phase(outer_len, RADIX, grid_len, -1.0))
    pair = complex_product("zkb,bc->zkc", pair, phase(RADIX, RADIX, RADIX, -1.0))
    full_y, _ = edge_waves(grid_len)
    magnitude = jnp.sqrt(
        jnp.asarray(np.stack([full_y * full_y, full_y * full_y + np.float32(math.pi) ** 2]))
    )
    scale = (
        2.0
        * math.pi
        / (grid_len * grid_len)
        * (1.0 - jnp.exp(-magnitude * layer_thick))
        * jnp.exp(-magnitude * layer_top)
    )
    return jnp.stack([pair[0] * scale, pair[1] * scale])


def edge_inverse(total, row_start, row_share):
    outer_len = total.shape[2]
    grid_len = outer_len * RADIX
    full_y, odd_y = edge_waves(grid_len)
    full_x = np.array([0.0, math.pi], np.float32)[:, None, None]
    squared = full_x * full_x + full_y * full_y
    safe = np.where(squared > 0.0, squared, np.float32(1.0))
    none = np.zeros_like(safe)
    plain = f32(np.stack([-full_x * full_x / safe, none, none, -full_y * full_y / safe, none]))
    turned = f32(np.stack([none, none, none, none, odd_y / np.sqrt(safe)]))
    pair = (total[0] * plain - total[1] * turned, total[1] * plain + total[0] * turned)
    pair = complex_product("fzkc,cb->fzkb", pair, phase(RADIX, RADIX, RADIX, 1.0))
    pair = times_table(pair, phase(outer_len, RADIX, grid_len, 1.0))
    last = phase(outer_len, outer_len, outer_len, 1.0)
    last = [lax.dynamic_slice_in_dim(item, row_start, row_share, 0) for item in last]
    real = product("fzkb,ak->fzab", pair[0], last[0]) - product("fzkb,ak->fzab", pair[1], last[1])
    return jnp.moveaxis(real.reshape(FIELDS, 2, row_share * RADIX), 1, 2)


def cubic_kernel(distance):
    near_part = (1.5 * distance - 2.5) * distance * distance + 1.0
    far_part = ((-0.5 * distance + 2.5) * distance - 4.0) * distance + 2.0
    return jnp.where(distance <= 1.0, near_part, jnp.where(distance < 2.0, far_part, 0.0))


def tap_weights(level):
    offset = (level.astype(jnp.float32) + 0.5) / QLEV - 0.5
    base = jnp.where(level < QLEV // 2, -1, 0).astype(jnp.int32)
    fraction = offset - base.astype(jnp.float32)
    taps = jnp.arange(4, dtype=jnp.int32)[None, :]
    weights = cubic_kernel(jnp.abs(fraction[:, None] - (taps.astype(jnp.float32) - 1.0)))
    return weights, base[:, None] - 1 + taps


def choose(which, candidates):
    picked = None
    for key, value in candidates.items():
        picked = value if picked is None else jnp.where(which == key, value, picked)
    return picked


def depth_scan(pieces, jobs, total):
    count = lax.axis_size("depth")
    here = lax.axis_index("depth")
    up = [(i, i + 1) for i in range(count - 1)]
    down = [(i + 1, i) for i in range(count - 1)]
    from_below, from_above = [], []

    def complete(index):
        below = {d: from_below[index + d - 1] for d in range(1, count)}
        above = {count - 1 - d: from_above[index + d - 1] for d in range(1, count)}
        return pieces[index], below, above

    for step in range(total + count - 2):
        live = [d for d in range(count - 1) if 0 <= step - d < total]
        rising = choose(here, {d: pieces[step - d] for d in live})
        falling = choose(here, {count - 1 - d: pieces[step - d] for d in live})
        if step:
            rising, falling = rising + from_below[-1], falling + from_above[-1]
        work = jobs.get(step, [])
        keys = [key for _, key in work]
        rising, falling, keys = lax.optimization_barrier((rising, falling, keys))
        below = lax.ppermute(rising, "depth", up)
        above = lax.ppermute(falling, "depth", down)
        results = [task(key, complete) for (task, _), key in zip(work, keys)]
        below, above, _ = lax.optimization_barrier((below, above, results))
        from_below.append(below)
        from_above.append(above)
    return complete


def per_device(density, layer_top, layer_thick, sample_row, sample_col, sample_frac, sample_owner):
    wide_count = lax.axis_size("wide")
    depth_count = lax.axis_size("depth")
    rows_here, grid_len = density.shape[1], density.shape[2]
    outer_len = grid_len // RADIX
    tile_rows = rows_here // depth_count
    chunks = 2 * SLOTS // wide_count
    wide_id, depth_id = lax.axis_index("wide"), lax.axis_index("depth")

    def exchange(block):
        return lax.all_to_all(block, "wide", split_axis=0, concat_axis=0, tiled=True)

    groups = [range(0, SLOTS, 2), range(1, SLOTS, 2)] if chunks == 4 else [range(SLOTS)]
    spectra, field = [], density[0]
    for group in groups:
        made = row_forward(field, wide_count, tuple(group))
        spectra += [exchange(item) for item in made]
        field, _ = lax.optimization_barrier((field, made[0]))
    columns = [item.reshape(grid_len, RADIX) for item in spectra]

    lane = jnp.arange(RADIX, dtype=jnp.int32)[None, :] % HALF
    waves = []
    for chunk in range(chunks):
        block = wide_id * chunks + chunk
        slot = block // 2
        place = (block % 2) * HALF + lane
        low = jnp.where(
            place < HALF, outer_len * place, outer_len // 2 + outer_len * (place - HALF)
        )
        index = jnp.where(slot == 0, low, slot + outer_len * place)
        signed = jnp.where(index < grid_len // 2, index, index - grid_len).astype(jnp.float32)
        waves.append(signed * (2.0 * math.pi / grid_len))

    depths = jnp.concatenate([layer_top, layer_thick])
    edge = edge_forward(
        jnp.stack([columns[0][:, 0], columns[0][:, HALF]]), layer_top[0], layer_thick[0]
    )
    edge = lax.psum(edge, "depth")
    row_share = outer_len // depth_count
    row_start = depth_id * row_share
    place = (jnp.stack([wide_id, depth_id]).astype(jnp.int32), row_start, row_share)
    sizes = (grid_len, wide_count, tile_rows)
    taps_y, offset_y = tap_weights(sample_frac[0, 0])
    taps_x, offset_x = tap_weights(sample_frac[0, 1])
    row_ids = sample_row[0][:, None] + offset_y
    col_ids = (sample_col[0][:, None] + offset_x) % grid_len
    row_ids = jnp.where(
        row_ids < 0,
        row_ids + tile_rows + 2,
        jnp.where(row_ids >= tile_rows, row_ids + 2, row_ids),
    )
    row_marks = row_ids[:, :, None] == jnp.arange(tile_rows + 8, dtype=jnp.int32)
    weight_y = jnp.sum(jnp.where(row_marks, taps_y[:, :, None], 0.0), axis=1)
    sample_count = sample_row.shape[1]
    capacity = max(2 * sample_count // wide_count, 2)
    slot_total = wide_count * capacity
    owner_ids = sample_owner[0, :, 0]
    same = owner_ids[:, None] == owner_ids[None, :]
    order = jnp.arange(sample_count, dtype=jnp.int32)
    slot_ids = jnp.sum((same & (order[None, :] < order[:, None])).astype(jnp.int32), axis=1)
    target = owner_ids * capacity + slot_ids
    placement = (target[:, None] == jnp.arange(slot_total, dtype=jnp.int32)[None, :]).astype(
        jnp.float32
    )
    pieces, blocks, partial_sums, edges = [], {}, {}, []

    def forward_job(chunk, wave, complete):
        pieces.extend(column_forward(columns[chunk], wave, depths))
        return pieces[-1]

    def edge_job(key, complete):
        edges.append(edge_inverse(key[0], row_start, row_share))
        edges.append(column_mask(key[1], taps_x, grid_len))
        return edges

    def early_job(chunk, wave, complete):
        item = column_inverse(complete(2 * chunk), 0, wave, wave, place, None, None, sizes, EVERY)
        partial_sums[chunk] = item
        return item

    def late_job(chunk, wave, complete, groups=(EVERY,)):
        part = complete(2 * chunk + 1)
        if chunk:
            wave, _ = lax.optimization_barrier((wave, blocks[0, chunk - 1][0]))
        special = edges[0] if chunk == 0 else None
        for group in groups:
            item = column_inverse(
                part, outer_len // 2, wave, wave, place, special, partial_sums[chunk], sizes, group
            )
            moved = exchange(item)
            for spot, c in enumerate(group):
                blocks[c, chunk] = (moved, spot)
            if group != groups[-1]:
                wave, _ = lax.optimization_barrier((wave, item))
        return item

    forward_job(0, waves[0], None)
    jobs = {}
    last = chunks - 1

    def plan(step, task, chunk):
        jobs.setdefault(step, []).append((functools.partial(task, chunk), waves[chunk]))

    for chunk in range(1, chunks):
        plan(chunk - 1, forward_job, chunk)
    for chunk in range(chunks):
        plan(2 * chunk + depth_count - 1, early_job, chunk)
        if chunk != last:
            plan(2 * chunk + depth_count, late_job, chunk)
    jobs.setdefault(EDGE_STEP, []).append((edge_job, (edge, col_ids)))
    complete = depth_scan(pieces, jobs, 2 * chunks)
    late_job(last, waves[last], complete, GROUPS)

    tiles = depth_count * wide_count
    forward = [(i, (i + 1) % tiles) for i in range(tiles)]
    backward = [(target, source) for source, target in forward]
    gradient, halos = None, []
    for group in GROUPS:
        ready = [[blocks[c, chunk] for chunk in range(chunks)] for c in group]
        gradient, top, bottom = row_inverse(ready, grid_len, gradient)
        used = len(group)
        gradient, bottom, top = lax.optimization_barrier(
            (gradient, bottom[:used, 6:], top[:used, :2])
        )
        low = lax.ppermute(bottom, ("depth", "wide"), forward)
        high = lax.ppermute(top, ("depth", "wide"), backward)
        halos.append(
            jnp.concatenate([low, high, jnp.zeros((used, 4, grid_len), jnp.float32)], axis=1)
        )

    outgoing = [
        interpolate(gradient, halo, group, weight_y, edges[1], placement)
        for group, halo in zip(GROUPS, halos)
    ]
    outgoing = jnp.concatenate(outgoing)
    outgoing = outgoing.reshape(FIELDS, wide_count, capacity)
    arrived = lax.all_to_all(outgoing, "wide", split_axis=1, concat_axis=1, tiled=True)
    arrived = arrived.reshape(FIELDS, 1, slot_total)
    return (gradient, jnp.concatenate([arrived, -(arrived[0:1] + arrived[3:4])]))


def solution(mesh):
    in_specs = (
        P("depth", "wide", None),
        P("depth"),
        P("depth"),
        P(("depth", "wide"), None),
        P(("depth", "wide"), None),
        P(("depth", "wide"), None, None),
        P(("depth", "wide"), None, None),
    )
    out_specs = (P(None, ("depth", "wide"), None), P(None, ("depth", "wide"), None))
    return jax.shard_map(
        per_device, mesh=mesh, in_specs=in_specs, out_specs=out_specs, check_vma=False
    )
```
